256 devices in a mesh: gx: 8 (over x, core), gy: 32 (over y, z).
Axes of the slice: x: 4, y: 4, z: 8, core: 2. Of those that a mesh axis runs over, the one named last changes fastest.
Arguments:
- state: float32 [2, 8, 512, 1024], P(None, None, 'gy', 'gx'), may hold values from 0 to 1, as said below
- previous: float32 [2, 8, 512, 1024], P(None, None, 'gy', 'gx'), may hold values from 0 to 1
- feed: float32 [8, 512, 1024], P(None, 'gy', 'gx'), may hold values from 0.01 to 0.1
- kill: float32 [8, 512, 1024], P(None, 'gy', 'gx'), may hold values from 0.03 to 0.1
Outputs:
- correction: float32 [2, 8, 512, 1024], P(None, None, 'gy', 'gx')
The draws below stay inside these ranges and needn't reach their ends.
Inputs may be any that keep to these rules, and one draw needn't show every extreme that they name: `state`: u and v of every cell lie in the stated range.
All inputs are finite; a program needn't handle non-finite values.
Results may differ from the reference program's by a relative error of at most 0.0001.
Values sent between devices are 32-bit elements; how exact they have to be, the bound alone decides.
A program may use at most 128 MiB of HBM per device.

```python
import math
import jax
import jax.numpy as jnp

NX = 1024
NY = 512
NZ = 8


def draw_state(key, part):
    first_key = jax.random.fold_in(key, 11)
    second_key = jax.random.fold_in(key, 23)
    shape = (NZ, NY, NX)
    cols = jnp.arange(NX, dtype=jnp.float32).reshape(1, 1, NX)
    rows = jnp.arange(NY, dtype=jnp.float32).reshape(1, NY, 1)
    across = 0.5 + 0.5 * jnp.cos(2.0 * math.pi * cols / NX)
    down = 0.5 + 0.5 * jnp.cos(2.0 * math.pi * rows / NY)
    envelope = 0.08 + 0.92 * across * down
    substrate = jax.random.uniform(first_key, shape, jnp.float32)
    catalyst = envelope * jax.random.uniform(second_key, shape, jnp.float32)
    return jnp.stack([substrate, catalyst]).astype(jnp.float32)


def level_of(key, dims, shards, least, largest):
    gain = 1.0
    for axis_at, parts in shards:
        draws = jax.random.uniform(jax.random.fold_in(jax.random.fold_in(key, 6), axis_at), (parts,), jnp.float32, least / len(shards), largest / len(shards))
        gain = gain * jnp.repeat(jnp.exp(draws), dims[axis_at] // parts).reshape((-1,) + (1,) * (len(dims) - 1 - axis_at))
    return gain


def setup_inputs(seed: int = 0) -> dict:
    seeds = jax.random.split(jax.random.key(seed), 5)
    return {
        "state": draw_state(jax.random.fold_in(seeds[4], 71), 0),
        "previous": jnp.clip(1.0 * jax.random.uniform(seeds[1], (2, NZ, NY, NX), jnp.float32) ** level_of(seeds[1], (2, NZ, NY, NX), ((2, 32), (3, 8)), -0.2, 0.2), 0.0, 1.0),
        "feed": jnp.clip(jnp.exp(math.log(0.1) - 2.3025851 * jax.random.uniform(seeds[2], (NZ, NY, NX), jnp.float32) ** level_of(seeds[2], (NZ, NY, NX), ((1, 32), (2, 8)), -0.2, 0.2)), 0.01, 0.1),
        "kill": jnp.clip(jnp.exp(math.log(0.1) - 1.2039728 * jax.random.uniform(seeds[3], (NZ, NY, NX), jnp.float32) ** level_of(seeds[3], (NZ, NY, NX), ((1, 32), (2, 8)), -0.2, 0.2)), 0.03, 0.1),
    }


substrate_diffusion = 40.0
catalyst_diffusion = 20.0
inverse_step = 2.0
lower_fraction = 0.25
coarsenings = 2


def neighbour_sum(field):
    along_x = jnp.roll(field, 1, 3) + jnp.roll(field, -1, 3)
    along_y = jnp.roll(field, 1, 2) + jnp.roll(field, -1, 2)
    along_z = jnp.roll(field, 1, 1) + jnp.roll(field, -1, 1)
    return along_x + along_y + along_z


def restrict(field):
    lead, depth, rows, cols = field.shape
    blocks = field.reshape(lead, depth // 2, 2, rows // 2, 2, cols // 2, 2)
    return jnp.mean(blocks, axis=(2, 4, 6))


def prolong(field):
    return jnp.repeat(jnp.repeat(jnp.repeat(field, 2, 1), 2, 2), 2, 3)


def diffusions(level):
    scale = 0.25 ** level
    return jnp.array([substrate_diffusion * scale, catalyst_diffusion * scale], jnp.float32).reshape(2, 1, 1, 1)


def coefficients(fields, level):
    scale = 0.25 ** level
    diff_first = substrate_diffusion * scale
    diff_second = catalyst_diffusion * scale
    substrate, catalyst, feed_rate, kill_rate = fields[0], fields[1], fields[2], fields[3]
    product = substrate * catalyst
    squared = catalyst * catalyst
    self_first = inverse_step + squared + feed_rate + 6.0 * diff_first
    cross_first = 2.0 * product
    cross_second = -squared
    self_second = inverse_step + feed_rate + kill_rate - 2.0 * product + 6.0 * diff_second
    coeff = jnp.stack([self_first, cross_first, cross_second, self_second])
    spread = jnp.maximum(jnp.max((6.0 * diff_first + cross_first) / self_first),
                         jnp.max((6.0 * diff_second + squared) / self_second))
    return coeff, spread


def apply_operator(coeff, field, neighbours, level):
    first = coeff[0] * field[0] + coeff[1] * field[1]
    second = coeff[2] * field[0] + coeff[3] * field[1]
    return jnp.stack([first, second]) - diffusions(level) * neighbours


def chebyshev(operate, coeff, source, start, spread):
    upper = 1.0 + spread
    lower = lower_fraction * upper
    centre = (upper + lower) / 2.0
    half_width = (upper - lower) / 2.0
    ratio = centre / half_width
    damping = 1.0 / ratio
    diagonal = jnp.stack([coeff[0], coeff[3]])
    if start is None:
        resid = source / diagonal
        update = resid / centre
        iterate = update
    else:
        resid = (source - operate(start)) / diagonal
        update = resid / centre
        iterate = start + update
    for sweep in range(2):
        resid = (source - operate(iterate)) / diagonal
        damping_next = 1.0 / (2.0 * ratio - damping)
        update = damping_next * damping * update + (2.0 * damping_next / half_width) * resid
        iterate = iterate + update
        damping = damping_next
    return iterate


def vcycle(level, source, coeffs, spreads):
    coeff = coeffs[level]
    spread = spreads[level]

    def operate(field):
        return apply_operator(coeff, field, neighbour_sum(field), level)

    iterate = chebyshev(operate, coeff, source, None, spread)
    if level < coarsenings:
        resid = source - operate(iterate)
        iterate = iterate + prolong(vcycle(level + 1, restrict(resid), coeffs, spreads))
    return chebyshev(operate, coeff, source, iterate, spread)


def reference(state, previous, feed, kill):
    fields = jnp.concatenate([state, feed[None], kill[None]], 0)
    coeffs = []
    spreads = []
    for level in range(coarsenings + 1):
        coeff, spread = coefficients(fields, level)
        coeffs.append(coeff)
        spreads.append(spread)
        if level < coarsenings:
            fields = restrict(fields)
    substrate, catalyst = state[0], state[1]
    reaction = substrate * catalyst * catalyst
    laplace = neighbour_sum(state) - 6.0 * state
    local_terms = jnp.stack([reaction - feed * (1.0 - substrate), -reaction + (feed + kill) * catalyst])
    nonlinear = inverse_step * (state - previous) - diffusions(0) * laplace + local_terms
    return vcycle(0, -nonlinear, coeffs, spreads)
```

```python
import jax
import jax.numpy as jnp
from jax import lax
from jax.sharding import PartitionSpec as P

substrate_diffusion = 40.0
catalyst_diffusion = 20.0
inverse_step = 2.0
lower_fraction = 0.25
coarsenings = 2


def shifted_pair(cells, axis, dim):
    count = lax.axis_size(axis)
    size = cells.shape[dim]
    head = lax.slice_in_dim(cells, 0, 1, axis=dim)
    tail = lax.slice_in_dim(cells, size - 1, size, axis=dim)
    from_low = lax.ppermute(tail, axis, [(i, (i + 1) % count) for i in range(count)])
    from_high = lax.ppermute(head, axis, [((i + 1) % count, i) for i in range(count)])
    low = jnp.concatenate([from_low, lax.slice_in_dim(cells, 0, size - 1, axis=dim)], axis=dim)
    high = jnp.concatenate([lax.slice_in_dim(cells, 1, size, axis=dim), from_high], axis=dim)
    return low + high


def neighbour_sum(cells):
    along_x = shifted_pair(cells, "gx", 3)
    along_y = shifted_pair(cells, "gy", 2)
    along_z = jnp.roll(cells, 1, 1) + jnp.roll(cells, -1, 1)
    return along_x + along_y + along_z


def global_max(value):
    for axis in ("gx", "gy"):
        count = lax.axis_size(axis)
        step = 1
        while step < count:
            other = lax.ppermute(value, axis, [(i, i ^ step) for i in range(count)])
            value = jnp.maximum(value, other)
            step *= 2
    return value


def restrict(field):
    lead, depth, rows, cols = field.shape
    blocks = field.reshape(lead, depth // 2, 2, rows // 2, 2, cols // 2, 2)
    return jnp.mean(blocks, axis=(2, 4, 6))


def prolong(field):
    return jnp.repeat(jnp.repeat(jnp.repeat(field, 2, 1), 2, 2), 2, 3)


def diffusions(level):
    scale = 0.25**level
    return jnp.array(
        [substrate_diffusion * scale, catalyst_diffusion * scale], jnp.float32
    ).reshape(2, 1, 1, 1)


def coefficients(fields, level):
    scale = 0.25**level
    diff_first = substrate_diffusion * scale
    diff_second = catalyst_diffusion * scale
    substrate, catalyst, feed_rate, kill_rate = (fields[0], fields[1], fields[2], fields[3])
    product = substrate * catalyst
    squared = catalyst * catalyst
    self_first = inverse_step + squared + feed_rate + 6.0 * diff_first
    cross_first = 2.0 * product
    cross_second = -squared
    self_second = inverse_step + feed_rate + kill_rate - 2.0 * product + 6.0 * diff_second
    coeff = jnp.stack([self_first, cross_first, cross_second, self_second])
    spread = jnp.maximum(
        jnp.max((6.0 * diff_first + cross_first) / self_first),
        jnp.max((6.0 * diff_second + squared) / self_second),
    )
    return (coeff, spread)


def apply_operator(coeff, field, neighbours, level):
    first = coeff[0] * field[0] + coeff[1] * field[1]
    second = coeff[2] * field[0] + coeff[3] * field[1]
    return jnp.stack([first, second]) - diffusions(level) * neighbours


def chebyshev(operate, coeff, source, start, spread):
    upper = 1.0 + spread
    lower = lower_fraction * upper
    centre = (upper + lower) / 2.0
    half_width = (upper - lower) / 2.0
    ratio = centre / half_width
    damping = 1.0 / ratio
    diagonal = jnp.stack([coeff[0], coeff[3]])
    if start is None:
        resid = source / diagonal
        update = resid / centre
        iterate = update
    else:
        resid = (source - operate(start)) / diagonal
        update = resid / centre
        iterate = start + update
    for sweep in range(2):
        resid = (source - operate(iterate)) / diagonal
        damping_next = 1.0 / (2.0 * ratio - damping)
        update = damping_next * damping * update + 2.0 * damping_next / half_width * resid
        iterate = iterate + update
        damping = damping_next
    return iterate


def face_operator(coeff, level):

    def operate(field):
        return apply_operator(coeff, field, neighbour_sum(field), level)

    return operate


def vcycle(level, source, coeffs, spreads):
    coeff = coeffs[level]
    spread = spreads[level]
    operate = face_operator(coeff, level)
    iterate = chebyshev(operate, coeff, source, None, spread)
    if level < coarsenings:
        resid = source - operate(iterate)
        iterate = iterate + prolong(vcycle(level + 1, restrict(resid), coeffs, spreads))
    return chebyshev(operate, coeff, source, iterate, spread)


def body(state, previous, feed, kill):
    fields = jnp.concatenate([state, feed[None], kill[None]], 0)
    coeffs = []
    local_spreads = []
    for level in range(coarsenings + 1):
        coeff, spread = coefficients(fields, level)
        coeffs.append(coeff)
        local_spreads.append(spread)
        if level < coarsenings:
            fields = restrict(fields)
    spreads = global_max(jnp.stack(local_spreads))
    substrate, catalyst = (state[0], state[1])
    reaction = substrate * catalyst * catalyst
    laplace = neighbour_sum(state) - 6.0 * state
    local_terms = jnp.stack(
        [reaction - feed * (1.0 - substrate), -reaction + (feed + kill) * catalyst]
    )
    nonlinear = inverse_step * (state - previous) - diffusions(0) * laplace + local_terms
    return vcycle(0, -nonlinear, coeffs, spreads)


def solution(mesh):
    placed = (
        P(None, None, "gy", "gx"),
        P(None, None, "gy", "gx"),
        P(None, "gy", "gx"),
        P(None, "gy", "gx"),
    )
    return jax.shard_map(
        body, mesh=mesh, in_specs=placed, out_specs=P(None, None, "gy", "gx"), check_vma=False
    )
```

```python
import jax
import jax.numpy as jnp
from jax import lax
from jax.sharding import PartitionSpec as P
from jax.experimental import pallas as pl
from jax.experimental.pallas import tpu as pltpu

substrate_diffusion = 40.0
catalyst_diffusion = 20.0
inverse_step = 2.0
lower_fraction = 0.25
coarsenings = 2


def exchange_kernel(low_x, high_x, low_y, high_y, got_lx, got_hx, got_ly, got_hy,
                    land_lx, land_hx, land_ly, land_hy, send_sem, recv_sem):
    count_x = lax.axis_size("gx")
    count_y = lax.axis_size("gy")
    at_x = lax.axis_index("gx")
    at_y = lax.axis_index("gy")
    left = lax.rem(at_x + count_x - 1, count_x)
    right = lax.rem(at_x + 1, count_x)
    down = lax.rem(at_y + count_y - 1, count_y)
    up = lax.rem(at_y + 1, count_y)
    mesh_ids = pl.DeviceIdType.MESH
    barrier = pltpu.get_barrier_semaphore()
    for device in ((left, at_y), (right, at_y), (at_x, down), (at_x, up)):
        pl.semaphore_signal(barrier, 1, device_id=device, device_id_type=mesh_ids)
    pl.semaphore_wait(barrier, 4)
    plan = (
        (high_x, land_lx, (right, at_y)),
        (low_x, land_hx, (left, at_y)),
        (high_y, land_ly, (at_x, up)),
        (low_y, land_hy, (at_x, down)),
    )
    copies = []
    for slot, (source, target, device) in enumerate(plan):
        copy = pltpu.make_async_remote_copy(
            src_ref=source,
            dst_ref=target,
            send_sem=send_sem.at[slot],
            recv_sem=recv_sem.at[slot],
            device_id=device,
            device_id_type=mesh_ids,
        )
        copy.start()
        copies.append(copy)
    for copy in copies:
        copy.wait()
    got_lx[...] = land_lx[...]
    got_hx[...] = land_hx[...]
    got_ly[...] = land_ly[...]
    got_hy[...] = land_hy[...]


def exchange(faces_x, faces_y, tag):
    vmem = pl.BlockSpec(memory_space=pltpu.VMEM)
    x_shape = jax.ShapeDtypeStruct(faces_x[0].shape, jnp.float32)
    y_shape = jax.ShapeDtypeStruct(faces_y[0].shape, jnp.float32)
    return pl.pallas_call(
        exchange_kernel,
        out_shape=(x_shape, x_shape, y_shape, y_shape),
        in_specs=[vmem] * 4,
        out_specs=(vmem,) * 4,
        scratch_shapes=[
            pltpu.VMEM(x_shape.shape, jnp.float32),
            pltpu.VMEM(x_shape.shape, jnp.float32),
            pltpu.VMEM(y_shape.shape, jnp.float32),
            pltpu.VMEM(y_shape.shape, jnp.float32),
            pltpu.SemaphoreType.DMA((4,)),
            pltpu.SemaphoreType.DMA((4,)),
        ],
        compiler_params=pltpu.CompilerParams(collective_id=tag, has_side_effects=True),
    )(faces_x[0], faces_x[1], faces_y[0], faces_y[1])


def neighbour_sum(cells):
    lead, depth, rows, cols = cells.shape
    face_x = lambda part: part.reshape(lead * depth, rows)
    face_y = lambda part: part.reshape(lead * depth, cols)
    got_lx, got_hx, got_ly, got_hy = exchange(
        (face_x(cells[:, :, :, :1]), face_x(cells[:, :, :, cols - 1:])),
        (face_y(cells[:, :, :1, :]), face_y(cells[:, :, rows - 1:, :])),
        {128: 0, 64: 1, 32: 2}.get(cols, 3),
    )
    got_lx = got_lx.reshape(lead, depth, rows, 1)
    got_hx = got_hx.reshape(lead, depth, rows, 1)
    got_ly = got_ly.reshape(lead, depth, 1, cols)
    got_hy = got_hy.reshape(lead, depth, 1, cols)
    along_x = (jnp.concatenate([got_lx, cells[:, :, :, :cols - 1]], 3)
               + jnp.concatenate([cells[:, :, :, 1:], got_hx], 3))
    along_y = (jnp.concatenate([got_ly, cells[:, :, :rows - 1, :]], 2)
               + jnp.concatenate([cells[:, :, 1:, :], got_hy], 2))
    along_z = jnp.roll(cells, 1, 1) + jnp.roll(cells, -1, 1)
    return along_x + along_y + along_z


def global_max(value):
    for axis in ("gx", "gy"):
        count = lax.axis_size(axis)
        step = 1
        while step < count:
            other = lax.ppermute(value, axis, [(i, i ^ step) for i in range(count)])
            value = jnp.maximum(value, other)
            step *= 2
    return value


def restrict(field):
    lead, depth, rows, cols = field.shape
    blocks = field.reshape(lead, depth // 2, 2, rows // 2, 2, cols // 2, 2)
    return jnp.mean(blocks, axis=(2, 4, 6))


def prolong(field):
    return jnp.repeat(jnp.repeat(jnp.repeat(field, 2, 1), 2, 2), 2, 3)


def diffusions(level):
    scale = 0.25**level
    return jnp.array(
        [substrate_diffusion * scale, catalyst_diffusion * scale], jnp.float32
    ).reshape(2, 1, 1, 1)


def coefficients(fields, level):
    scale = 0.25**level
    diff_first = substrate_diffusion * scale
    diff_second = catalyst_diffusion * scale
    substrate, catalyst, feed_rate, kill_rate = (fields[0], fields[1], fields[2], fields[3])
    product = substrate * catalyst
    squared = catalyst * catalyst
    self_first = inverse_step + squared + feed_rate + 6.0 * diff_first
    cross_first = 2.0 * product
    cross_second = -squared
    self_second = inverse_step + feed_rate + kill_rate - 2.0 * product + 6.0 * diff_second
    coeff = jnp.stack([self_first, cross_first, cross_second, self_second])
    spread = jnp.maximum(
        jnp.max((6.0 * diff_first + cross_first) / self_first),
        jnp.max((6.0 * diff_second + squared) / self_second),
    )
    return (coeff, spread)


def apply_operator(coeff, field, neighbours, level):
    first = coeff[0] * field[0] + coeff[1] * field[1]
    second = coeff[2] * field[0] + coeff[3] * field[1]
    return jnp.stack([first, second]) - diffusions(level) * neighbours


def chebyshev(operate, coeff, source, start, spread):
    upper = 1.0 + spread
    lower = lower_fraction * upper
    centre = (upper + lower) / 2.0
    half_width = (upper - lower) / 2.0
    ratio = centre / half_width
    damping = 1.0 / ratio
    diagonal = jnp.stack([coeff[0], coeff[3]])
    if start is None:
        resid = source / diagonal
        update = resid / centre
        iterate = update
    else:
        resid = (source - operate(start)) / diagonal
        update = resid / centre
        iterate = start + update
    for sweep in range(2):
        resid = (source - operate(iterate)) / diagonal
        damping_next = 1.0 / (2.0 * ratio - damping)
        update = damping_next * damping * update + 2.0 * damping_next / half_width * resid
        iterate = iterate + update
        damping = damping_next
    return iterate


def face_operator(coeff, level):

    def operate(field):
        return apply_operator(coeff, field, neighbour_sum(field), level)

    return operate


def vcycle(level, source, coeffs, spreads):
    coeff = coeffs[level]
    spread = spreads[level]
    operate = face_operator(coeff, level)
    iterate = chebyshev(operate, coeff, source, None, spread)
    if level < coarsenings:
        resid = source - operate(iterate)
        iterate = iterate + prolong(vcycle(level + 1, restrict(resid), coeffs, spreads))
    return chebyshev(operate, coeff, source, iterate, spread)


def body(state, previous, feed, kill):
    fields = jnp.concatenate([state, feed[None], kill[None]], 0)
    coeffs = []
    local_spreads = []
    for level in range(coarsenings + 1):
        coeff, spread = coefficients(fields, level)
        coeffs.append(coeff)
        local_spreads.append(spread)
        if level < coarsenings:
            fields = restrict(fields)
    spreads = global_max(jnp.stack(local_spreads))
    substrate, catalyst = (state[0], state[1])
    reaction = substrate * catalyst * catalyst
    laplace = neighbour_sum(state) - 6.0 * state
    local_terms = jnp.stack(
        [reaction - feed * (1.0 - substrate), -reaction + (feed + kill) * catalyst]
    )
    nonlinear = inverse_step * (state - previous) - diffusions(0) * laplace + local_terms
    return vcycle(0, -nonlinear, coeffs, spreads)


def solution(mesh):
    placed = (
        P(None, None, "gy", "gx"),
        P(None, None, "gy", "gx"),
        P(None, "gy", "gx"),
        P(None, "gy", "gx"),
    )
    return jax.shard_map(
        body, mesh=mesh, in_specs=placed, out_specs=P(None, None, "gy", "gx"), check_vma=False
    )
```

```python
import jax
import jax.numpy as jnp
from jax import lax
from jax.sharding import PartitionSpec as P

substrate_diffusion = 40.0
catalyst_diffusion = 20.0
inverse_step = 2.0
lower_fraction = 0.25
coarsenings = 2


def padded(cells, width):
    for axis, dim in (("gx", 3), ("gy", 2)):
        count = lax.axis_size(axis)
        size = cells.shape[dim]
        head = lax.slice_in_dim(cells, 0, width, axis=dim)
        tail = lax.slice_in_dim(cells, size - width, size, axis=dim)
        cells = jnp.concatenate(
            [
                lax.ppermute(tail, axis, [(i, (i + 1) % count) for i in range(count)]),
                cells,
                lax.ppermute(head, axis, [((i + 1) % count, i) for i in range(count)]),
            ],
            axis=dim,
        )
    return cells


def crop(cells, have, want):
    cut = have - want
    if cut == 0:
        return cells
    return cells[..., cut:cells.shape[-2] - cut, cut:cells.shape[-1] - cut]


def shrunk_neighbours(cells):
    centre = cells[:, :, 1:-1, 1:-1]
    along_x = cells[:, :, 1:-1, :-2] + cells[:, :, 1:-1, 2:]
    along_y = cells[:, :, :-2, 1:-1] + cells[:, :, 2:, 1:-1]
    along_z = jnp.roll(centre, 1, 1) + jnp.roll(centre, -1, 1)
    return along_x + along_y + along_z


def global_max(value):
    for axis in ("gx", "gy"):
        count = lax.axis_size(axis)
        step = 1
        while step < count:
            other = lax.ppermute(value, axis, [(i, i ^ step) for i in range(count)])
            value = jnp.maximum(value, other)
            step *= 2
    return value


def restrict(field):
    lead, depth, rows, cols = field.shape
    blocks = field.reshape(lead, depth // 2, 2, rows // 2, 2, cols // 2, 2)
    return jnp.mean(blocks, axis=(2, 4, 6))


def prolong(field):
    return jnp.repeat(jnp.repeat(jnp.repeat(field, 2, 1), 2, 2), 2, 3)


def diffusions(level):
    scale = 0.25**level
    return jnp.array(
        [substrate_diffusion * scale, catalyst_diffusion * scale], jnp.float32
    ).reshape(2, 1, 1, 1)


def coefficients(fields, level):
    scale = 0.25**level
    diff_first = substrate_diffusion * scale
    diff_second = catalyst_diffusion * scale
    substrate, catalyst, feed_rate, kill_rate = (fields[0], fields[1], fields[2], fields[3])
    product = substrate * catalyst
    squared = catalyst * catalyst
    self_first = inverse_step + squared + feed_rate + 6.0 * diff_first
    cross_first = 2.0 * product
    cross_second = -squared
    self_second = inverse_step + feed_rate + kill_rate - 2.0 * product + 6.0 * diff_second
    coeff = jnp.stack([self_first, cross_first, cross_second, self_second])
    return coeff, (6.0 * diff_first + cross_first) / self_first, (6.0 * diff_second + squared) / self_second


class Level:
    def __init__(self, coeff, halo, level):
        self.coeff = coeff
        self.halo = halo
        self.level = level

    def at(self, halo):
        return crop(self.coeff, self.halo, halo)

    def operate(self, field, halo):
        coeff = self.at(halo - 1)
        centre = crop(field, halo, halo - 1)
        first = coeff[0] * centre[0] + coeff[1] * centre[1]
        second = coeff[2] * centre[0] + coeff[3] * centre[1]
        return jnp.stack([first, second]) - diffusions(self.level) * shrunk_neighbours(field)

    def diagonal(self, halo):
        coeff = self.at(halo)
        return jnp.stack([coeff[0], coeff[3]])


def chebyshev(ops, source, source_halo, start, start_halo, spread):
    upper = 1.0 + spread
    lower = lower_fraction * upper
    centre = (upper + lower) / 2.0
    half_width = (upper - lower) / 2.0
    ratio = centre / half_width
    damping = 1.0 / ratio
    if start is None:
        halo = source_halo
        resid = source / ops.diagonal(halo)
        update = resid / centre
        iterate = update
    else:
        halo = min(source_halo, start_halo - 1)
        applied = ops.operate(start, start_halo)
        resid = (crop(source, source_halo, halo) - crop(applied, start_halo - 1, halo)) / ops.diagonal(halo)
        update = resid / centre
        iterate = crop(start, start_halo, halo) + update
    for sweep in range(2):
        applied = ops.operate(iterate, halo)
        halo = halo - 1
        resid = (crop(source, source_halo, halo) - applied) / ops.diagonal(halo)
        damping_next = 1.0 / (2.0 * ratio - damping)
        update = damping_next * damping * crop(update, halo + 1, halo) + 2.0 * damping_next / half_width * resid
        iterate = crop(iterate, halo + 1, halo) + update
        damping = damping_next
    return iterate, halo


def body(state, previous, feed, kill):
    deep = 3
    fields = jnp.concatenate([state, feed[None], kill[None]], 0)
    fields_1 = restrict(fields)
    fields_2 = restrict(fields_1)
    local = []
    for level, level_fields in enumerate((fields, fields_1, fields_2)):
        _, first, second = coefficients(level_fields, level)
        local.extend([jnp.max(first), jnp.max(second)])
    local = jnp.stack(local).reshape(3, 2)
    spreads = global_max(jnp.maximum(local[:, 0], local[:, 1]))

    wide = padded(jnp.concatenate([fields, previous], 0), deep + 1)
    ops_0 = Level(coefficients(crop(wide[:4], deep + 1, deep), 0)[0], deep, 0)
    state_w = wide[:2]
    substrate, catalyst = crop(state_w[0], deep + 1, deep), crop(state_w[1], deep + 1, deep)
    centre = crop(state_w, deep + 1, deep)
    reaction = substrate * catalyst * catalyst
    laplace = shrunk_neighbours(state_w) - 6.0 * centre
    feed_w = crop(wide[2], deep + 1, deep)
    kill_w = crop(wide[3], deep + 1, deep)
    previous_w = crop(wide[4:6], deep + 1, deep)
    local_terms = jnp.stack(
        [reaction - feed_w * (1.0 - substrate), -reaction + (feed_w + kill_w) * catalyst]
    )
    nonlinear = inverse_step * (centre - previous_w) - diffusions(0) * laplace + local_terms
    source_0 = -nonlinear
    pre_0, pre_0_halo = chebyshev(ops_0, source_0, deep, None, None, spreads[0])
    resid_0 = crop(source_0, deep, 0) - ops_0.operate(crop(pre_0, pre_0_halo, 1), 1)

    wide_1 = padded(jnp.concatenate([restrict(resid_0), fields_1], 0), deep)
    ops_1 = Level(coefficients(wide_1[2:], 1)[0], deep, 1)
    source_1 = wide_1[:2]
    pre_1, pre_1_halo = chebyshev(ops_1, source_1, deep, None, None, spreads[1])
    resid_1 = crop(source_1, deep, 0) - ops_1.operate(crop(pre_1, pre_1_halo, 1), 1)

    wide_2 = padded(jnp.concatenate([restrict(resid_1), fields_2], 0), deep)
    ops_2 = Level(coefficients(wide_2[2:], 2)[0], deep, 2)
    source_2 = wide_2[:2]
    first_2, first_2_halo = chebyshev(ops_2, source_2, deep, None, None, spreads[2])
    start_2 = padded(crop(first_2, first_2_halo, 0), deep)
    coarse_2, coarse_2_halo = chebyshev(ops_2, source_2, deep, start_2, deep, spreads[2])

    start_1 = padded(crop(pre_1, pre_1_halo, 0) + prolong(crop(coarse_2, coarse_2_halo, 0)), deep)
    post_1, post_1_halo = chebyshev(ops_1, source_1, deep, start_1, deep, spreads[1])

    start_0 = padded(crop(pre_0, pre_0_halo, 0) + prolong(crop(post_1, post_1_halo, 0)), deep)
    post_0, post_0_halo = chebyshev(ops_0, source_0, deep, start_0, deep, spreads[0])
    return crop(post_0, post_0_halo, 0)


def solution(mesh):
    placed = (
        P(None, None, "gy", "gx"),
        P(None, None, "gy", "gx"),
        P(None, "gy", "gx"),
        P(None, "gy", "gx"),
    )
    return jax.shard_map(
        body, mesh=mesh, in_specs=placed, out_specs=P(None, None, "gy", "gx"), check_vma=False
    )
```

```python
import jax
import jax.numpy as jnp
from jax import lax
from jax.sharding import PartitionSpec as P

substrate_diffusion = 40.0
catalyst_diffusion = 20.0
inverse_step = 2.0
lower_fraction = 0.25
coarsenings = 2


def padded(cells, width):
    for axis, dim in (("gx", 3), ("gy", 2)):
        count = lax.axis_size(axis)
        size = cells.shape[dim]
        head = lax.slice_in_dim(cells, 0, width, axis=dim)
        tail = lax.slice_in_dim(cells, size - width, size, axis=dim)
        cells = jnp.concatenate(
            [
                lax.ppermute(tail, axis, [(i, (i + 1) % count) for i in range(count)]),
                cells,
                lax.ppermute(head, axis, [((i + 1) % count, i) for i in range(count)]),
            ],
            axis=dim,
        )
    return cells


def crop(cells, have, want):
    cut = have - want
    if cut == 0:
        return cells
    return cells[..., cut:cells.shape[-2] - cut, cut:cells.shape[-1] - cut]


def shrunk_neighbours(cells):
    centre = cells[:, :, 1:-1, 1:-1]
    along_x = cells[:, :, 1:-1, :-2] + cells[:, :, 1:-1, 2:]
    along_y = cells[:, :, :-2, 1:-1] + cells[:, :, 2:, 1:-1]
    along_z = jnp.roll(centre, 1, 1) + jnp.roll(centre, -1, 1)
    return along_x + along_y + along_z


def global_max(value):
    for axis in ("gx", "gy"):
        count = lax.axis_size(axis)
        step = 1
        while step < count:
            other = lax.ppermute(value, axis, [(i, i ^ step) for i in range(count)])
            value = jnp.maximum(value, other)
            step *= 2
    return value


def restrict(field):
    cols = field.shape[-1]
    pairs = field[:, 0::2] + field[:, 1::2]
    pairs = pairs[:, :, 0::2] + pairs[:, :, 1::2]
    pick = (lax.broadcasted_iota(jnp.int32, (cols, cols // 2), 0) // 2
            == lax.broadcasted_iota(jnp.int32, (cols, cols // 2), 1)).astype(jnp.float32)
    pairs = jnp.dot(pairs, pick, precision=lax.Precision.HIGHEST)
    return pairs * 0.125


def prolong(field):
    return jnp.repeat(jnp.repeat(jnp.repeat(field, 2, 1), 2, 2), 2, 3)


def diffusions(level):
    scale = 0.25**level
    return jnp.array(
        [substrate_diffusion * scale, catalyst_diffusion * scale], jnp.float32
    ).reshape(2, 1, 1, 1)


def coefficients(fields, level):
    scale = 0.25**level
    diff_first = substrate_diffusion * scale
    diff_second = catalyst_diffusion * scale
    substrate, catalyst, feed_rate, kill_rate = (fields[0], fields[1], fields[2], fields[3])
    product = substrate * catalyst
    squared = catalyst * catalyst
    self_first = inverse_step + squared + feed_rate + 6.0 * diff_first
    cross_first = 2.0 * product
    cross_second = -squared
    self_second = inverse_step + feed_rate + kill_rate - 2.0 * product + 6.0 * diff_second
    coeff = jnp.stack([self_first, cross_first, cross_second, self_second])
    return coeff, (6.0 * diff_first + cross_first) / self_first, (6.0 * diff_second + squared) / self_second


class Level:
    def __init__(self, coeff, halo, level):
        self.coeff = coeff
        self.halo = halo
        self.level = level

    def at(self, halo):
        return crop(self.coeff, self.halo, halo)

    def operate(self, field, halo):
        coeff = self.at(halo - 1)
        centre = crop(field, halo, halo - 1)
        first = coeff[0] * centre[0] + coeff[1] * centre[1]
        second = coeff[2] * centre[0] + coeff[3] * centre[1]
        return jnp.stack([first, second]) - diffusions(self.level) * shrunk_neighbours(field)

    def diagonal(self, halo):
        coeff = self.at(halo)
        return jnp.stack([coeff[0], coeff[3]])


def chebyshev(ops, source, source_halo, start, start_halo, spread):
    upper = 1.0 + spread
    lower = lower_fraction * upper
    centre = (upper + lower) / 2.0
    half_width = (upper - lower) / 2.0
    ratio = centre / half_width
    damping = 1.0 / ratio
    if start is None:
        halo = source_halo
        resid = source / ops.diagonal(halo)
        update = resid / centre
        iterate = update
    else:
        halo = min(source_halo, start_halo - 1)
        applied = ops.operate(start, start_halo)
        resid = (crop(source, source_halo, halo) - crop(applied, start_halo - 1, halo)) / ops.diagonal(halo)
        update = resid / centre
        iterate = crop(start, start_halo, halo) + update
    for sweep in range(2):
        applied = ops.operate(iterate, halo)
        halo = halo - 1
        resid = (crop(source, source_halo, halo) - applied) / ops.diagonal(halo)
        damping_next = 1.0 / (2.0 * ratio - damping)
        update = damping_next * damping * crop(update, halo + 1, halo) + 2.0 * damping_next / half_width * resid
        iterate = crop(iterate, halo + 1, halo) + update
        damping = damping_next
    return iterate, halo


def body(state, previous, feed, kill):
    deep = 3
    everything = jnp.concatenate([state, feed[None], kill[None], previous], 0)
    fields = everything[:4]
    fields_1 = restrict(fields)
    fields_2 = restrict(fields_1)
    local = []
    for level, level_fields in enumerate((fields, fields_1, fields_2)):
        _, first, second = coefficients(level_fields, level)
        local.extend([jnp.max(first), jnp.max(second)])
    local = jnp.stack(local).reshape(3, 2)
    spreads = global_max(jnp.maximum(local[:, 0], local[:, 1]))

    wide = padded(everything, deep + 1)
    ops_0 = Level(coefficients(crop(wide[:4], deep + 1, deep), 0)[0], deep, 0)
    state_w = wide[:2]
    substrate, catalyst = crop(state_w[0], deep + 1, deep), crop(state_w[1], deep + 1, deep)
    centre = crop(state_w, deep + 1, deep)
    reaction = substrate * catalyst * catalyst
    laplace = shrunk_neighbours(state_w) - 6.0 * centre
    feed_w = crop(wide[2], deep + 1, deep)
    kill_w = crop(wide[3], deep + 1, deep)
    previous_w = crop(wide[4:6], deep + 1, deep)
    local_terms = jnp.stack(
        [reaction - feed_w * (1.0 - substrate), -reaction + (feed_w + kill_w) * catalyst]
    )
    nonlinear = inverse_step * (centre - previous_w) - diffusions(0) * laplace + local_terms
    source_0 = -nonlinear
    pre_0, pre_0_halo = chebyshev(ops_0, source_0, deep, None, None, spreads[0])
    resid_0 = crop(source_0, deep, 0) - ops_0.operate(crop(pre_0, pre_0_halo, 1), 1)

    wide_1 = padded(jnp.concatenate([restrict(resid_0), fields_1], 0), deep)
    ops_1 = Level(coefficients(wide_1[2:], 1)[0], deep, 1)
    source_1 = wide_1[:2]
    pre_1, pre_1_halo = chebyshev(ops_1, source_1, deep, None, None, spreads[1])
    resid_1 = crop(source_1, deep, 0) - ops_1.operate(crop(pre_1, pre_1_halo, 1), 1)

    wide_2 = padded(jnp.concatenate([restrict(resid_1), fields_2], 0), deep)
    ops_2 = Level(coefficients(wide_2[2:], 2)[0], deep, 2)
    source_2 = wide_2[:2]
    first_2, first_2_halo = chebyshev(ops_2, source_2, deep, None, None, spreads[2])
    start_2 = padded(crop(first_2, first_2_halo, 0), deep)
    coarse_2, coarse_2_halo = chebyshev(ops_2, source_2, deep, start_2, deep, spreads[2])

    start_1 = padded(crop(pre_1, pre_1_halo, 0) + prolong(crop(coarse_2, coarse_2_halo, 0)), deep)
    post_1, post_1_halo = chebyshev(ops_1, source_1, deep, start_1, deep, spreads[1])

    start_0 = padded(crop(pre_0, pre_0_halo, 0) + prolong(crop(post_1, post_1_halo, 0)), deep)
    post_0, post_0_halo = chebyshev(ops_0, source_0, deep, start_0, deep, spreads[0])
    return crop(post_0, post_0_halo, 0)


def solution(mesh):
    placed = (
        P(None, None, "gy", "gx"),
        P(None, None, "gy", "gx"),
        P(None, "gy", "gx"),
        P(None, "gy", "gx"),
    )
    return jax.shard_map(
        body, mesh=mesh, in_specs=placed, out_specs=P(None, None, "gy", "gx"), check_vma=False
    )
```

```python
import jax
import jax.numpy as jnp
from jax import lax
from jax.sharding import PartitionSpec as P

substrate_diffusion = 40.0
catalyst_diffusion = 20.0
inverse_step = 2.0
lower_fraction = 0.25
coarsenings = 2


def padded(cells, width):
    for axis, dim in (("gx", 3), ("gy", 2)):
        count = lax.axis_size(axis)
        size = cells.shape[dim]
        head = lax.slice_in_dim(cells, 0, width, axis=dim)
        tail = lax.slice_in_dim(cells, size - width, size, axis=dim)
        cells = jnp.concatenate(
            [
                lax.ppermute(tail, axis, [(i, (i + 1) % count) for i in range(count)]),
                cells,
                lax.ppermute(head, axis, [((i + 1) % count, i) for i in range(count)]),
            ],
            axis=dim,
        )
    return cells


def crop(cells, have, want):
    cut = have - want
    if cut == 0:
        return cells
    return cells[..., cut:cells.shape[-2] - cut, cut:cells.shape[-1] - cut]


def shrunk_neighbours(cells):
    centre = cells[:, :, 1:-1, 1:-1]
    along_x = cells[:, :, 1:-1, :-2] + cells[:, :, 1:-1, 2:]
    along_y = cells[:, :, :-2, 1:-1] + cells[:, :, 2:, 1:-1]
    along_z = jnp.roll(centre, 1, 1) + jnp.roll(centre, -1, 1)
    return along_x + along_y + along_z


def global_max(value):
    for axis in ("gx", "gy"):
        count = lax.axis_size(axis)
        step = 1
        while step < count:
            other = lax.ppermute(value, axis, [(i, i ^ step) for i in range(count)])
            value = jnp.maximum(value, other)
            step *= 2
    return value


def restrict(field):
    lead, depth, rows, cols = field.shape
    count = lead * depth * rows
    pick_x = (lax.broadcasted_iota(jnp.int32, (cols, cols // 2), 0) // 2
              == lax.broadcasted_iota(jnp.int32, (cols, cols // 2), 1)).astype(jnp.float32)
    row = lax.broadcasted_iota(jnp.int32, (count // 4, count), 1)
    target = ((row // (depth * rows)) * (depth // 2) + (row // rows) % depth // 2) * (rows // 2) + row % rows // 2
    pick_rows = (lax.broadcasted_iota(jnp.int32, (count // 4, count), 0) == target).astype(jnp.float32)
    pairs = jnp.dot(field.reshape(count, cols), pick_x, precision=lax.Precision.HIGHEST)
    blocks = jnp.dot(pick_rows, pairs, precision=lax.Precision.HIGHEST)
    return (blocks * 0.125).reshape(lead, depth // 2, rows // 2, cols // 2)


def prolong(field):
    return jnp.repeat(jnp.repeat(jnp.repeat(field, 2, 1), 2, 2), 2, 3)


def diffusions(level):
    scale = 0.25**level
    return jnp.array(
        [substrate_diffusion * scale, catalyst_diffusion * scale], jnp.float32
    ).reshape(2, 1, 1, 1)


def coefficients(fields, level):
    scale = 0.25**level
    diff_first = substrate_diffusion * scale
    diff_second = catalyst_diffusion * scale
    substrate, catalyst, feed_rate, kill_rate = (fields[0], fields[1], fields[2], fields[3])
    product = substrate * catalyst
    squared = catalyst * catalyst
    self_first = inverse_step + squared + feed_rate + 6.0 * diff_first
    cross_first = 2.0 * product
    cross_second = -squared
    self_second = inverse_step + feed_rate + kill_rate - 2.0 * product + 6.0 * diff_second
    coeff = jnp.stack([self_first, cross_first, cross_second, self_second])
    return coeff, (6.0 * diff_first + cross_first) / self_first, (6.0 * diff_second + squared) / self_second


class Level:
    def __init__(self, coeff, halo, level):
        self.coeff = coeff
        self.halo = halo
        self.level = level

    def at(self, halo):
        return crop(self.coeff, self.halo, halo)

    def operate(self, field, halo):
        coeff = self.at(halo - 1)
        centre = crop(field, halo, halo - 1)
        first = coeff[0] * centre[0] + coeff[1] * centre[1]
        second = coeff[2] * centre[0] + coeff[3] * centre[1]
        return jnp.stack([first, second]) - diffusions(self.level) * shrunk_neighbours(field)

    def diagonal(self, halo):
        coeff = self.at(halo)
        return jnp.stack([coeff[0], coeff[3]])


def chebyshev(ops, source, source_halo, start, start_halo, spread):
    upper = 1.0 + spread
    lower = lower_fraction * upper
    centre = (upper + lower) / 2.0
    half_width = (upper - lower) / 2.0
    ratio = centre / half_width
    damping = 1.0 / ratio
    if start is None:
        halo = source_halo
        resid = source / ops.diagonal(halo)
        update = resid / centre
        iterate = update
    else:
        halo = min(source_halo, start_halo - 1)
        applied = ops.operate(start, start_halo)
        resid = (crop(source, source_halo, halo) - crop(applied, start_halo - 1, halo)) / ops.diagonal(halo)
        update = resid / centre
        iterate = crop(start, start_halo, halo) + update
    for sweep in range(2):
        applied = ops.operate(iterate, halo)
        halo = halo - 1
        resid = (crop(source, source_halo, halo) - applied) / ops.diagonal(halo)
        damping_next = 1.0 / (2.0 * ratio - damping)
        update = damping_next * damping * crop(update, halo + 1, halo) + 2.0 * damping_next / half_width * resid
        iterate = crop(iterate, halo + 1, halo) + update
        damping = damping_next
    return iterate, halo


def body(state, previous, feed, kill):
    deep = 3
    fields = jnp.concatenate([state, feed[None], kill[None]], 0)
    fields_1 = restrict(fields)
    fields_2 = restrict(fields_1)
    local = []
    for level, level_fields in enumerate((fields, fields_1, fields_2)):
        _, first, second = coefficients(level_fields, level)
        local.extend([jnp.max(first), jnp.max(second)])
    local = jnp.stack(local).reshape(3, 2)
    spreads = global_max(jnp.maximum(local[:, 0], local[:, 1]))

    wide = padded(jnp.concatenate([fields, previous], 0), deep + 1)
    ops_0 = Level(coefficients(crop(wide[:4], deep + 1, deep), 0)[0], deep, 0)
    state_w = wide[:2]
    substrate, catalyst = crop(state_w[0], deep + 1, deep), crop(state_w[1], deep + 1, deep)
    centre = crop(state_w, deep + 1, deep)
    reaction = substrate * catalyst * catalyst
    laplace = shrunk_neighbours(state_w) - 6.0 * centre
    feed_w = crop(wide[2], deep + 1, deep)
    kill_w = crop(wide[3], deep + 1, deep)
    previous_w = crop(wide[4:6], deep + 1, deep)
    local_terms = jnp.stack(
        [reaction - feed_w * (1.0 - substrate), -reaction + (feed_w + kill_w) * catalyst]
    )
    nonlinear = inverse_step * (centre - previous_w) - diffusions(0) * laplace + local_terms
    source_0 = -nonlinear
    pre_0, pre_0_halo = chebyshev(ops_0, source_0, deep, None, None, spreads[0])
    resid_0 = crop(source_0, deep, 0) - ops_0.operate(crop(pre_0, pre_0_halo, 1), 1)

    wide_1 = padded(jnp.concatenate([restrict(resid_0), fields_1], 0), deep)
    ops_1 = Level(coefficients(wide_1[2:], 1)[0], deep, 1)
    source_1 = wide_1[:2]
    pre_1, pre_1_halo = chebyshev(ops_1, source_1, deep, None, None, spreads[1])
    resid_1 = crop(source_1, deep, 0) - ops_1.operate(crop(pre_1, pre_1_halo, 1), 1)

    wide_2 = padded(jnp.concatenate([restrict(resid_1), fields_2], 0), deep)
    ops_2 = Level(coefficients(wide_2[2:], 2)[0], deep, 2)
    source_2 = wide_2[:2]
    first_2, first_2_halo = chebyshev(ops_2, source_2, deep, None, None, spreads[2])
    start_2 = padded(crop(first_2, first_2_halo, 0), deep)
    coarse_2, coarse_2_halo = chebyshev(ops_2, source_2, deep, start_2, deep, spreads[2])

    start_1 = padded(crop(pre_1, pre_1_halo, 0) + prolong(crop(coarse_2, coarse_2_halo, 0)), deep)
    post_1, post_1_halo = chebyshev(ops_1, source_1, deep, start_1, deep, spreads[1])

    start_0 = padded(crop(pre_0, pre_0_halo, 0) + prolong(crop(post_1, post_1_halo, 0)), deep)
    post_0, post_0_halo = chebyshev(ops_0, source_0, deep, start_0, deep, spreads[0])
    return crop(post_0, post_0_halo, 0)


def solution(mesh):
    placed = (
        P(None, None, "gy", "gx"),
        P(None, None, "gy", "gx"),
        P(None, "gy", "gx"),
        P(None, "gy", "gx"),
    )
    return jax.shard_map(
        body, mesh=mesh, in_specs=placed, out_specs=P(None, None, "gy", "gx"), check_vma=False
    )
```

```python
import jax
import jax.numpy as jnp
from jax import lax
from jax.sharding import PartitionSpec as P
from jax.experimental import pallas as pl
from jax.experimental.pallas import tpu as pltpu

substrate_diffusion = 40.0
catalyst_diffusion = 20.0
inverse_step = 2.0
lower_fraction = 0.25
coarsenings = 2


def padded(cells, width):
    for axis, dim in (("gx", 3), ("gy", 2)):
        count = lax.axis_size(axis)
        size = cells.shape[dim]
        head = lax.slice_in_dim(cells, 0, width, axis=dim)
        tail = lax.slice_in_dim(cells, size - width, size, axis=dim)
        cells = jnp.concatenate(
            [
                lax.ppermute(tail, axis, [(i, (i + 1) % count) for i in range(count)]),
                cells,
                lax.ppermute(head, axis, [((i + 1) % count, i) for i in range(count)]),
            ],
            axis=dim,
        )
    return cells


def crop(cells, have, want):
    cut = have - want
    if cut == 0:
        return cells
    return cells[..., cut:cells.shape[-2] - cut, cut:cells.shape[-1] - cut]


def shrunk_neighbours(cells):
    centre = cells[:, :, 1:-1, 1:-1]
    along_x = cells[:, :, 1:-1, :-2] + cells[:, :, 1:-1, 2:]
    along_y = cells[:, :, :-2, 1:-1] + cells[:, :, 2:, 1:-1]
    along_z = jnp.roll(centre, 1, 1) + jnp.roll(centre, -1, 1)
    return along_x + along_y + along_z


def gather_kernel(axis, value, out, land, send_sem, recv_sem, own_sem):
    count = lax.axis_size(axis)
    me = lax.axis_index(axis)
    other = lax.axis_index("gy" if axis == "gx" else "gx")
    mesh_ids = pl.DeviceIdType.MESH

    def device(index):
        return (index, other) if axis == "gx" else (other, index)

    barrier = pltpu.get_barrier_semaphore()
    for step in range(1, count):
        pl.semaphore_signal(barrier, 1, device_id=device(lax.rem(me + step, count)),
                            device_id_type=mesh_ids)
    pl.semaphore_wait(barrier, count - 1)
    copies = []
    for step in range(1, count):
        copy = pltpu.make_async_remote_copy(
            src_ref=value,
            dst_ref=land.at[me],
            send_sem=send_sem.at[step],
            recv_sem=recv_sem.at[me],
            device_id=device(lax.rem(me + step, count)),
            device_id_type=mesh_ids,
        )
        copy.start()
        copies.append(copy)
    own = pltpu.make_async_copy(value, land.at[me], own_sem)
    own.start()
    for step in range(1, count):
        copies[step - 1].wait_send()
        source = lax.rem(me + count - step, count)
        pltpu.make_async_remote_copy(
            src_ref=value,
            dst_ref=land.at[source],
            send_sem=send_sem.at[step],
            recv_sem=recv_sem.at[source],
            device_id=device(source),
            device_id_type=mesh_ids,
        ).wait_recv()
    own.wait()
    out[...] = land[...]


def gather_axis(block, axis, tag):
    count = lax.axis_size(axis)
    vmem = pl.BlockSpec(memory_space=pltpu.VMEM)
    shape = (count,) + block.shape
    return pl.pallas_call(
        lambda *refs: gather_kernel(axis, *refs),
        out_shape=jax.ShapeDtypeStruct(shape, jnp.float32),
        in_specs=[vmem],
        out_specs=vmem,
        scratch_shapes=[
            pltpu.VMEM(shape, jnp.float32),
            pltpu.SemaphoreType.DMA((count,)),
            pltpu.SemaphoreType.DMA((count,)),
            pltpu.SemaphoreType.DMA(()),
        ],
        compiler_params=pltpu.CompilerParams(collective_id=tag, has_side_effects=True),
    )(block)


def global_max(block):
    for tag, axis in enumerate(("gx", "gy")):
        block = jnp.max(gather_axis(block, axis, tag), axis=0)
    return block


def restrict(field):
    lead, depth, rows, cols = field.shape
    count = lead * depth * rows
    pick_x = (lax.broadcasted_iota(jnp.int32, (cols, cols // 2), 0) // 2
              == lax.broadcasted_iota(jnp.int32, (cols, cols // 2), 1)).astype(jnp.float32)
    row = lax.broadcasted_iota(jnp.int32, (count // 4, count), 1)
    target = ((row // (depth * rows)) * (depth // 2) + (row // rows) % depth // 2) * (rows // 2) + row % rows // 2
    pick_rows = (lax.broadcasted_iota(jnp.int32, (count // 4, count), 0) == target).astype(jnp.float32)
    pairs = jnp.dot(field.reshape(count, cols), pick_x, precision=lax.Precision.HIGHEST)
    blocks = jnp.dot(pick_rows, pairs, precision=lax.Precision.HIGHEST)
    return (blocks * 0.125).reshape(lead, depth // 2, rows // 2, cols // 2)


def prolong(field):
    return jnp.repeat(jnp.repeat(jnp.repeat(field, 2, 1), 2, 2), 2, 3)


def diffusions(level):
    scale = 0.25**level
    return jnp.array(
        [substrate_diffusion * scale, catalyst_diffusion * scale], jnp.float32
    ).reshape(2, 1, 1, 1)


def coefficients(fields, level):
    scale = 0.25**level
    diff_first = substrate_diffusion * scale
    diff_second = catalyst_diffusion * scale
    substrate, catalyst, feed_rate, kill_rate = (fields[0], fields[1], fields[2], fields[3])
    product = substrate * catalyst
    squared = catalyst * catalyst
    self_first = inverse_step + squared + feed_rate + 6.0 * diff_first
    cross_first = 2.0 * product
    cross_second = -squared
    self_second = inverse_step + feed_rate + kill_rate - 2.0 * product + 6.0 * diff_second
    coeff = jnp.stack([self_first, cross_first, cross_second, self_second])
    return coeff, (6.0 * diff_first + cross_first) / self_first, (6.0 * diff_second + squared) / self_second


class Level:
    def __init__(self, coeff, halo, level):
        self.coeff = coeff
        self.halo = halo
        self.level = level

    def at(self, halo):
        return crop(self.coeff, self.halo, halo)

    def operate(self, field, halo):
        coeff = self.at(halo - 1)
        centre = crop(field, halo, halo - 1)
        first = coeff[0] * centre[0] + coeff[1] * centre[1]
        second = coeff[2] * centre[0] + coeff[3] * centre[1]
        return jnp.stack([first, second]) - diffusions(self.level) * shrunk_neighbours(field)

    def diagonal(self, halo):
        coeff = self.at(halo)
        return jnp.stack([coeff[0], coeff[3]])


def chebyshev(ops, source, source_halo, start, start_halo, spread):
    upper = 1.0 + spread
    lower = lower_fraction * upper
    centre = (upper + lower) / 2.0
    half_width = (upper - lower) / 2.0
    ratio = centre / half_width
    damping = 1.0 / ratio
    if start is None:
        halo = source_halo
        resid = source / ops.diagonal(halo)
        update = resid / centre
        iterate = update
    else:
        halo = min(source_halo, start_halo - 1)
        applied = ops.operate(start, start_halo)
        resid = (crop(source, source_halo, halo) - crop(applied, start_halo - 1, halo)) / ops.diagonal(halo)
        update = resid / centre
        iterate = crop(start, start_halo, halo) + update
    for sweep in range(2):
        applied = ops.operate(iterate, halo)
        halo = halo - 1
        resid = (crop(source, source_halo, halo) - applied) / ops.diagonal(halo)
        damping_next = 1.0 / (2.0 * ratio - damping)
        update = damping_next * damping * crop(update, halo + 1, halo) + 2.0 * damping_next / half_width * resid
        iterate = crop(iterate, halo + 1, halo) + update
        damping = damping_next
    return iterate, halo


def body(state, previous, feed, kill):
    deep = 3
    fields = jnp.concatenate([state, feed[None], kill[None]], 0)
    fields_1 = restrict(fields)
    fields_2 = restrict(fields_1)
    lane = lax.broadcasted_iota(jnp.int32, (8, 128), 1)
    local = jnp.zeros((8, 128), jnp.float32)
    for level, level_fields in enumerate((fields, fields_1, fields_2)):
        _, first, second = coefficients(level_fields, level)
        local = jnp.where(lane == level, jnp.maximum(jnp.max(first), jnp.max(second)), local)
    spreads = global_max(local)[0]

    wide = padded(jnp.concatenate([fields, previous], 0), deep + 1)
    ops_0 = Level(coefficients(crop(wide[:4], deep + 1, deep), 0)[0], deep, 0)
    state_w = wide[:2]
    substrate, catalyst = crop(state_w[0], deep + 1, deep), crop(state_w[1], deep + 1, deep)
    centre = crop(state_w, deep + 1, deep)
    reaction = substrate * catalyst * catalyst
    laplace = shrunk_neighbours(state_w) - 6.0 * centre
    feed_w = crop(wide[2], deep + 1, deep)
    kill_w = crop(wide[3], deep + 1, deep)
    previous_w = crop(wide[4:6], deep + 1, deep)
    local_terms = jnp.stack(
        [reaction - feed_w * (1.0 - substrate), -reaction + (feed_w + kill_w) * catalyst]
    )
    nonlinear = inverse_step * (centre - previous_w) - diffusions(0) * laplace + local_terms
    source_0 = -nonlinear
    pre_0, pre_0_halo = chebyshev(ops_0, source_0, deep, None, None, spreads[0])
    resid_0 = crop(source_0, deep, 0) - ops_0.operate(crop(pre_0, pre_0_halo, 1), 1)

    wide_1 = padded(jnp.concatenate([restrict(resid_0), fields_1], 0), deep)
    ops_1 = Level(coefficients(wide_1[2:], 1)[0], deep, 1)
    source_1 = wide_1[:2]
    pre_1, pre_1_halo = chebyshev(ops_1, source_1, deep, None, None, spreads[1])
    resid_1 = crop(source_1, deep, 0) - ops_1.operate(crop(pre_1, pre_1_halo, 1), 1)

    wide_2 = padded(jnp.concatenate([restrict(resid_1), fields_2], 0), deep)
    ops_2 = Level(coefficients(wide_2[2:], 2)[0], deep, 2)
    source_2 = wide_2[:2]
    first_2, first_2_halo = chebyshev(ops_2, source_2, deep, None, None, spreads[2])
    start_2 = padded(crop(first_2, first_2_halo, 0), deep)
    coarse_2, coarse_2_halo = chebyshev(ops_2, source_2, deep, start_2, deep, spreads[2])

    start_1 = padded(crop(pre_1, pre_1_halo, 0) + prolong(crop(coarse_2, coarse_2_halo, 0)), deep)
    post_1, post_1_halo = chebyshev(ops_1, source_1, deep, start_1, deep, spreads[1])

    start_0 = padded(crop(pre_0, pre_0_halo, 0) + prolong(crop(post_1, post_1_halo, 0)), deep)
    post_0, post_0_halo = chebyshev(ops_0, source_0, deep, start_0, deep, spreads[0])
    return crop(post_0, post_0_halo, 0)


def solution(mesh):
    placed = (
        P(None, None, "gy", "gx"),
        P(None, None, "gy", "gx"),
        P(None, "gy", "gx"),
        P(None, "gy", "gx"),
    )
    return jax.shard_map(
        body, mesh=mesh, in_specs=placed, out_specs=P(None, None, "gy", "gx"), check_vma=False
    )
```

```python
import jax
import jax.numpy as jnp
from jax import lax
from jax.sharding import PartitionSpec as P
from jax.experimental import pallas as pl
from jax.experimental.pallas import tpu as pltpu

substrate_diffusion = 40.0
catalyst_diffusion = 20.0
inverse_step = 2.0
lower_fraction = 0.25
coarsenings = 2


def padded(cells, width):
    for axis, dim in (("gx", 3), ("gy", 2)):
        count = lax.axis_size(axis)
        size = cells.shape[dim]
        head = lax.slice_in_dim(cells, 0, width, axis=dim)
        tail = lax.slice_in_dim(cells, size - width, size, axis=dim)
        cells = jnp.concatenate(
            [
                lax.ppermute(tail, axis, [(i, (i + 1) % count) for i in range(count)]),
                cells,
                lax.ppermute(head, axis, [((i + 1) % count, i) for i in range(count)]),
            ],
            axis=dim,
        )
    return cells


def crop(cells, have, want):
    cut = have - want
    assert cut >= 0
    if cut == 0:
        return cells
    return cells[..., cut:cells.shape[-2] - cut, cut:cells.shape[-1] - cut]


def shrunk_neighbours(cells):
    centre = cells[:, :, 1:-1, 1:-1]
    along_x = cells[:, :, 1:-1, :-2] + cells[:, :, 1:-1, 2:]
    along_y = cells[:, :, :-2, 1:-1] + cells[:, :, 2:, 1:-1]
    along_z = jnp.roll(centre, 1, 1) + jnp.roll(centre, -1, 1)
    return along_x + along_y + along_z


def gather_kernel(axis, value, out, land, send_sem, recv_sem, own_sem):
    count = lax.axis_size(axis)
    me = lax.axis_index(axis)
    other = lax.axis_index("gy" if axis == "gx" else "gx")
    mesh_ids = pl.DeviceIdType.MESH

    def device(index):
        return (index, other) if axis == "gx" else (other, index)

    barrier = pltpu.get_barrier_semaphore()
    for step in range(1, count):
        pl.semaphore_signal(barrier, 1, device_id=device(lax.rem(me + step, count)),
                            device_id_type=mesh_ids)
    pl.semaphore_wait(barrier, count - 1)
    copies = []
    for step in range(1, count):
        copy = pltpu.make_async_remote_copy(
            src_ref=value,
            dst_ref=land.at[me],
            send_sem=send_sem.at[step],
            recv_sem=recv_sem.at[me],
            device_id=device(lax.rem(me + step, count)),
            device_id_type=mesh_ids,
        )
        copy.start()
        copies.append(copy)
    own = pltpu.make_async_copy(value, land.at[me], own_sem)
    own.start()
    for step in range(1, count):
        copies[step - 1].wait_send()
        source = lax.rem(me + count - step, count)
        pltpu.make_async_remote_copy(
            src_ref=value,
            dst_ref=land.at[source],
            send_sem=send_sem.at[step],
            recv_sem=recv_sem.at[source],
            device_id=device(source),
            device_id_type=mesh_ids,
        ).wait_recv()
    own.wait()
    out[...] = land[...]


def gather_axis(block, axis, tag):
    count = lax.axis_size(axis)
    vmem = pl.BlockSpec(memory_space=pltpu.VMEM)
    shape = (count,) + block.shape
    return pl.pallas_call(
        lambda *refs: gather_kernel(axis, *refs),
        out_shape=jax.ShapeDtypeStruct(shape, jnp.float32),
        in_specs=[vmem],
        out_specs=vmem,
        scratch_shapes=[
            pltpu.VMEM(shape, jnp.float32),
            pltpu.SemaphoreType.DMA((count,)),
            pltpu.SemaphoreType.DMA((count,)),
            pltpu.SemaphoreType.DMA(()),
        ],
        compiler_params=pltpu.CompilerParams(collective_id=tag, has_side_effects=True),
    )(block)


def global_max(block):
    for tag, axis in enumerate(("gx", "gy")):
        block = jnp.max(gather_axis(block, axis, tag), axis=0)
    return block


def restrict(field):
    lead, depth, rows, cols = field.shape
    count = lead * depth * rows
    pick_x = (lax.broadcasted_iota(jnp.int32, (cols, cols // 2), 0) // 2
              == lax.broadcasted_iota(jnp.int32, (cols, cols // 2), 1)).astype(jnp.float32)
    row = lax.broadcasted_iota(jnp.int32, (count // 4, count), 1)
    target = ((row // (depth * rows)) * (depth // 2) + (row // rows) % depth // 2) * (rows // 2) + row % rows // 2
    pick_rows = (lax.broadcasted_iota(jnp.int32, (count // 4, count), 0) == target).astype(jnp.float32)
    pairs = jnp.dot(field.reshape(count, cols), pick_x, precision=lax.Precision.HIGHEST)
    blocks = jnp.dot(pick_rows, pairs, precision=lax.Precision.HIGHEST)
    return (blocks * 0.125).reshape(lead, depth // 2, rows // 2, cols // 2)


def prolong(field):
    return jnp.repeat(jnp.repeat(jnp.repeat(field, 2, 1), 2, 2), 2, 3)


def diffusions(level):
    scale = 0.25**level
    return jnp.array(
        [substrate_diffusion * scale, catalyst_diffusion * scale], jnp.float32
    ).reshape(2, 1, 1, 1)


def coefficients(fields, level):
    scale = 0.25**level
    diff_first = substrate_diffusion * scale
    diff_second = catalyst_diffusion * scale
    substrate, catalyst, feed_rate, kill_rate = (fields[0], fields[1], fields[2], fields[3])
    product = substrate * catalyst
    squared = catalyst * catalyst
    self_first = inverse_step + squared + feed_rate + 6.0 * diff_first
    cross_first = 2.0 * product
    cross_second = -squared
    self_second = inverse_step + feed_rate + kill_rate - 2.0 * product + 6.0 * diff_second
    coeff = jnp.stack([self_first, cross_first, cross_second, self_second])
    return coeff, (6.0 * diff_first + cross_first) / self_first, (6.0 * diff_second + squared) / self_second


class Level:
    def __init__(self, coeff, halo, level):
        self.coeff = coeff
        self.halo = halo
        self.level = level

    def at(self, halo):
        return crop(self.coeff, self.halo, halo)

    def operate(self, field, halo):
        coeff = self.at(halo - 1)
        centre = crop(field, halo, halo - 1)
        first = coeff[0] * centre[0] + coeff[1] * centre[1]
        second = coeff[2] * centre[0] + coeff[3] * centre[1]
        return jnp.stack([first, second]) - diffusions(self.level) * shrunk_neighbours(field)

    def diagonal(self, halo):
        coeff = self.at(halo)
        return jnp.stack([coeff[0], coeff[3]])


def chebyshev(ops, source, source_halo, start, start_halo, spread):
    upper = 1.0 + spread
    lower = lower_fraction * upper
    centre = (upper + lower) / 2.0
    half_width = (upper - lower) / 2.0
    ratio = centre / half_width
    damping = 1.0 / ratio
    if start is None:
        halo = source_halo
        resid = source / ops.diagonal(halo)
        update = resid / centre
        iterate = update
    else:
        halo = min(source_halo, start_halo - 1)
        applied = ops.operate(start, start_halo)
        resid = (crop(source, source_halo, halo) - crop(applied, start_halo - 1, halo)) / ops.diagonal(halo)
        update = resid / centre
        iterate = crop(start, start_halo, halo) + update
    for sweep in range(2):
        applied = ops.operate(iterate, halo)
        halo = halo - 1
        resid = (crop(source, source_halo, halo) - applied) / ops.diagonal(halo)
        damping_next = 1.0 / (2.0 * ratio - damping)
        update = damping_next * damping * crop(update, halo + 1, halo) + 2.0 * damping_next / half_width * resid
        iterate = crop(iterate, halo + 1, halo) + update
        damping = damping_next
    return iterate, halo


def body(state, previous, feed, kill):
    deep = 3
    fields = jnp.concatenate([state, feed[None], kill[None]], 0)
    fields_1 = restrict(fields)
    fields_2 = restrict(fields_1)
    lane = lax.broadcasted_iota(jnp.int32, (8, 128), 1)
    local = jnp.zeros((8, 128), jnp.float32)
    for level, level_fields in enumerate((fields, fields_1, fields_2)):
        _, first, second = coefficients(level_fields, level)
        local = jnp.where(lane == level, jnp.maximum(jnp.max(first), jnp.max(second)), local)
    spreads = global_max(local)[0]

    wide = padded(jnp.concatenate([fields, previous], 0), 14)
    ops_0 = Level(coefficients(crop(wide[:4], 14, 13), 0)[0], 13, 0)
    state_w = wide[:2]
    substrate, catalyst = crop(state_w[0], 14, 13), crop(state_w[1], 14, 13)
    centre = crop(state_w, 14, 13)
    reaction = substrate * catalyst * catalyst
    laplace = shrunk_neighbours(state_w) - 6.0 * centre
    feed_w = crop(wide[2], 14, 13)
    kill_w = crop(wide[3], 14, 13)
    previous_w = crop(wide[4:6], 14, 13)
    local_terms = jnp.stack(
        [reaction - feed_w * (1.0 - substrate), -reaction + (feed_w + kill_w) * catalyst]
    )
    nonlinear = inverse_step * (centre - previous_w) - diffusions(0) * laplace + local_terms
    source_0 = -nonlinear
    pre_0, pre_0_halo = chebyshev(ops_0, source_0, 13, None, None, spreads[0])
    resid_0 = crop(source_0, 13, 10) - ops_0.operate(crop(pre_0, pre_0_halo, 11), 11)

    source_1 = restrict(resid_0)
    ops_1 = Level(coefficients(restrict(crop(wide[:4], 14, 10)), 1)[0], 5, 1)
    pre_1, pre_1_halo = chebyshev(ops_1, source_1, 5, None, None, spreads[1])
    resid_1 = crop(source_1, 5, 0) - ops_1.operate(crop(pre_1, pre_1_halo, 1), 1)

    wide_2 = padded(jnp.concatenate([restrict(resid_1), fields_2], 0), deep)
    ops_2 = Level(coefficients(wide_2[2:], 2)[0], deep, 2)
    source_2 = wide_2[:2]
    first_2, first_2_halo = chebyshev(ops_2, source_2, deep, None, None, spreads[2])
    start_2 = padded(crop(first_2, first_2_halo, 0), deep)
    coarse_2, coarse_2_halo = chebyshev(ops_2, source_2, deep, start_2, deep, spreads[2])

    start_1 = padded(crop(pre_1, pre_1_halo, 0) + prolong(crop(coarse_2, coarse_2_halo, 0)), 5)
    post_1, post_1_halo = chebyshev(ops_1, source_1, 5, start_1, 5, spreads[1])

    start_0 = crop(pre_0, pre_0_halo, 3) + crop(prolong(post_1), 2 * post_1_halo, 3)
    post_0, post_0_halo = chebyshev(ops_0, source_0, 13, start_0, 3, spreads[0])
    return crop(post_0, post_0_halo, 0)


def solution(mesh):
    placed = (
        P(None, None, "gy", "gx"),
        P(None, None, "gy", "gx"),
        P(None, "gy", "gx"),
        P(None, "gy", "gx"),
    )
    return jax.shard_map(
        body, mesh=mesh, in_specs=placed, out_specs=P(None, None, "gy", "gx"), check_vma=False
    )
```

```python
import jax
import jax.numpy as jnp
from jax import lax
from jax.sharding import PartitionSpec as P
from jax.experimental import pallas as pl
from jax.experimental.pallas import tpu as pltpu

substrate_diffusion = 40.0
catalyst_diffusion = 20.0
inverse_step = 2.0
lower_fraction = 0.25
coarsenings = 2


def padded(cells, width):
    for axis, dim in (("gx", 3), ("gy", 2)):
        count = lax.axis_size(axis)
        size = cells.shape[dim]
        head = lax.slice_in_dim(cells, 0, width, axis=dim)
        tail = lax.slice_in_dim(cells, size - width, size, axis=dim)
        cells = jnp.concatenate(
            [
                lax.ppermute(tail, axis, [(i, (i + 1) % count) for i in range(count)]),
                cells,
                lax.ppermute(head, axis, [((i + 1) % count, i) for i in range(count)]),
            ],
            axis=dim,
        )
    return cells


def crop(cells, have, want):
    cut = have - want
    assert cut >= 0
    if cut == 0:
        return cells
    return cells[..., cut:cells.shape[-2] - cut, cut:cells.shape[-1] - cut]


def shrunk_neighbours(cells):
    centre = cells[:, :, 1:-1, 1:-1]
    along_x = cells[:, :, 1:-1, :-2] + cells[:, :, 1:-1, 2:]
    along_y = cells[:, :, :-2, 1:-1] + cells[:, :, 2:, 1:-1]
    along_z = jnp.roll(centre, 1, 1) + jnp.roll(centre, -1, 1)
    return along_x + along_y + along_z


def gather_kernel(axis, value, out, land, send_sem, recv_sem, own_sem):
    count = lax.axis_size(axis)
    me = lax.axis_index(axis)
    other = lax.axis_index("gy" if axis == "gx" else "gx")
    mesh_ids = pl.DeviceIdType.MESH

    def device(index):
        return (index, other) if axis == "gx" else (other, index)

    barrier = pltpu.get_barrier_semaphore()
    for step in range(1, count):
        pl.semaphore_signal(barrier, 1, device_id=device(lax.rem(me + step, count)),
                            device_id_type=mesh_ids)
    pl.semaphore_wait(barrier, count - 1)
    copies = []
    for step in range(1, count):
        copy = pltpu.make_async_remote_copy(
            src_ref=value,
            dst_ref=land.at[me],
            send_sem=send_sem.at[step],
            recv_sem=recv_sem.at[me],
            device_id=device(lax.rem(me + step, count)),
            device_id_type=mesh_ids,
        )
        copy.start()
        copies.append(copy)
    own = pltpu.make_async_copy(value, land.at[me], own_sem)
    own.start()
    for step in range(1, count):
        copies[step - 1].wait_send()
        source = lax.rem(me + count - step, count)
        pltpu.make_async_remote_copy(
            src_ref=value,
            dst_ref=land.at[source],
            send_sem=send_sem.at[step],
            recv_sem=recv_sem.at[source],
            device_id=device(source),
            device_id_type=mesh_ids,
        ).wait_recv()
    own.wait()
    out[...] = land[...]


def gather_axis(block, axis, tag):
    count = lax.axis_size(axis)
    vmem = pl.BlockSpec(memory_space=pltpu.VMEM)
    shape = (count,) + block.shape
    return pl.pallas_call(
        lambda *refs: gather_kernel(axis, *refs),
        out_shape=jax.ShapeDtypeStruct(shape, jnp.float32),
        in_specs=[vmem],
        out_specs=vmem,
        scratch_shapes=[
            pltpu.VMEM(shape, jnp.float32),
            pltpu.SemaphoreType.DMA((count,)),
            pltpu.SemaphoreType.DMA((count,)),
            pltpu.SemaphoreType.DMA(()),
        ],
        compiler_params=pltpu.CompilerParams(collective_id=tag, has_side_effects=True),
    )(block)


def global_max(block):
    for tag, axis in enumerate(("gx", "gy")):
        block = jnp.max(gather_axis(block, axis, tag), axis=0)
    return block


def restrict(field):
    lead, depth, rows, cols = field.shape
    count = lead * depth * rows
    pick_x = (lax.broadcasted_iota(jnp.int32, (cols, cols // 2), 0) // 2
              == lax.broadcasted_iota(jnp.int32, (cols, cols // 2), 1)).astype(jnp.float32)
    row = lax.broadcasted_iota(jnp.int32, (count // 4, count), 1)
    target = ((row // (depth * rows)) * (depth // 2) + (row // rows) % depth // 2) * (rows // 2) + row % rows // 2
    pick_rows = (lax.broadcasted_iota(jnp.int32, (count // 4, count), 0) == target).astype(jnp.float32)
    pairs = jnp.dot(field.reshape(count, cols), pick_x, precision=lax.Precision.HIGHEST)
    blocks = jnp.dot(pick_rows, pairs, precision=lax.Precision.HIGHEST)
    return (blocks * 0.125).reshape(lead, depth // 2, rows // 2, cols // 2)


def prolong(field):
    return jnp.repeat(jnp.repeat(jnp.repeat(field, 2, 1), 2, 2), 2, 3)


def diffusions(level):
    scale = 0.25**level
    return jnp.array(
        [substrate_diffusion * scale, catalyst_diffusion * scale], jnp.float32
    ).reshape(2, 1, 1, 1)


def coefficients(fields, level):
    scale = 0.25**level
    diff_first = substrate_diffusion * scale
    diff_second = catalyst_diffusion * scale
    substrate, catalyst, feed_rate, kill_rate = (fields[0], fields[1], fields[2], fields[3])
    product = substrate * catalyst
    squared = catalyst * catalyst
    self_first = inverse_step + squared + feed_rate + 6.0 * diff_first
    cross_first = 2.0 * product
    cross_second = -squared
    self_second = inverse_step + feed_rate + kill_rate - 2.0 * product + 6.0 * diff_second
    coeff = jnp.stack([self_first, cross_first, cross_second, self_second])
    return coeff, (6.0 * diff_first + cross_first) / self_first, (6.0 * diff_second + squared) / self_second


class Level:
    def __init__(self, coeff, halo, level):
        self.coeff = coeff
        self.halo = halo
        self.level = level

    def at(self, halo):
        return crop(self.coeff, self.halo, halo)

    def operate(self, field, halo):
        coeff = self.at(halo - 1)
        centre = crop(field, halo, halo - 1)
        first = coeff[0] * centre[0] + coeff[1] * centre[1]
        second = coeff[2] * centre[0] + coeff[3] * centre[1]
        return jnp.stack([first, second]) - diffusions(self.level) * shrunk_neighbours(field)

    def diagonal(self, halo):
        coeff = self.at(halo)
        return jnp.stack([coeff[0], coeff[3]])


def chebyshev(ops, source, source_halo, start, start_halo, spread):
    upper = 1.0 + spread
    lower = lower_fraction * upper
    centre = (upper + lower) / 2.0
    half_width = (upper - lower) / 2.0
    ratio = centre / half_width
    damping = 1.0 / ratio
    if start is None:
        halo = source_halo
        resid = source / ops.diagonal(halo)
        update = resid / centre
        iterate = update
    else:
        halo = min(source_halo, start_halo - 1)
        applied = ops.operate(start, start_halo)
        resid = (crop(source, source_halo, halo) - crop(applied, start_halo - 1, halo)) / ops.diagonal(halo)
        update = resid / centre
        iterate = crop(start, start_halo, halo) + update
    for sweep in range(2):
        applied = ops.operate(iterate, halo)
        halo = halo - 1
        resid = (crop(source, source_halo, halo) - applied) / ops.diagonal(halo)
        damping_next = 1.0 / (2.0 * ratio - damping)
        update = damping_next * damping * crop(update, halo + 1, halo) + 2.0 * damping_next / half_width * resid
        iterate = crop(iterate, halo + 1, halo) + update
        damping = damping_next
    return iterate, halo


def body(state, previous, feed, kill):
    deep = 3
    fields = jnp.concatenate([state, feed[None], kill[None]], 0)
    fields_1 = restrict(fields)
    fields_2 = restrict(fields_1)
    lane = lax.broadcasted_iota(jnp.int32, (8, 128), 1)
    local = jnp.zeros((8, 128), jnp.float32)
    for level, level_fields in enumerate((fields, fields_1, fields_2)):
        _, first, second = coefficients(level_fields, level)
        local = jnp.where(lane == level, jnp.maximum(jnp.max(first), jnp.max(second)), local)
    spreads = global_max(local)[0]

    wide = padded(jnp.concatenate([fields, previous], 0), 6)
    ops_0 = Level(coefficients(crop(wide[:4], 6, 5), 0)[0], 5, 0)
    state_w = wide[:2]
    substrate, catalyst = crop(state_w[0], 6, 5), crop(state_w[1], 6, 5)
    centre = crop(state_w, 6, 5)
    reaction = substrate * catalyst * catalyst
    laplace = shrunk_neighbours(state_w) - 6.0 * centre
    feed_w = crop(wide[2], 6, 5)
    kill_w = crop(wide[3], 6, 5)
    previous_w = crop(wide[4:6], 6, 5)
    local_terms = jnp.stack(
        [reaction - feed_w * (1.0 - substrate), -reaction + (feed_w + kill_w) * catalyst]
    )
    nonlinear = inverse_step * (centre - previous_w) - diffusions(0) * laplace + local_terms
    source_0 = -nonlinear
    pre_0, pre_0_halo = chebyshev(ops_0, source_0, 5, None, None, spreads[0])
    resid_0 = crop(source_0, 5, 0) - ops_0.operate(crop(pre_0, pre_0_halo, 1), 1)

    wide_1 = padded(jnp.concatenate([restrict(resid_0), fields_1], 0), 5)
    ops_1 = Level(coefficients(wide_1[2:], 1)[0], 5, 1)
    source_1 = wide_1[:2]
    pre_1, pre_1_halo = chebyshev(ops_1, source_1, 5, None, None, spreads[1])
    resid_1 = crop(source_1, 5, 0) - ops_1.operate(crop(pre_1, pre_1_halo, 1), 1)

    wide_2 = padded(jnp.concatenate([restrict(resid_1), fields_2], 0), deep)
    ops_2 = Level(coefficients(wide_2[2:], 2)[0], deep, 2)
    source_2 = wide_2[:2]
    first_2, first_2_halo = chebyshev(ops_2, source_2, deep, None, None, spreads[2])
    start_2 = padded(crop(first_2, first_2_halo, 0), deep)
    coarse_2, coarse_2_halo = chebyshev(ops_2, source_2, deep, start_2, deep, spreads[2])

    start_1 = padded(crop(pre_1, pre_1_halo, 0) + prolong(crop(coarse_2, coarse_2_halo, 0)), 5)
    post_1, post_1_halo = chebyshev(ops_1, source_1, 5, start_1, 5, spreads[1])

    start_0 = crop(pre_0, pre_0_halo, 3) + crop(prolong(post_1), 2 * post_1_halo, 3)
    post_0, post_0_halo = chebyshev(ops_0, source_0, 5, start_0, 3, spreads[0])
    return crop(post_0, post_0_halo, 0)


def solution(mesh):
    placed = (
        P(None, None, "gy", "gx"),
        P(None, None, "gy", "gx"),
        P(None, "gy", "gx"),
        P(None, "gy", "gx"),
    )
    return jax.shard_map(
        body, mesh=mesh, in_specs=placed, out_specs=P(None, None, "gy", "gx"), check_vma=False
    )
```

```python
import jax
import jax.numpy as jnp
from jax import lax
from jax.sharding import PartitionSpec as P
from jax.experimental import pallas as pl
from jax.experimental.pallas import tpu as pltpu

substrate_diffusion = 40.0
catalyst_diffusion = 20.0
inverse_step = 2.0
lower_fraction = 0.25
coarsenings = 2


def padded(cells, width):
    for axis, dim in (("gx", 3), ("gy", 2)):
        count = lax.axis_size(axis)
        size = cells.shape[dim]
        below, above = [], []
        remaining, distance = width, 1
        while remaining > 0:
            take = min(remaining, size)
            tail = lax.slice_in_dim(cells, size - take, size, axis=dim)
            head = lax.slice_in_dim(cells, 0, take, axis=dim)
            below.insert(0, lax.ppermute(tail, axis, [(i, (i + distance) % count) for i in range(count)]))
            above.append(lax.ppermute(head, axis, [((i + distance) % count, i) for i in range(count)]))
            remaining -= take
            distance += 1
        cells = jnp.concatenate(below + [cells] + above, axis=dim)
    return cells


def crop(cells, have, want):
    cut = have - want
    assert cut >= 0
    if cut == 0:
        return cells
    return cells[..., cut:cells.shape[-2] - cut, cut:cells.shape[-1] - cut]


def shrunk_neighbours(cells):
    centre = cells[:, :, 1:-1, 1:-1]
    along_x = cells[:, :, 1:-1, :-2] + cells[:, :, 1:-1, 2:]
    along_y = cells[:, :, :-2, 1:-1] + cells[:, :, 2:, 1:-1]
    along_z = jnp.roll(centre, 1, 1) + jnp.roll(centre, -1, 1)
    return along_x + along_y + along_z


def gather_kernel(axis, value, out, land, send_sem, recv_sem, own_sem):
    count = lax.axis_size(axis)
    me = lax.axis_index(axis)
    other = lax.axis_index("gy" if axis == "gx" else "gx")
    mesh_ids = pl.DeviceIdType.MESH

    def device(index):
        return (index, other) if axis == "gx" else (other, index)

    barrier = pltpu.get_barrier_semaphore()
    for step in range(1, count):
        pl.semaphore_signal(barrier, 1, device_id=device(lax.rem(me + step, count)),
                            device_id_type=mesh_ids)
    pl.semaphore_wait(barrier, count - 1)
    copies = []
    for step in range(1, count):
        copy = pltpu.make_async_remote_copy(
            src_ref=value,
            dst_ref=land.at[me],
            send_sem=send_sem.at[step],
            recv_sem=recv_sem.at[me],
            device_id=device(lax.rem(me + step, count)),
            device_id_type=mesh_ids,
        )
        copy.start()
        copies.append(copy)
    own = pltpu.make_async_copy(value, land.at[me], own_sem)
    own.start()
    for step in range(1, count):
        copies[step - 1].wait_send()
        source = lax.rem(me + count - step, count)
        pltpu.make_async_remote_copy(
            src_ref=value,
            dst_ref=land.at[source],
            send_sem=send_sem.at[step],
            recv_sem=recv_sem.at[source],
            device_id=device(source),
            device_id_type=mesh_ids,
        ).wait_recv()
    own.wait()
    out[...] = land[...]


def gather_axis(block, axis, tag):
    count = lax.axis_size(axis)
    vmem = pl.BlockSpec(memory_space=pltpu.VMEM)
    shape = (count,) + block.shape
    return pl.pallas_call(
        lambda *refs: gather_kernel(axis, *refs),
        out_shape=jax.ShapeDtypeStruct(shape, jnp.float32),
        in_specs=[vmem],
        out_specs=vmem,
        scratch_shapes=[
            pltpu.VMEM(shape, jnp.float32),
            pltpu.SemaphoreType.DMA((count,)),
            pltpu.SemaphoreType.DMA((count,)),
            pltpu.SemaphoreType.DMA(()),
        ],
        compiler_params=pltpu.CompilerParams(collective_id=tag, has_side_effects=True),
    )(block)


def global_max(block):
    for tag, axis in enumerate(("gx", "gy")):
        block = jnp.max(gather_axis(block, axis, tag), axis=0)
    return block


def restrict(field):
    lead, depth, rows, cols = field.shape
    count = lead * depth * rows
    pick_x = (lax.broadcasted_iota(jnp.int32, (cols, cols // 2), 0) // 2
              == lax.broadcasted_iota(jnp.int32, (cols, cols // 2), 1)).astype(jnp.float32)
    row = lax.broadcasted_iota(jnp.int32, (count // 4, count), 1)
    target = ((row // (depth * rows)) * (depth // 2) + (row // rows) % depth // 2) * (rows // 2) + row % rows // 2
    pick_rows = (lax.broadcasted_iota(jnp.int32, (count // 4, count), 0) == target).astype(jnp.float32)
    pairs = jnp.dot(field.reshape(count, cols), pick_x, precision=lax.Precision.HIGHEST)
    blocks = jnp.dot(pick_rows, pairs, precision=lax.Precision.HIGHEST)
    return (blocks * 0.125).reshape(lead, depth // 2, rows // 2, cols // 2)


def prolong(field):
    return jnp.repeat(jnp.repeat(jnp.repeat(field, 2, 1), 2, 2), 2, 3)


def diffusions(level):
    scale = 0.25**level
    return jnp.array(
        [substrate_diffusion * scale, catalyst_diffusion * scale], jnp.float32
    ).reshape(2, 1, 1, 1)


def coefficients(fields, level):
    scale = 0.25**level
    diff_first = substrate_diffusion * scale
    diff_second = catalyst_diffusion * scale
    substrate, catalyst, feed_rate, kill_rate = (fields[0], fields[1], fields[2], fields[3])
    product = substrate * catalyst
    squared = catalyst * catalyst
    self_first = inverse_step + squared + feed_rate + 6.0 * diff_first
    cross_first = 2.0 * product
    cross_second = -squared
    self_second = inverse_step + feed_rate + kill_rate - 2.0 * product + 6.0 * diff_second
    coeff = jnp.stack([self_first, cross_first, cross_second, self_second])
    return coeff, (6.0 * diff_first + cross_first) / self_first, (6.0 * diff_second + squared) / self_second


class Level:
    def __init__(self, coeff, halo, level):
        self.coeff = coeff
        self.halo = halo
        self.level = level

    def at(self, halo):
        return crop(self.coeff, self.halo, halo)

    def operate(self, field, halo):
        coeff = self.at(halo - 1)
        centre = crop(field, halo, halo - 1)
        first = coeff[0] * centre[0] + coeff[1] * centre[1]
        second = coeff[2] * centre[0] + coeff[3] * centre[1]
        return jnp.stack([first, second]) - diffusions(self.level) * shrunk_neighbours(field)

    def diagonal(self, halo):
        coeff = self.at(halo)
        return jnp.stack([coeff[0], coeff[3]])


def chebyshev(ops, source, source_halo, start, start_halo, spread):
    upper = 1.0 + spread
    lower = lower_fraction * upper
    centre = (upper + lower) / 2.0
    half_width = (upper - lower) / 2.0
    ratio = centre / half_width
    damping = 1.0 / ratio
    if start is None:
        halo = source_halo
        resid = source / ops.diagonal(halo)
        update = resid / centre
        iterate = update
    else:
        halo = min(source_halo, start_halo - 1)
        applied = ops.operate(start, start_halo)
        resid = (crop(source, source_halo, halo) - crop(applied, start_halo - 1, halo)) / ops.diagonal(halo)
        update = resid / centre
        iterate = crop(start, start_halo, halo) + update
    for sweep in range(2):
        applied = ops.operate(iterate, halo)
        halo = halo - 1
        resid = (crop(source, source_halo, halo) - applied) / ops.diagonal(halo)
        damping_next = 1.0 / (2.0 * ratio - damping)
        update = damping_next * damping * crop(update, halo + 1, halo) + 2.0 * damping_next / half_width * resid
        iterate = crop(iterate, halo + 1, halo) + update
        damping = damping_next
    return iterate, halo


def body(state, previous, feed, kill):
    deep = 3
    fields = jnp.concatenate([state, feed[None], kill[None]], 0)
    fields_1 = restrict(fields)
    fields_2 = restrict(fields_1)
    lane = lax.broadcasted_iota(jnp.int32, (8, 128), 1)
    local = jnp.zeros((8, 128), jnp.float32)
    for level, level_fields in enumerate((fields, fields_1, fields_2)):
        _, first, second = coefficients(level_fields, level)
        local = jnp.where(lane == level, jnp.maximum(jnp.max(first), jnp.max(second)), local)
    spreads = global_max(local)[0]

    wide = padded(jnp.concatenate([fields, previous], 0), 6)
    ops_0 = Level(coefficients(crop(wide[:4], 6, 5), 0)[0], 5, 0)
    state_w = wide[:2]
    substrate, catalyst = crop(state_w[0], 6, 5), crop(state_w[1], 6, 5)
    centre = crop(state_w, 6, 5)
    reaction = substrate * catalyst * catalyst
    laplace = shrunk_neighbours(state_w) - 6.0 * centre
    feed_w = crop(wide[2], 6, 5)
    kill_w = crop(wide[3], 6, 5)
    previous_w = crop(wide[4:6], 6, 5)
    local_terms = jnp.stack(
        [reaction - feed_w * (1.0 - substrate), -reaction + (feed_w + kill_w) * catalyst]
    )
    nonlinear = inverse_step * (centre - previous_w) - diffusions(0) * laplace + local_terms
    source_0 = -nonlinear
    pre_0, pre_0_halo = chebyshev(ops_0, source_0, 5, None, None, spreads[0])
    resid_0 = crop(source_0, 5, 0) - ops_0.operate(crop(pre_0, pre_0_halo, 1), 1)

    wide_1 = padded(jnp.concatenate([restrict(resid_0), fields_1], 0), 7)
    ops_1 = Level(coefficients(wide_1[2:], 1)[0], 7, 1)
    source_1 = wide_1[:2]
    pre_1, pre_1_halo = chebyshev(ops_1, source_1, 7, None, None, spreads[1])
    resid_1 = crop(source_1, 7, 0) - ops_1.operate(crop(pre_1, pre_1_halo, 1), 1)

    wide_2 = padded(jnp.concatenate([restrict(resid_1), fields_2], 0), 8)
    ops_2 = Level(coefficients(wide_2[2:], 2)[0], 8, 2)
    source_2 = wide_2[:2]
    first_2, first_2_halo = chebyshev(ops_2, source_2, 8, None, None, spreads[2])
    coarse_2, coarse_2_halo = chebyshev(ops_2, source_2, 8, first_2, first_2_halo, spreads[2])

    start_1 = crop(pre_1, pre_1_halo, 5) + crop(prolong(coarse_2), 2 * coarse_2_halo, 5)
    post_1, post_1_halo = chebyshev(ops_1, source_1, 7, start_1, 5, spreads[1])

    start_0 = crop(pre_0, pre_0_halo, 3) + crop(prolong(post_1), 2 * post_1_halo, 3)
    post_0, post_0_halo = chebyshev(ops_0, source_0, 5, start_0, 3, spreads[0])
    return crop(post_0, post_0_halo, 0)


def solution(mesh):
    placed = (
        P(None, None, "gy", "gx"),
        P(None, None, "gy", "gx"),
        P(None, "gy", "gx"),
        P(None, "gy", "gx"),
    )
    return jax.shard_map(
        body, mesh=mesh, in_specs=placed, out_specs=P(None, None, "gy", "gx"), check_vma=False
    )
```

```python
import jax
import jax.numpy as jnp
from jax import lax
from jax.sharding import PartitionSpec as P
from jax.experimental import pallas as pl
from jax.experimental.pallas import tpu as pltpu

substrate_diffusion = 40.0
catalyst_diffusion = 20.0
inverse_step = 2.0
lower_fraction = 0.25
coarsenings = 2


def padded_along(cells, width, axis, dim):
    count = lax.axis_size(axis)
    size = cells.shape[dim]
    below, above = [], []
    remaining, distance = width, 1
    while remaining > 0:
        take = min(remaining, size)
        tail = lax.slice_in_dim(cells, size - take, size, axis=dim)
        head = lax.slice_in_dim(cells, 0, take, axis=dim)
        below.insert(0, lax.ppermute(tail, axis, [(i, (i + distance) % count) for i in range(count)]))
        above.append(lax.ppermute(head, axis, [((i + distance) % count, i) for i in range(count)]))
        remaining -= take
        distance += 1
    return jnp.concatenate(below + [cells] + above, axis=dim)


def padded(cells, width):
    return padded_along(padded_along(cells, width, "gx", 3), width, "gy", 2)


def crop(cells, have, want):
    cut = have - want
    assert cut >= 0
    if cut == 0:
        return cells
    return cells[..., cut:cells.shape[-2] - cut, cut:cells.shape[-1] - cut]


def shrunk_neighbours(cells):
    centre = cells[:, :, 1:-1, 1:-1]
    along_x = cells[:, :, 1:-1, :-2] + cells[:, :, 1:-1, 2:]
    along_y = cells[:, :, :-2, 1:-1] + cells[:, :, 2:, 1:-1]
    along_z = jnp.roll(centre, 1, 1) + jnp.roll(centre, -1, 1)
    return along_x + along_y + along_z


def gather_kernel(axis, value, out, land, send_sem, recv_sem, own_sem):
    count = lax.axis_size(axis)
    me = lax.axis_index(axis)
    other = lax.axis_index("gy" if axis == "gx" else "gx")
    mesh_ids = pl.DeviceIdType.MESH

    def device(index):
        return (index, other) if axis == "gx" else (other, index)

    barrier = pltpu.get_barrier_semaphore()
    for step in range(1, count):
        pl.semaphore_signal(barrier, 1, device_id=device(lax.rem(me + step, count)),
                            device_id_type=mesh_ids)
    pl.semaphore_wait(barrier, count - 1)
    copies = []
    for step in range(1, count):
        copy = pltpu.make_async_remote_copy(
            src_ref=value,
            dst_ref=land.at[me],
            send_sem=send_sem.at[step],
            recv_sem=recv_sem.at[me],
            device_id=device(lax.rem(me + step, count)),
            device_id_type=mesh_ids,
        )
        copy.start()
        copies.append(copy)
    own = pltpu.make_async_copy(value, land.at[me], own_sem)
    own.start()
    for step in range(1, count):
        copies[step - 1].wait_send()
        source = lax.rem(me + count - step, count)
        pltpu.make_async_remote_copy(
            src_ref=value,
            dst_ref=land.at[source],
            send_sem=send_sem.at[step],
            recv_sem=recv_sem.at[source],
            device_id=device(source),
            device_id_type=mesh_ids,
        ).wait_recv()
    own.wait()
    out[...] = land[...]


def gather_axis(block, axis, tag):
    count = lax.axis_size(axis)
    vmem = pl.BlockSpec(memory_space=pltpu.VMEM)
    shape = (count,) + block.shape
    return pl.pallas_call(
        lambda *refs: gather_kernel(axis, *refs),
        out_shape=jax.ShapeDtypeStruct(shape, jnp.float32),
        in_specs=[vmem],
        out_specs=vmem,
        scratch_shapes=[
            pltpu.VMEM(shape, jnp.float32),
            pltpu.SemaphoreType.DMA((count,)),
            pltpu.SemaphoreType.DMA((count,)),
            pltpu.SemaphoreType.DMA(()),
        ],
        compiler_params=pltpu.CompilerParams(collective_id=tag, has_side_effects=True),
    )(block)


def global_max(block):
    for tag, axis in enumerate(("gx", "gy")):
        block = jnp.max(gather_axis(block, axis, tag), axis=0)
    return block


def restrict(field):
    lead, depth, rows, cols = field.shape
    count = lead * depth * rows
    pick_x = (lax.broadcasted_iota(jnp.int32, (cols, cols // 2), 0) // 2
              == lax.broadcasted_iota(jnp.int32, (cols, cols // 2), 1)).astype(jnp.float32)
    row = lax.broadcasted_iota(jnp.int32, (count // 4, count), 1)
    target = ((row // (depth * rows)) * (depth // 2) + (row // rows) % depth // 2) * (rows // 2) + row % rows // 2
    pick_rows = (lax.broadcasted_iota(jnp.int32, (count // 4, count), 0) == target).astype(jnp.float32)
    pairs = jnp.dot(field.reshape(count, cols), pick_x, precision=lax.Precision.HIGHEST)
    blocks = jnp.dot(pick_rows, pairs, precision=lax.Precision.HIGHEST)
    return (blocks * 0.125).reshape(lead, depth // 2, rows // 2, cols // 2)


def prolong(field):
    return jnp.repeat(jnp.repeat(jnp.repeat(field, 2, 1), 2, 2), 2, 3)


def diffusions(level):
    scale = 0.25**level
    return jnp.array(
        [substrate_diffusion * scale, catalyst_diffusion * scale], jnp.float32
    ).reshape(2, 1, 1, 1)


def coefficients(fields, level):
    scale = 0.25**level
    diff_first = substrate_diffusion * scale
    diff_second = catalyst_diffusion * scale
    substrate, catalyst, feed_rate, kill_rate = (fields[0], fields[1], fields[2], fields[3])
    product = substrate * catalyst
    squared = catalyst * catalyst
    self_first = inverse_step + squared + feed_rate + 6.0 * diff_first
    cross_first = 2.0 * product
    cross_second = -squared
    self_second = inverse_step + feed_rate + kill_rate - 2.0 * product + 6.0 * diff_second
    coeff = jnp.stack([self_first, cross_first, cross_second, self_second])
    return coeff, (6.0 * diff_first + cross_first) / self_first, (6.0 * diff_second + squared) / self_second


class Level:
    def __init__(self, coeff, halo, level):
        self.coeff = coeff
        self.halo = halo
        self.level = level

    def at(self, halo):
        return crop(self.coeff, self.halo, halo)

    def operate(self, field, halo):
        coeff = self.at(halo - 1)
        centre = crop(field, halo, halo - 1)
        first = coeff[0] * centre[0] + coeff[1] * centre[1]
        second = coeff[2] * centre[0] + coeff[3] * centre[1]
        return jnp.stack([first, second]) - diffusions(self.level) * shrunk_neighbours(field)

    def diagonal(self, halo):
        coeff = self.at(halo)
        return jnp.stack([coeff[0], coeff[3]])


def chebyshev(ops, source, source_halo, start, start_halo, spread):
    upper = 1.0 + spread
    lower = lower_fraction * upper
    centre = (upper + lower) / 2.0
    half_width = (upper - lower) / 2.0
    ratio = centre / half_width
    damping = 1.0 / ratio
    if start is None:
        halo = source_halo
        resid = source / ops.diagonal(halo)
        update = resid / centre
        iterate = update
    else:
        halo = min(source_halo, start_halo - 1)
        applied = ops.operate(start, start_halo)
        resid = (crop(source, source_halo, halo) - crop(applied, start_halo - 1, halo)) / ops.diagonal(halo)
        update = resid / centre
        iterate = crop(start, start_halo, halo) + update
    for sweep in range(2):
        applied = ops.operate(iterate, halo)
        halo = halo - 1
        resid = (crop(source, source_halo, halo) - applied) / ops.diagonal(halo)
        damping_next = 1.0 / (2.0 * ratio - damping)
        update = damping_next * damping * crop(update, halo + 1, halo) + 2.0 * damping_next / half_width * resid
        iterate = crop(iterate, halo + 1, halo) + update
        damping = damping_next
    return iterate, halo


def body(state, previous, feed, kill):
    deep = 3
    fields = jnp.concatenate([state, feed[None], kill[None]], 0)
    fields_1 = restrict(fields)
    fields_2 = restrict(fields_1)
    lane = lax.broadcasted_iota(jnp.int32, (8, 128), 1)
    local = jnp.zeros((8, 128), jnp.float32)
    for level, level_fields in enumerate((fields, fields_1, fields_2)):
        _, first, second = coefficients(level_fields, level)
        local = jnp.where(lane == level, jnp.maximum(jnp.max(first), jnp.max(second)), local)
    wide_x = padded_along(jnp.concatenate([fields, previous], 0), 6, "gx", 3)
    local, wide_x = lax.optimization_barrier((local, wide_x))
    spreads = global_max(local)[0]

    wide = padded_along(wide_x, 6, "gy", 2)
    ops_0 = Level(coefficients(crop(wide[:4], 6, 5), 0)[0], 5, 0)
    state_w = wide[:2]
    substrate, catalyst = crop(state_w[0], 6, 5), crop(state_w[1], 6, 5)
    centre = crop(state_w, 6, 5)
    reaction = substrate * catalyst * catalyst
    laplace = shrunk_neighbours(state_w) - 6.0 * centre
    feed_w = crop(wide[2], 6, 5)
    kill_w = crop(wide[3], 6, 5)
    previous_w = crop(wide[4:6], 6, 5)
    local_terms = jnp.stack(
        [reaction - feed_w * (1.0 - substrate), -reaction + (feed_w + kill_w) * catalyst]
    )
    nonlinear = inverse_step * (centre - previous_w) - diffusions(0) * laplace + local_terms
    source_0 = -nonlinear
    pre_0, pre_0_halo = chebyshev(ops_0, source_0, 5, None, None, spreads[0])
    resid_0 = crop(source_0, 5, 0) - ops_0.operate(crop(pre_0, pre_0_halo, 1), 1)

    wide_1 = padded(jnp.concatenate([restrict(resid_0), fields_1], 0), 7)
    ops_1 = Level(coefficients(wide_1[2:], 1)[0], 7, 1)
    source_1 = wide_1[:2]
    pre_1, pre_1_halo = chebyshev(ops_1, source_1, 7, None, None, spreads[1])
    resid_1 = crop(source_1, 7, 0) - ops_1.operate(crop(pre_1, pre_1_halo, 1), 1)

    wide_2 = padded(jnp.concatenate([restrict(resid_1), fields_2], 0), 8)
    ops_2 = Level(coefficients(wide_2[2:], 2)[0], 8, 2)
    source_2 = wide_2[:2]
    first_2, first_2_halo = chebyshev(ops_2, source_2, 8, None, None, spreads[2])
    coarse_2, coarse_2_halo = chebyshev(ops_2, source_2, 8, first_2, first_2_halo, spreads[2])

    start_1 = crop(pre_1, pre_1_halo, 5) + crop(prolong(coarse_2), 2 * coarse_2_halo, 5)
    post_1, post_1_halo = chebyshev(ops_1, source_1, 7, start_1, 5, spreads[1])

    start_0 = crop(pre_0, pre_0_halo, 3) + crop(prolong(post_1), 2 * post_1_halo, 3)
    post_0, post_0_halo = chebyshev(ops_0, source_0, 5, start_0, 3, spreads[0])
    return crop(post_0, post_0_halo, 0)


def solution(mesh):
    placed = (
        P(None, None, "gy", "gx"),
        P(None, None, "gy", "gx"),
        P(None, "gy", "gx"),
        P(None, "gy", "gx"),
    )
    return jax.shard_map(
        body, mesh=mesh, in_specs=placed, out_specs=P(None, None, "gy", "gx"), check_vma=False
    )
```

```python
import jax
import jax.numpy as jnp
from jax import lax
from jax.sharding import PartitionSpec as P
from jax.experimental import pallas as pl
from jax.experimental.pallas import tpu as pltpu

substrate_diffusion = 40.0
catalyst_diffusion = 20.0
inverse_step = 2.0
lower_fraction = 0.25
coarsenings = 2


def padded_along(cells, width, axis, dim):
    count = lax.axis_size(axis)
    size = cells.shape[dim]
    below, above = [], []
    remaining, distance = width, 1
    while remaining > 0:
        take = min(remaining, size)
        tail = lax.slice_in_dim(cells, size - take, size, axis=dim)
        head = lax.slice_in_dim(cells, 0, take, axis=dim)
        below.insert(0, lax.ppermute(tail, axis, [(i, (i + distance) % count) for i in range(count)]))
        above.append(lax.ppermute(head, axis, [((i + distance) % count, i) for i in range(count)]))
        remaining -= take
        distance += 1
    return jnp.concatenate(below + [cells] + above, axis=dim)


def halo_kernel(offsets, *refs):
    count = len(offsets)
    pieces, got, land = refs[:count], refs[count:2 * count], refs[2 * count:3 * count]
    send_sem, recv_sem = refs[3 * count], refs[3 * count + 1]
    count_x = lax.axis_size("gx")
    count_y = lax.axis_size("gy")
    at_x = lax.axis_index("gx")
    at_y = lax.axis_index("gy")
    mesh_ids = pl.DeviceIdType.MESH

    def device(step_y, step_x):
        return (lax.rem(at_x + step_x + 4 * count_x, count_x), lax.rem(at_y + step_y + 4 * count_y, count_y))

    barrier = pltpu.get_barrier_semaphore()
    for step_y, step_x in offsets:
        pl.semaphore_signal(barrier, 1, device_id=device(step_y, step_x), device_id_type=mesh_ids)
    pl.semaphore_wait(barrier, count)
    copies = []
    for slot, (step_y, step_x) in enumerate(offsets):
        copy = pltpu.make_async_remote_copy(
            src_ref=pieces[slot],
            dst_ref=land[slot],
            send_sem=send_sem.at[slot],
            recv_sem=recv_sem.at[slot],
            device_id=device(-step_y, -step_x),
            device_id_type=mesh_ids,
        )
        copy.start()
        copies.append(copy)
    for copy in copies:
        copy.wait()
    for slot in range(count):
        got[slot][...] = land[slot][...]


def segments(width, size):
    below, above = [], []
    remaining, distance = width, 1
    while remaining > 0:
        take = min(remaining, size)
        below.insert(0, (-distance, size - take, size))
        above.append((distance, 0, take))
        remaining -= take
        distance += 1
    return below + [(0, 0, size)] + above


def padded_at_once(cells, width, tag):
    rows, cols = cells.shape[2], cells.shape[3]
    runs_y, runs_x = segments(width, rows), segments(width, cols)
    pieces, offsets = [], []
    for step_y, first_y, last_y in runs_y:
        for step_x, first_x, last_x in runs_x:
            if (step_y, step_x) != (0, 0):
                pieces.append(cells[:, :, first_y:last_y, first_x:last_x])
                offsets.append((step_y, step_x))
    vmem = pl.BlockSpec(memory_space=pltpu.VMEM)
    shapes = [jax.ShapeDtypeStruct(piece.shape, jnp.float32) for piece in pieces]
    got = pl.pallas_call(
        lambda *refs: halo_kernel(offsets, *refs),
        out_shape=shapes,
        in_specs=[vmem] * len(pieces),
        out_specs=[vmem] * len(pieces),
        scratch_shapes=[pltpu.VMEM(shape.shape, jnp.float32) for shape in shapes]
        + [pltpu.SemaphoreType.DMA((len(pieces),)), pltpu.SemaphoreType.DMA((len(pieces),))],
        compiler_params=pltpu.CompilerParams(collective_id=tag, has_side_effects=True),
    )(*pieces)
    received = iter(got)
    bands = []
    for step_y, _, _ in runs_y:
        band = [cells if (step_y, step_x) == (0, 0) else next(received) for step_x, _, _ in runs_x]
        bands.append(jnp.concatenate(band, axis=3))
    return jnp.concatenate(bands, axis=2)


def padded(cells, width):
    return padded_along(padded_along(cells, width, "gx", 3), width, "gy", 2)


def crop(cells, have, want):
    cut = have - want
    assert cut >= 0
    if cut == 0:
        return cells
    return cells[..., cut:cells.shape[-2] - cut, cut:cells.shape[-1] - cut]


def shrunk_neighbours(cells):
    centre = cells[:, :, 1:-1, 1:-1]
    along_x = cells[:, :, 1:-1, :-2] + cells[:, :, 1:-1, 2:]
    along_y = cells[:, :, :-2, 1:-1] + cells[:, :, 2:, 1:-1]
    along_z = jnp.roll(centre, 1, 1) + jnp.roll(centre, -1, 1)
    return along_x + along_y + along_z


def gather_kernel(axis, value, out, land, send_sem, recv_sem, own_sem):
    count = lax.axis_size(axis)
    me = lax.axis_index(axis)
    other = lax.axis_index("gy" if axis == "gx" else "gx")
    mesh_ids = pl.DeviceIdType.MESH

    def device(index):
        return (index, other) if axis == "gx" else (other, index)

    barrier = pltpu.get_barrier_semaphore()
    for step in range(1, count):
        pl.semaphore_signal(barrier, 1, device_id=device(lax.rem(me + step, count)),
                            device_id_type=mesh_ids)
    pl.semaphore_wait(barrier, count - 1)
    copies = []
    for step in range(1, count):
        copy = pltpu.make_async_remote_copy(
            src_ref=value,
            dst_ref=land.at[me],
            send_sem=send_sem.at[step],
            recv_sem=recv_sem.at[me],
            device_id=device(lax.rem(me + step, count)),
            device_id_type=mesh_ids,
        )
        copy.start()
        copies.append(copy)
    own = pltpu.make_async_copy(value, land.at[me], own_sem)
    own.start()
    for step in range(1, count):
        copies[step - 1].wait_send()
        source = lax.rem(me + count - step, count)
        pltpu.make_async_remote_copy(
            src_ref=value,
            dst_ref=land.at[source],
            send_sem=send_sem.at[step],
            recv_sem=recv_sem.at[source],
            device_id=device(source),
            device_id_type=mesh_ids,
        ).wait_recv()
    own.wait()
    out[...] = land[...]


def gather_axis(block, axis, tag):
    count = lax.axis_size(axis)
    vmem = pl.BlockSpec(memory_space=pltpu.VMEM)
    shape = (count,) + block.shape
    return pl.pallas_call(
        lambda *refs: gather_kernel(axis, *refs),
        out_shape=jax.ShapeDtypeStruct(shape, jnp.float32),
        in_specs=[vmem],
        out_specs=vmem,
        scratch_shapes=[
            pltpu.VMEM(shape, jnp.float32),
            pltpu.SemaphoreType.DMA((count,)),
            pltpu.SemaphoreType.DMA((count,)),
            pltpu.SemaphoreType.DMA(()),
        ],
        compiler_params=pltpu.CompilerParams(collective_id=tag, has_side_effects=True),
    )(block)


def global_max(block):
    for tag, axis in enumerate(("gx", "gy")):
        block = jnp.max(gather_axis(block, axis, tag), axis=0)
    return block


def restrict(field):
    lead, depth, rows, cols = field.shape
    count = lead * depth * rows
    pick_x = (lax.broadcasted_iota(jnp.int32, (cols, cols // 2), 0) // 2
              == lax.broadcasted_iota(jnp.int32, (cols, cols // 2), 1)).astype(jnp.float32)
    row = lax.broadcasted_iota(jnp.int32, (count // 4, count), 1)
    target = ((row // (depth * rows)) * (depth // 2) + (row // rows) % depth // 2) * (rows // 2) + row % rows // 2
    pick_rows = (lax.broadcasted_iota(jnp.int32, (count // 4, count), 0) == target).astype(jnp.float32)
    pairs = jnp.dot(field.reshape(count, cols), pick_x, precision=lax.Precision.HIGHEST)
    blocks = jnp.dot(pick_rows, pairs, precision=lax.Precision.HIGHEST)
    return (blocks * 0.125).reshape(lead, depth // 2, rows // 2, cols // 2)


def prolong(field):
    return jnp.repeat(jnp.repeat(jnp.repeat(field, 2, 1), 2, 2), 2, 3)


def diffusions(level):
    scale = 0.25**level
    return jnp.array(
        [substrate_diffusion * scale, catalyst_diffusion * scale], jnp.float32
    ).reshape(2, 1, 1, 1)


def coefficients(fields, level):
    scale = 0.25**level
    diff_first = substrate_diffusion * scale
    diff_second = catalyst_diffusion * scale
    substrate, catalyst, feed_rate, kill_rate = (fields[0], fields[1], fields[2], fields[3])
    product = substrate * catalyst
    squared = catalyst * catalyst
    self_first = inverse_step + squared + feed_rate + 6.0 * diff_first
    cross_first = 2.0 * product
    cross_second = -squared
    self_second = inverse_step + feed_rate + kill_rate - 2.0 * product + 6.0 * diff_second
    coeff = jnp.stack([self_first, cross_first, cross_second, self_second])
    return coeff, (6.0 * diff_first + cross_first) / self_first, (6.0 * diff_second + squared) / self_second


class Level:
    def __init__(self, coeff, halo, level):
        self.coeff = coeff
        self.halo = halo
        self.level = level

    def at(self, halo):
        return crop(self.coeff, self.halo, halo)

    def operate(self, field, halo):
        coeff = self.at(halo - 1)
        centre = crop(field, halo, halo - 1)
        first = coeff[0] * centre[0] + coeff[1] * centre[1]
        second = coeff[2] * centre[0] + coeff[3] * centre[1]
        return jnp.stack([first, second]) - diffusions(self.level) * shrunk_neighbours(field)

    def diagonal(self, halo):
        coeff = self.at(halo)
        return jnp.stack([coeff[0], coeff[3]])


def chebyshev(ops, source, source_halo, start, start_halo, spread):
    upper = 1.0 + spread
    lower = lower_fraction * upper
    centre = (upper + lower) / 2.0
    half_width = (upper - lower) / 2.0
    ratio = centre / half_width
    damping = 1.0 / ratio
    if start is None:
        halo = source_halo
        resid = source / ops.diagonal(halo)
        update = resid / centre
        iterate = update
    else:
        halo = min(source_halo, start_halo - 1)
        applied = ops.operate(start, start_halo)
        resid = (crop(source, source_halo, halo) - crop(applied, start_halo - 1, halo)) / ops.diagonal(halo)
        update = resid / centre
        iterate = crop(start, start_halo, halo) + update
    for sweep in range(2):
        applied = ops.operate(iterate, halo)
        halo = halo - 1
        resid = (crop(source, source_halo, halo) - applied) / ops.diagonal(halo)
        damping_next = 1.0 / (2.0 * ratio - damping)
        update = damping_next * damping * crop(update, halo + 1, halo) + 2.0 * damping_next / half_width * resid
        iterate = crop(iterate, halo + 1, halo) + update
        damping = damping_next
    return iterate, halo


def body(state, previous, feed, kill):
    deep = 3
    fields = jnp.concatenate([state, feed[None], kill[None]], 0)
    fields_1 = restrict(fields)
    fields_2 = restrict(fields_1)
    lane = lax.broadcasted_iota(jnp.int32, (8, 128), 1)
    local = jnp.zeros((8, 128), jnp.float32)
    for level, level_fields in enumerate((fields, fields_1, fields_2)):
        _, first, second = coefficients(level_fields, level)
        local = jnp.where(lane == level, jnp.maximum(jnp.max(first), jnp.max(second)), local)
    wide_x = padded_along(jnp.concatenate([fields, previous], 0), 6, "gx", 3)
    local, wide_x = lax.optimization_barrier((local, wide_x))
    spreads = global_max(local)[0]

    wide = padded_along(wide_x, 6, "gy", 2)
    ops_0 = Level(coefficients(crop(wide[:4], 6, 5), 0)[0], 5, 0)
    state_w = wide[:2]
    substrate, catalyst = crop(state_w[0], 6, 5), crop(state_w[1], 6, 5)
    centre = crop(state_w, 6, 5)
    reaction = substrate * catalyst * catalyst
    laplace = shrunk_neighbours(state_w) - 6.0 * centre
    feed_w = crop(wide[2], 6, 5)
    kill_w = crop(wide[3], 6, 5)
    previous_w = crop(wide[4:6], 6, 5)
    local_terms = jnp.stack(
        [reaction - feed_w * (1.0 - substrate), -reaction + (feed_w + kill_w) * catalyst]
    )
    nonlinear = inverse_step * (centre - previous_w) - diffusions(0) * laplace + local_terms
    source_0 = -nonlinear
    pre_0, pre_0_halo = chebyshev(ops_0, source_0, 5, None, None, spreads[0])
    resid_0 = crop(source_0, 5, 0) - ops_0.operate(crop(pre_0, pre_0_halo, 1), 1)

    wide_1 = padded_at_once(jnp.concatenate([restrict(resid_0), fields_1], 0), 7, 2)
    ops_1 = Level(coefficients(wide_1[2:], 1)[0], 7, 1)
    source_1 = wide_1[:2]
    pre_1, pre_1_halo = chebyshev(ops_1, source_1, 7, None, None, spreads[1])
    resid_1 = crop(source_1, 7, 0) - ops_1.operate(crop(pre_1, pre_1_halo, 1), 1)

    wide_2 = padded_at_once(jnp.concatenate([restrict(resid_1), fields_2], 0), 8, 3)
    ops_2 = Level(coefficients(wide_2[2:], 2)[0], 8, 2)
    source_2 = wide_2[:2]
    first_2, first_2_halo = chebyshev(ops_2, source_2, 8, None, None, spreads[2])
    coarse_2, coarse_2_halo = chebyshev(ops_2, source_2, 8, first_2, first_2_halo, spreads[2])

    start_1 = crop(pre_1, pre_1_halo, 5) + crop(prolong(coarse_2), 2 * coarse_2_halo, 5)
    post_1, post_1_halo = chebyshev(ops_1, source_1, 7, start_1, 5, spreads[1])

    start_0 = crop(pre_0, pre_0_halo, 3) + crop(prolong(post_1), 2 * post_1_halo, 3)
    post_0, post_0_halo = chebyshev(ops_0, source_0, 5, start_0, 3, spreads[0])
    return crop(post_0, post_0_halo, 0)


def solution(mesh):
    placed = (
        P(None, None, "gy", "gx"),
        P(None, None, "gy", "gx"),
        P(None, "gy", "gx"),
        P(None, "gy", "gx"),
    )
    return jax.shard_map(
        body, mesh=mesh, in_specs=placed, out_specs=P(None, None, "gy", "gx"), check_vma=False
    )
```

```python
import numpy as np
import jax
import jax.numpy as jnp
from jax import lax
from jax.sharding import PartitionSpec as P
from jax.experimental import pallas as pl
from jax.experimental.pallas import tpu as pltpu

substrate_diffusion = 40.0
catalyst_diffusion = 20.0
inverse_step = 2.0
lower_fraction = 0.25
coarsenings = 2


def padded_along(cells, width, axis, dim):
    count = lax.axis_size(axis)
    size = cells.shape[dim]
    below, above = [], []
    remaining, distance = width, 1
    while remaining > 0:
        take = min(remaining, size)
        tail = lax.slice_in_dim(cells, size - take, size, axis=dim)
        head = lax.slice_in_dim(cells, 0, take, axis=dim)
        below.insert(0, lax.ppermute(tail, axis, [(i, (i + distance) % count) for i in range(count)]))
        above.append(lax.ppermute(head, axis, [((i + distance) % count, i) for i in range(count)]))
        remaining -= take
        distance += 1
    return jnp.concatenate(below + [cells] + above, axis=dim)


def padded(cells, width):
    return padded_along(padded_along(cells, width, "gx", 3), width, "gy", 2)


def crop(cells, have, want):
    cut = have - want
    assert cut >= 0
    if cut == 0:
        return cells
    return cells[..., cut:cells.shape[-2] - cut, cut:cells.shape[-1] - cut]


def shrunk_neighbours(cells):
    centre = cells[:, :, 1:-1, 1:-1]
    along_x = cells[:, :, 1:-1, :-2] + cells[:, :, 1:-1, 2:]
    along_y = cells[:, :, :-2, 1:-1] + cells[:, :, 2:, 1:-1]
    along_z = jnp.roll(centre, 1, 1) + jnp.roll(centre, -1, 1)
    return along_x + along_y + along_z


def gather_kernel(axis, value, out, land, send_sem, recv_sem, own_sem):
    count = lax.axis_size(axis)
    me = lax.axis_index(axis)
    other = lax.axis_index("gy" if axis == "gx" else "gx")
    mesh_ids = pl.DeviceIdType.MESH

    def device(index):
        return (index, other) if axis == "gx" else (other, index)

    barrier = pltpu.get_barrier_semaphore()
    for step in range(1, count):
        pl.semaphore_signal(barrier, 1, device_id=device(lax.rem(me + step, count)),
                            device_id_type=mesh_ids)
    pl.semaphore_wait(barrier, count - 1)
    copies = []
    for step in range(1, count):
        copy = pltpu.make_async_remote_copy(
            src_ref=value,
            dst_ref=land.at[me],
            send_sem=send_sem.at[step],
            recv_sem=recv_sem.at[me],
            device_id=device(lax.rem(me + step, count)),
            device_id_type=mesh_ids,
        )
        copy.start()
        copies.append(copy)
    own = pltpu.make_async_copy(value, land.at[me], own_sem)
    own.start()
    for step in range(1, count):
        copies[step - 1].wait_send()
        source = lax.rem(me + count - step, count)
        pltpu.make_async_remote_copy(
            src_ref=value,
            dst_ref=land.at[source],
            send_sem=send_sem.at[step],
            recv_sem=recv_sem.at[source],
            device_id=device(source),
            device_id_type=mesh_ids,
        ).wait_recv()
    own.wait()
    out[...] = land[...]


def gather_axis(block, axis, tag):
    count = lax.axis_size(axis)
    vmem = pl.BlockSpec(memory_space=pltpu.VMEM)
    shape = (count,) + block.shape
    return pl.pallas_call(
        lambda *refs: gather_kernel(axis, *refs),
        out_shape=jax.ShapeDtypeStruct(shape, jnp.float32),
        in_specs=[vmem],
        out_specs=vmem,
        scratch_shapes=[
            pltpu.VMEM(shape, jnp.float32),
            pltpu.SemaphoreType.DMA((count,)),
            pltpu.SemaphoreType.DMA((count,)),
            pltpu.SemaphoreType.DMA(()),
        ],
        compiler_params=pltpu.CompilerParams(collective_id=tag, has_side_effects=True),
    )(block)


def global_max(block):
    for tag, axis in enumerate(("gx", "gy")):
        block = jnp.max(gather_axis(block, axis, tag), axis=0)
    return block


def restrict(field):
    lead, depth, rows, cols = field.shape
    count = lead * depth * rows
    pick_x = (np.arange(cols)[:, None] // 2 == np.arange(cols // 2)[None, :]).astype(np.float32)
    row = np.arange(count)
    target = ((row // (depth * rows)) * (depth // 2) + (row // rows) % depth // 2) * (rows // 2) + row % rows // 2
    pick_rows = (np.arange(count // 4)[:, None] == target[None, :]).astype(np.float32)
    pairs = jnp.dot(field.reshape(count, cols), pick_x, precision=lax.Precision.HIGHEST)
    blocks = jnp.dot(pick_rows, pairs, precision=lax.Precision.HIGHEST)
    return (blocks * 0.125).reshape(lead, depth // 2, rows // 2, cols // 2)


def prolong(field):
    return jnp.repeat(jnp.repeat(jnp.repeat(field, 2, 1), 2, 2), 2, 3)


def diffusions(level):
    scale = 0.25**level
    return jnp.array(
        [substrate_diffusion * scale, catalyst_diffusion * scale], jnp.float32
    ).reshape(2, 1, 1, 1)


def coefficients(fields, level):
    scale = 0.25**level
    diff_first = substrate_diffusion * scale
    diff_second = catalyst_diffusion * scale
    substrate, catalyst, feed_rate, kill_rate = (fields[0], fields[1], fields[2], fields[3])
    product = substrate * catalyst
    squared = catalyst * catalyst
    self_first = inverse_step + squared + feed_rate + 6.0 * diff_first
    cross_first = 2.0 * product
    cross_second = -squared
    self_second = inverse_step + feed_rate + kill_rate - 2.0 * product + 6.0 * diff_second
    coeff = jnp.stack([self_first, cross_first, cross_second, self_second])
    return coeff, (6.0 * diff_first + cross_first) / self_first, (6.0 * diff_second + squared) / self_second


class Level:
    def __init__(self, coeff, halo, level):
        self.coeff = coeff
        self.halo = halo
        self.level = level

    def at(self, halo):
        return crop(self.coeff, self.halo, halo)

    def operate(self, field, halo):
        coeff = self.at(halo - 1)
        centre = crop(field, halo, halo - 1)
        first = coeff[0] * centre[0] + coeff[1] * centre[1]
        second = coeff[2] * centre[0] + coeff[3] * centre[1]
        return jnp.stack([first, second]) - diffusions(self.level) * shrunk_neighbours(field)

    def diagonal(self, halo):
        coeff = self.at(halo)
        return jnp.stack([coeff[0], coeff[3]])


def chebyshev(ops, source, source_halo, start, start_halo, spread):
    upper = 1.0 + spread
    lower = lower_fraction * upper
    centre = (upper + lower) / 2.0
    half_width = (upper - lower) / 2.0
    ratio = centre / half_width
    damping = 1.0 / ratio
    if start is None:
        halo = source_halo
        resid = source / ops.diagonal(halo)
        update = resid / centre
        iterate = update
    else:
        halo = min(source_halo, start_halo - 1)
        applied = ops.operate(start, start_halo)
        resid = (crop(source, source_halo, halo) - crop(applied, start_halo - 1, halo)) / ops.diagonal(halo)
        update = resid / centre
        iterate = crop(start, start_halo, halo) + update
    for sweep in range(2):
        applied = ops.operate(iterate, halo)
        halo = halo - 1
        resid = (crop(source, source_halo, halo) - applied) / ops.diagonal(halo)
        damping_next = 1.0 / (2.0 * ratio - damping)
        update = damping_next * damping * crop(update, halo + 1, halo) + 2.0 * damping_next / half_width * resid
        iterate = crop(iterate, halo + 1, halo) + update
        damping = damping_next
    return iterate, halo


def body(state, previous, feed, kill):
    deep = 3
    fields = jnp.concatenate([state, feed[None], kill[None]], 0)
    fields_1 = restrict(fields)
    fields_2 = restrict(fields_1)
    lane = lax.broadcasted_iota(jnp.int32, (8, 128), 1)
    local = jnp.zeros((8, 128), jnp.float32)
    for level, level_fields in enumerate((fields, fields_1, fields_2)):
        _, first, second = coefficients(level_fields, level)
        local = jnp.where(lane == level, jnp.maximum(jnp.max(first), jnp.max(second)), local)
    wide_x = padded_along(jnp.concatenate([fields, previous], 0), 6, "gx", 3)
    local, wide_x = lax.optimization_barrier((local, wide_x))
    spreads = global_max(local)[0]

    wide = padded_along(wide_x, 6, "gy", 2)
    ops_0 = Level(coefficients(crop(wide[:4], 6, 5), 0)[0], 5, 0)
    state_w = wide[:2]
    substrate, catalyst = crop(state_w[0], 6, 5), crop(state_w[1], 6, 5)
    centre = crop(state_w, 6, 5)
    reaction = substrate * catalyst * catalyst
    laplace = shrunk_neighbours(state_w) - 6.0 * centre
    feed_w = crop(wide[2], 6, 5)
    kill_w = crop(wide[3], 6, 5)
    previous_w = crop(wide[4:6], 6, 5)
    local_terms = jnp.stack(
        [reaction - feed_w * (1.0 - substrate), -reaction + (feed_w + kill_w) * catalyst]
    )
    nonlinear = inverse_step * (centre - previous_w) - diffusions(0) * laplace + local_terms
    source_0 = -nonlinear
    pre_0, pre_0_halo = chebyshev(ops_0, source_0, 5, None, None, spreads[0])
    resid_0 = crop(source_0, 5, 0) - ops_0.operate(crop(pre_0, pre_0_halo, 1), 1)

    wide_1 = padded(jnp.concatenate([restrict(resid_0), fields_1], 0), 7)
    ops_1 = Level(coefficients(wide_1[2:], 1)[0], 7, 1)
    source_1 = wide_1[:2]
    pre_1, pre_1_halo = chebyshev(ops_1, source_1, 7, None, None, spreads[1])
    resid_1 = crop(source_1, 7, 0) - ops_1.operate(crop(pre_1, pre_1_halo, 1), 1)

    wide_2 = padded(jnp.concatenate([restrict(resid_1), fields_2], 0), 8)
    ops_2 = Level(coefficients(wide_2[2:], 2)[0], 8, 2)
    source_2 = wide_2[:2]
    first_2, first_2_halo = chebyshev(ops_2, source_2, 8, None, None, spreads[2])
    coarse_2, coarse_2_halo = chebyshev(ops_2, source_2, 8, first_2, first_2_halo, spreads[2])

    start_1 = crop(pre_1, pre_1_halo, 5) + crop(prolong(coarse_2), 2 * coarse_2_halo, 5)
    post_1, post_1_halo = chebyshev(ops_1, source_1, 7, start_1, 5, spreads[1])

    start_0 = crop(pre_0, pre_0_halo, 3) + crop(prolong(post_1), 2 * post_1_halo, 3)
    post_0, post_0_halo = chebyshev(ops_0, source_0, 5, start_0, 3, spreads[0])
    return crop(post_0, post_0_halo, 0)


def solution(mesh):
    placed = (
        P(None, None, "gy", "gx"),
        P(None, None, "gy", "gx"),
        P(None, "gy", "gx"),
        P(None, "gy", "gx"),
    )
    return jax.shard_map(
        body, mesh=mesh, in_specs=placed, out_specs=P(None, None, "gy", "gx"), check_vma=False
    )
```

```python
import numpy as np
import jax
import jax.numpy as jnp
from jax import lax
from jax.sharding import PartitionSpec as P
from jax.experimental import pallas as pl
from jax.experimental.pallas import tpu as pltpu

substrate_diffusion = 40.0
catalyst_diffusion = 20.0
inverse_step = 2.0
lower_fraction = 0.25
coarsenings = 2


def padded_along(cells, width, axis, dim):
    count = lax.axis_size(axis)
    size = cells.shape[dim]
    below, above = [], []
    remaining, distance = width, 1
    while remaining > 0:
        take = min(remaining, size)
        tail = lax.slice_in_dim(cells, size - take, size, axis=dim)
        head = lax.slice_in_dim(cells, 0, take, axis=dim)
        below.insert(0, lax.ppermute(tail, axis, [(i, (i + distance) % count) for i in range(count)]))
        above.append(lax.ppermute(head, axis, [((i + distance) % count, i) for i in range(count)]))
        remaining -= take
        distance += 1
    return jnp.concatenate(below + [cells] + above, axis=dim)


def segments(width, size):
    below, above = [], []
    remaining, distance = width, 1
    while remaining > 0:
        take = min(remaining, size)
        below.insert(0, (-distance, size - take, size))
        above.append((distance, 0, take))
        remaining -= take
        distance += 1
    return below + [(0, 0, size)] + above


def padded_at_once(cells, width):
    rows, cols = cells.shape[2], cells.shape[3]
    count_x = lax.axis_size("gx")
    count_y = lax.axis_size("gy")
    runs_y, runs_x = segments(width, rows), segments(width, cols)
    bands = []
    for step_y, first_y, last_y in runs_y:
        band = []
        for step_x, first_x, last_x in runs_x:
            if (step_y, step_x) == (0, 0):
                band.append(cells)
                continue
            piece = cells[:, :, first_y:last_y, first_x:last_x]
            if step_y == 0:
                pairs = [(i, (i - step_x) % count_x) for i in range(count_x)]
                band.append(lax.ppermute(piece, "gx", pairs))
            elif step_x == 0:
                pairs = [(i, (i - step_y) % count_y) for i in range(count_y)]
                band.append(lax.ppermute(piece, "gy", pairs))
            else:
                pairs = [(i * count_y + j, ((i - step_x) % count_x) * count_y + (j - step_y) % count_y)
                         for i in range(count_x) for j in range(count_y)]
                band.append(lax.ppermute(piece, ("gx", "gy"), pairs))
        bands.append(jnp.concatenate(band, axis=3))
    return jnp.concatenate(bands, axis=2)


def padded(cells, width):
    return padded_along(padded_along(cells, width, "gx", 3), width, "gy", 2)


def crop(cells, have, want):
    cut = have - want
    assert cut >= 0
    if cut == 0:
        return cells
    return cells[..., cut:cells.shape[-2] - cut, cut:cells.shape[-1] - cut]


def shrunk_neighbours(cells):
    centre = cells[:, :, 1:-1, 1:-1]
    along_x = cells[:, :, 1:-1, :-2] + cells[:, :, 1:-1, 2:]
    along_y = cells[:, :, :-2, 1:-1] + cells[:, :, 2:, 1:-1]
    along_z = jnp.roll(centre, 1, 1) + jnp.roll(centre, -1, 1)
    return along_x + along_y + along_z


def gather_kernel(axis, value, out, land, send_sem, recv_sem, own_sem):
    count = lax.axis_size(axis)
    me = lax.axis_index(axis)
    other = lax.axis_index("gy" if axis == "gx" else "gx")
    mesh_ids = pl.DeviceIdType.MESH

    def device(index):
        return (index, other) if axis == "gx" else (other, index)

    barrier = pltpu.get_barrier_semaphore()
    for step in range(1, count):
        pl.semaphore_signal(barrier, 1, device_id=device(lax.rem(me + step, count)),
                            device_id_type=mesh_ids)
    pl.semaphore_wait(barrier, count - 1)
    copies = []
    for step in range(1, count):
        copy = pltpu.make_async_remote_copy(
            src_ref=value,
            dst_ref=land.at[me],
            send_sem=send_sem.at[step],
            recv_sem=recv_sem.at[me],
            device_id=device(lax.rem(me + step, count)),
            device_id_type=mesh_ids,
        )
        copy.start()
        copies.append(copy)
    own = pltpu.make_async_copy(value, land.at[me], own_sem)
    own.start()
    for step in range(1, count):
        copies[step - 1].wait_send()
        source = lax.rem(me + count - step, count)
        pltpu.make_async_remote_copy(
            src_ref=value,
            dst_ref=land.at[source],
            send_sem=send_sem.at[step],
            recv_sem=recv_sem.at[source],
            device_id=device(source),
            device_id_type=mesh_ids,
        ).wait_recv()
    own.wait()
    out[...] = land[...]


def gather_axis(block, axis, tag):
    count = lax.axis_size(axis)
    vmem = pl.BlockSpec(memory_space=pltpu.VMEM)
    shape = (count,) + block.shape
    return pl.pallas_call(
        lambda *refs: gather_kernel(axis, *refs),
        out_shape=jax.ShapeDtypeStruct(shape, jnp.float32),
        in_specs=[vmem],
        out_specs=vmem,
        scratch_shapes=[
            pltpu.VMEM(shape, jnp.float32),
            pltpu.SemaphoreType.DMA((count,)),
            pltpu.SemaphoreType.DMA((count,)),
            pltpu.SemaphoreType.DMA(()),
        ],
        compiler_params=pltpu.CompilerParams(collective_id=tag, has_side_effects=True),
    )(block)


def global_max(block):
    for tag, axis in enumerate(("gx", "gy")):
        block = jnp.max(gather_axis(block, axis, tag), axis=0)
    return block


def restrict(field):
    lead, depth, rows, cols = field.shape
    count = lead * depth * rows
    pick_x = (np.arange(cols)[:, None] // 2 == np.arange(cols // 2)[None, :]).astype(np.float32)
    row = np.arange(count)
    target = ((row // (depth * rows)) * (depth // 2) + (row // rows) % depth // 2) * (rows // 2) + row % rows // 2
    pick_rows = (np.arange(count // 4)[:, None] == target[None, :]).astype(np.float32)
    pairs = jnp.dot(field.reshape(count, cols), pick_x, precision=lax.Precision.HIGHEST)
    blocks = jnp.dot(pick_rows, pairs, precision=lax.Precision.HIGHEST)
    return (blocks * 0.125).reshape(lead, depth // 2, rows // 2, cols // 2)


def prolong(field):
    return jnp.repeat(jnp.repeat(jnp.repeat(field, 2, 1), 2, 2), 2, 3)


def diffusions(level):
    scale = 0.25**level
    return jnp.array(
        [substrate_diffusion * scale, catalyst_diffusion * scale], jnp.float32
    ).reshape(2, 1, 1, 1)


def coefficients(fields, level):
    scale = 0.25**level
    diff_first = substrate_diffusion * scale
    diff_second = catalyst_diffusion * scale
    substrate, catalyst, feed_rate, kill_rate = (fields[0], fields[1], fields[2], fields[3])
    product = substrate * catalyst
    squared = catalyst * catalyst
    self_first = inverse_step + squared + feed_rate + 6.0 * diff_first
    cross_first = 2.0 * product
    cross_second = -squared
    self_second = inverse_step + feed_rate + kill_rate - 2.0 * product + 6.0 * diff_second
    coeff = jnp.stack([self_first, cross_first, cross_second, self_second])
    return coeff, (6.0 * diff_first + cross_first) / self_first, (6.0 * diff_second + squared) / self_second


class Level:
    def __init__(self, coeff, halo, level):
        self.coeff = coeff
        self.halo = halo
        self.level = level

    def at(self, halo):
        return crop(self.coeff, self.halo, halo)

    def operate(self, field, halo):
        coeff = self.at(halo - 1)
        centre = crop(field, halo, halo - 1)
        first = coeff[0] * centre[0] + coeff[1] * centre[1]
        second = coeff[2] * centre[0] + coeff[3] * centre[1]
        return jnp.stack([first, second]) - diffusions(self.level) * shrunk_neighbours(field)

    def diagonal(self, halo):
        coeff = self.at(halo)
        return jnp.stack([coeff[0], coeff[3]])


def chebyshev(ops, source, source_halo, start, start_halo, spread):
    upper = 1.0 + spread
    lower = lower_fraction * upper
    centre = (upper + lower) / 2.0
    half_width = (upper - lower) / 2.0
    ratio = centre / half_width
    damping = 1.0 / ratio
    if start is None:
        halo = source_halo
        resid = source / ops.diagonal(halo)
        update = resid / centre
        iterate = update
    else:
        halo = min(source_halo, start_halo - 1)
        applied = ops.operate(start, start_halo)
        resid = (crop(source, source_halo, halo) - crop(applied, start_halo - 1, halo)) / ops.diagonal(halo)
        update = resid / centre
        iterate = crop(start, start_halo, halo) + update
    for sweep in range(2):
        applied = ops.operate(iterate, halo)
        halo = halo - 1
        resid = (crop(source, source_halo, halo) - applied) / ops.diagonal(halo)
        damping_next = 1.0 / (2.0 * ratio - damping)
        update = damping_next * damping * crop(update, halo + 1, halo) + 2.0 * damping_next / half_width * resid
        iterate = crop(iterate, halo + 1, halo) + update
        damping = damping_next
    return iterate, halo


def body(state, previous, feed, kill):
    deep = 3
    fields = jnp.concatenate([state, feed[None], kill[None]], 0)
    fields_1 = restrict(fields)
    fields_2 = restrict(fields_1)
    lane = lax.broadcasted_iota(jnp.int32, (8, 128), 1)
    local = jnp.zeros((8, 128), jnp.float32)
    for level, level_fields in enumerate((fields, fields_1, fields_2)):
        _, first, second = coefficients(level_fields, level)
        local = jnp.where(lane == level, jnp.maximum(jnp.max(first), jnp.max(second)), local)
    wide = padded_at_once(jnp.concatenate([fields, previous], 0), 6)
    spreads = global_max(local)[0]

    ops_0 = Level(coefficients(crop(wide[:4], 6, 5), 0)[0], 5, 0)
    state_w = wide[:2]
    substrate, catalyst = crop(state_w[0], 6, 5), crop(state_w[1], 6, 5)
    centre = crop(state_w, 6, 5)
    reaction = substrate * catalyst * catalyst
    laplace = shrunk_neighbours(state_w) - 6.0 * centre
    feed_w = crop(wide[2], 6, 5)
    kill_w = crop(wide[3], 6, 5)
    previous_w = crop(wide[4:6], 6, 5)
    local_terms = jnp.stack(
        [reaction - feed_w * (1.0 - substrate), -reaction + (feed_w + kill_w) * catalyst]
    )
    nonlinear = inverse_step * (centre - previous_w) - diffusions(0) * laplace + local_terms
    source_0 = -nonlinear
    pre_0, pre_0_halo = chebyshev(ops_0, source_0, 5, None, None, spreads[0])
    resid_0 = crop(source_0, 5, 0) - ops_0.operate(crop(pre_0, pre_0_halo, 1), 1)

    wide_1 = padded_at_once(jnp.concatenate([restrict(resid_0), fields_1], 0), 7)
    ops_1 = Level(coefficients(wide_1[2:], 1)[0], 7, 1)
    source_1 = wide_1[:2]
    pre_1, pre_1_halo = chebyshev(ops_1, source_1, 7, None, None, spreads[1])
    resid_1 = crop(source_1, 7, 0) - ops_1.operate(crop(pre_1, pre_1_halo, 1), 1)

    wide_2 = padded(jnp.concatenate([restrict(resid_1), fields_2], 0), 8)
    ops_2 = Level(coefficients(wide_2[2:], 2)[0], 8, 2)
    source_2 = wide_2[:2]
    first_2, first_2_halo = chebyshev(ops_2, source_2, 8, None, None, spreads[2])
    coarse_2, coarse_2_halo = chebyshev(ops_2, source_2, 8, first_2, first_2_halo, spreads[2])

    start_1 = crop(pre_1, pre_1_halo, 5) + crop(prolong(coarse_2), 2 * coarse_2_halo, 5)
    post_1, post_1_halo = chebyshev(ops_1, source_1, 7, start_1, 5, spreads[1])

    start_0 = crop(pre_0, pre_0_halo, 3) + crop(prolong(post_1), 2 * post_1_halo, 3)
    post_0, post_0_halo = chebyshev(ops_0, source_0, 5, start_0, 3, spreads[0])
    return crop(post_0, post_0_halo, 0)


def solution(mesh):
    placed = (
        P(None, None, "gy", "gx"),
        P(None, None, "gy", "gx"),
        P(None, "gy", "gx"),
        P(None, "gy", "gx"),
    )
    return jax.shard_map(
        body, mesh=mesh, in_specs=placed, out_specs=P(None, None, "gy", "gx"), check_vma=False
    )
```

```python
import numpy as np
import jax
import jax.numpy as jnp
from jax import lax
from jax.sharding import PartitionSpec as P
from jax.experimental import pallas as pl
from jax.experimental.pallas import tpu as pltpu

substrate_diffusion = 40.0
catalyst_diffusion = 20.0
inverse_step = 2.0
lower_fraction = 0.25
coarsenings = 2


def padded_along(cells, width, axis, dim):
    count = lax.axis_size(axis)
    size = cells.shape[dim]
    below, above = [], []
    remaining, distance = width, 1
    while remaining > 0:
        take = min(remaining, size)
        tail = lax.slice_in_dim(cells, size - take, size, axis=dim)
        head = lax.slice_in_dim(cells, 0, take, axis=dim)
        below.insert(0, lax.ppermute(tail, axis, [(i, (i + distance) % count) for i in range(count)]))
        above.append(lax.ppermute(head, axis, [((i + distance) % count, i) for i in range(count)]))
        remaining -= take
        distance += 1
    return jnp.concatenate(below + [cells] + above, axis=dim)


def padded(cells, width):
    return padded_along(padded_along(cells, width, "gx", 3), width, "gy", 2)


def crop(cells, have, want):
    cut = have - want
    assert cut >= 0
    if cut == 0:
        return cells
    return cells[..., cut:cells.shape[-2] - cut, cut:cells.shape[-1] - cut]


def shrunk_neighbours(cells):
    centre = cells[:, :, 1:-1, 1:-1]
    along_x = cells[:, :, 1:-1, :-2] + cells[:, :, 1:-1, 2:]
    along_y = cells[:, :, :-2, 1:-1] + cells[:, :, 2:, 1:-1]
    along_z = jnp.roll(centre, 1, 1) + jnp.roll(centre, -1, 1)
    return along_x + along_y + along_z


def spread_kernel(value, out, land_x, land_y, send_x, recv_x, send_y, recv_y, own_x, own_y):
    count_x = lax.axis_size("gx")
    count_y = lax.axis_size("gy")
    at_x = lax.axis_index("gx")
    at_y = lax.axis_index("gy")
    mesh_ids = pl.DeviceIdType.MESH
    barrier = pltpu.get_barrier_semaphore()
    for step in range(1, count_x):
        pl.semaphore_signal(barrier, 1, device_id=(lax.rem(at_x + step, count_x), at_y),
                            device_id_type=mesh_ids)
    for step in range(1, count_y):
        pl.semaphore_signal(barrier, 1, device_id=(at_x, lax.rem(at_y + step, count_y)),
                            device_id_type=mesh_ids)
    pl.semaphore_wait(barrier, count_x + count_y - 2)

    copies = []
    for step in range(1, count_x):
        copy = pltpu.make_async_remote_copy(
            src_ref=value,
            dst_ref=land_x.at[at_x],
            send_sem=send_x.at[step],
            recv_sem=recv_x.at[at_x],
            device_id=(lax.rem(at_x + step, count_x), at_y),
            device_id_type=mesh_ids,
        )
        copy.start()
        copies.append(copy)
    own = pltpu.make_async_copy(value, land_x.at[at_x], own_x)
    own.start()
    for step in range(1, count_x):
        copies[step - 1].wait_send()
        source = lax.rem(at_x + count_x - step, count_x)
        pltpu.make_async_remote_copy(
            src_ref=value,
            dst_ref=land_x.at[source],
            send_sem=send_x.at[step],
            recv_sem=recv_x.at[source],
            device_id=(source, at_y),
            device_id_type=mesh_ids,
        ).wait_recv()
    own.wait()

    rows = land_x.at[:, pl.ds(0, 1), :]
    copies = []
    for step in range(1, count_y):
        copy = pltpu.make_async_remote_copy(
            src_ref=rows,
            dst_ref=land_y.at[at_y],
            send_sem=send_y.at[step],
            recv_sem=recv_y.at[at_y],
            device_id=(at_x, lax.rem(at_y + step, count_y)),
            device_id_type=mesh_ids,
        )
        copy.start()
        copies.append(copy)
    own = pltpu.make_async_copy(rows, land_y.at[at_y], own_y)
    own.start()
    for step in range(1, count_y):
        copies[step - 1].wait_send()
        source = lax.rem(at_y + count_y - step, count_y)
        pltpu.make_async_remote_copy(
            src_ref=rows,
            dst_ref=land_y.at[source],
            send_sem=send_y.at[step],
            recv_sem=recv_y.at[source],
            device_id=(at_x, source),
            device_id_type=mesh_ids,
        ).wait_recv()
    own.wait()
    best = jnp.max(land_y[...], axis=(0, 1))
    out[...] = jnp.broadcast_to(best, out.shape)


def global_max(block):
    count_x = lax.axis_size("gx")
    count_y = lax.axis_size("gy")
    vmem = pl.BlockSpec(memory_space=pltpu.VMEM)
    return pl.pallas_call(
        spread_kernel,
        out_shape=jax.ShapeDtypeStruct(block.shape, jnp.float32),
        in_specs=[vmem],
        out_specs=vmem,
        scratch_shapes=[
            pltpu.VMEM((count_x,) + block.shape, jnp.float32),
            pltpu.VMEM((count_y, count_x, 1, block.shape[1]), jnp.float32),
            pltpu.SemaphoreType.DMA((count_x,)),
            pltpu.SemaphoreType.DMA((count_x,)),
            pltpu.SemaphoreType.DMA((count_y,)),
            pltpu.SemaphoreType.DMA((count_y,)),
            pltpu.SemaphoreType.DMA(()),
            pltpu.SemaphoreType.DMA(()),
        ],
        compiler_params=pltpu.CompilerParams(collective_id=0, has_side_effects=True),
    )(block)


def restrict(field):
    lead, depth, rows, cols = field.shape
    count = lead * depth * rows
    pick_x = (np.arange(cols)[:, None] // 2 == np.arange(cols // 2)[None, :]).astype(np.float32)
    row = np.arange(count)
    target = ((row // (depth * rows)) * (depth // 2) + (row // rows) % depth // 2) * (rows // 2) + row % rows // 2
    pick_rows = (np.arange(count // 4)[:, None] == target[None, :]).astype(np.float32)
    pairs = jnp.dot(field.reshape(count, cols), pick_x, precision=lax.Precision.HIGHEST)
    blocks = jnp.dot(pick_rows, pairs, precision=lax.Precision.HIGHEST)
    return (blocks * 0.125).reshape(lead, depth // 2, rows // 2, cols // 2)


def prolong(field):
    return jnp.repeat(jnp.repeat(jnp.repeat(field, 2, 1), 2, 2), 2, 3)


def diffusions(level):
    scale = 0.25**level
    return jnp.array(
        [substrate_diffusion * scale, catalyst_diffusion * scale], jnp.float32
    ).reshape(2, 1, 1, 1)


def coefficients(fields, level):
    scale = 0.25**level
    diff_first = substrate_diffusion * scale
    diff_second = catalyst_diffusion * scale
    substrate, catalyst, feed_rate, kill_rate = (fields[0], fields[1], fields[2], fields[3])
    product = substrate * catalyst
    squared = catalyst * catalyst
    self_first = inverse_step + squared + feed_rate + 6.0 * diff_first
    cross_first = 2.0 * product
    cross_second = -squared
    self_second = inverse_step + feed_rate + kill_rate - 2.0 * product + 6.0 * diff_second
    coeff = jnp.stack([self_first, cross_first, cross_second, self_second])
    return coeff, (6.0 * diff_first + cross_first) / self_first, (6.0 * diff_second + squared) / self_second


class Level:
    def __init__(self, coeff, halo, level):
        self.coeff = coeff
        self.halo = halo
        self.level = level

    def at(self, halo):
        return crop(self.coeff, self.halo, halo)

    def operate(self, field, halo):
        coeff = self.at(halo - 1)
        centre = crop(field, halo, halo - 1)
        first = coeff[0] * centre[0] + coeff[1] * centre[1]
        second = coeff[2] * centre[0] + coeff[3] * centre[1]
        return jnp.stack([first, second]) - diffusions(self.level) * shrunk_neighbours(field)

    def diagonal(self, halo):
        coeff = self.at(halo)
        return jnp.stack([coeff[0], coeff[3]])


def chebyshev(ops, source, source_halo, start, start_halo, spread):
    upper = 1.0 + spread
    lower = lower_fraction * upper
    centre = (upper + lower) / 2.0
    half_width = (upper - lower) / 2.0
    ratio = centre / half_width
    damping = 1.0 / ratio
    if start is None:
        halo = source_halo
        resid = source / ops.diagonal(halo)
        update = resid / centre
        iterate = update
    else:
        halo = min(source_halo, start_halo - 1)
        applied = ops.operate(start, start_halo)
        resid = (crop(source, source_halo, halo) - crop(applied, start_halo - 1, halo)) / ops.diagonal(halo)
        update = resid / centre
        iterate = crop(start, start_halo, halo) + update
    for sweep in range(2):
        applied = ops.operate(iterate, halo)
        halo = halo - 1
        resid = (crop(source, source_halo, halo) - applied) / ops.diagonal(halo)
        damping_next = 1.0 / (2.0 * ratio - damping)
        update = damping_next * damping * crop(update, halo + 1, halo) + 2.0 * damping_next / half_width * resid
        iterate = crop(iterate, halo + 1, halo) + update
        damping = damping_next
    return iterate, halo


def body(state, previous, feed, kill):
    deep = 3
    fields = jnp.concatenate([state, feed[None], kill[None]], 0)
    fields_1 = restrict(fields)
    fields_2 = restrict(fields_1)
    lane = lax.broadcasted_iota(jnp.int32, (8, 128), 1)
    local = jnp.zeros((8, 128), jnp.float32)
    for level, level_fields in enumerate((fields, fields_1, fields_2)):
        _, first, second = coefficients(level_fields, level)
        local = jnp.where(lane == level, jnp.maximum(jnp.max(first), jnp.max(second)), local)
    wide_x = padded_along(jnp.concatenate([fields, previous], 0), 6, "gx", 3)
    local, wide_x = lax.optimization_barrier((local, wide_x))
    spreads = global_max(local)[0]

    wide = padded_along(wide_x, 6, "gy", 2)
    ops_0 = Level(coefficients(crop(wide[:4], 6, 5), 0)[0], 5, 0)
    state_w = wide[:2]
    substrate, catalyst = crop(state_w[0], 6, 5), crop(state_w[1], 6, 5)
    centre = crop(state_w, 6, 5)
    reaction = substrate * catalyst * catalyst
    laplace = shrunk_neighbours(state_w) - 6.0 * centre
    feed_w = crop(wide[2], 6, 5)
    kill_w = crop(wide[3], 6, 5)
    previous_w = crop(wide[4:6], 6, 5)
    local_terms = jnp.stack(
        [reaction - feed_w * (1.0 - substrate), -reaction + (feed_w + kill_w) * catalyst]
    )
    nonlinear = inverse_step * (centre - previous_w) - diffusions(0) * laplace + local_terms
    source_0 = -nonlinear
    pre_0, pre_0_halo = chebyshev(ops_0, source_0, 5, None, None, spreads[0])
    resid_0 = crop(source_0, 5, 0) - ops_0.operate(crop(pre_0, pre_0_halo, 1), 1)

    wide_1 = padded(jnp.concatenate([restrict(resid_0), fields_1], 0), 7)
    ops_1 = Level(coefficients(wide_1[2:], 1)[0], 7, 1)
    source_1 = wide_1[:2]
    pre_1, pre_1_halo = chebyshev(ops_1, source_1, 7, None, None, spreads[1])
    resid_1 = crop(source_1, 7, 0) - ops_1.operate(crop(pre_1, pre_1_halo, 1), 1)

    wide_2 = padded(jnp.concatenate([restrict(resid_1), fields_2], 0), 8)
    ops_2 = Level(coefficients(wide_2[2:], 2)[0], 8, 2)
    source_2 = wide_2[:2]
    first_2, first_2_halo = chebyshev(ops_2, source_2, 8, None, None, spreads[2])
    coarse_2, coarse_2_halo = chebyshev(ops_2, source_2, 8, first_2, first_2_halo, spreads[2])

    start_1 = crop(pre_1, pre_1_halo, 5) + crop(prolong(coarse_2), 2 * coarse_2_halo, 5)
    post_1, post_1_halo = chebyshev(ops_1, source_1, 7, start_1, 5, spreads[1])

    start_0 = crop(pre_0, pre_0_halo, 3) + crop(prolong(post_1), 2 * post_1_halo, 3)
    post_0, post_0_halo = chebyshev(ops_0, source_0, 5, start_0, 3, spreads[0])
    return crop(post_0, post_0_halo, 0)


def solution(mesh):
    placed = (
        P(None, None, "gy", "gx"),
        P(None, None, "gy", "gx"),
        P(None, "gy", "gx"),
        P(None, "gy", "gx"),
    )
    return jax.shard_map(
        body, mesh=mesh, in_specs=placed, out_specs=P(None, None, "gy", "gx"), check_vma=False
    )
```

```python
import numpy as np
import jax
import jax.numpy as jnp
from jax import lax
from jax.sharding import PartitionSpec as P
from jax.experimental import pallas as pl
from jax.experimental.pallas import tpu as pltpu

substrate_diffusion = 40.0
catalyst_diffusion = 20.0
inverse_step = 2.0
lower_fraction = 0.25
coarsenings = 2


def padded_along(cells, width, axis, dim):
    count = lax.axis_size(axis)
    size = cells.shape[dim]
    below, above = [], []
    remaining, distance = width, 1
    while remaining > 0:
        take = min(remaining, size)
        tail = lax.slice_in_dim(cells, size - take, size, axis=dim)
        head = lax.slice_in_dim(cells, 0, take, axis=dim)
        below.insert(0, lax.ppermute(tail, axis, [(i, (i + distance) % count) for i in range(count)]))
        above.append(lax.ppermute(head, axis, [((i + distance) % count, i) for i in range(count)]))
        remaining -= take
        distance += 1
    return jnp.concatenate(below + [cells] + above, axis=dim)


def padded(cells, width):
    return padded_along(padded_along(cells, width, "gx", 3), width, "gy", 2)


def crop(cells, have, want):
    cut = have - want
    assert cut >= 0
    if cut == 0:
        return cells
    return cells[..., cut:cells.shape[-2] - cut, cut:cells.shape[-1] - cut]


def shrunk_neighbours(cells):
    centre = cells[:, :, 1:-1, 1:-1]
    along_x = cells[:, :, 1:-1, :-2] + cells[:, :, 1:-1, 2:]
    along_y = cells[:, :, :-2, 1:-1] + cells[:, :, 2:, 1:-1]
    along_z = jnp.roll(centre, 1, 1) + jnp.roll(centre, -1, 1)
    return along_x + along_y + along_z


def spread_kernel(width, value, cells, out, below, above, land_x, land_y, send_x, recv_x,
                  send_y, recv_y, own_x, own_y, land_below, land_above, send_halo, recv_halo):
    count_x = lax.axis_size("gx")
    count_y = lax.axis_size("gy")
    at_x = lax.axis_index("gx")
    at_y = lax.axis_index("gy")
    mesh_ids = pl.DeviceIdType.MESH
    barrier = pltpu.get_barrier_semaphore()
    for step in range(1, count_x):
        pl.semaphore_signal(barrier, 1, device_id=(lax.rem(at_x + step, count_x), at_y),
                            device_id_type=mesh_ids)
    for step in range(1, count_y):
        pl.semaphore_signal(barrier, 1, device_id=(at_x, lax.rem(at_y + step, count_y)),
                            device_id_type=mesh_ids)
    pl.semaphore_wait(barrier, count_x + count_y - 2)

    rows_in = cells.shape[2]
    halo = []
    for slot, (first, target, step) in enumerate(((rows_in - width, land_below, 1), (0, land_above, -1))):
        copy = pltpu.make_async_remote_copy(
            src_ref=cells.at[:, :, pl.ds(first, width), :],
            dst_ref=target,
            send_sem=send_halo.at[slot],
            recv_sem=recv_halo.at[slot],
            device_id=(at_x, lax.rem(at_y + step + count_y, count_y)),
            device_id_type=mesh_ids,
        )
        copy.start()
        halo.append(copy)

    copies = []
    for step in range(1, count_x):
        copy = pltpu.make_async_remote_copy(
            src_ref=value,
            dst_ref=land_x.at[at_x],
            send_sem=send_x.at[step],
            recv_sem=recv_x.at[at_x],
            device_id=(lax.rem(at_x + step, count_x), at_y),
            device_id_type=mesh_ids,
        )
        copy.start()
        copies.append(copy)
    own = pltpu.make_async_copy(value, land_x.at[at_x], own_x)
    own.start()
    for step in range(1, count_x):
        copies[step - 1].wait_send()
        source = lax.rem(at_x + count_x - step, count_x)
        pltpu.make_async_remote_copy(
            src_ref=value,
            dst_ref=land_x.at[source],
            send_sem=send_x.at[step],
            recv_sem=recv_x.at[source],
            device_id=(source, at_y),
            device_id_type=mesh_ids,
        ).wait_recv()
    own.wait()

    rows = land_x.at[:, pl.ds(0, 1), :]
    copies = []
    for step in range(1, count_y):
        copy = pltpu.make_async_remote_copy(
            src_ref=rows,
            dst_ref=land_y.at[at_y],
            send_sem=send_y.at[step],
            recv_sem=recv_y.at[at_y],
            device_id=(at_x, lax.rem(at_y + step, count_y)),
            device_id_type=mesh_ids,
        )
        copy.start()
        copies.append(copy)
    own = pltpu.make_async_copy(rows, land_y.at[at_y], own_y)
    own.start()
    for step in range(1, count_y):
        copies[step - 1].wait_send()
        source = lax.rem(at_y + count_y - step, count_y)
        pltpu.make_async_remote_copy(
            src_ref=rows,
            dst_ref=land_y.at[source],
            send_sem=send_y.at[step],
            recv_sem=recv_y.at[source],
            device_id=(at_x, source),
            device_id_type=mesh_ids,
        ).wait_recv()
    own.wait()
    best = jnp.max(land_y[...], axis=(0, 1))
    out[...] = jnp.broadcast_to(best, out.shape)
    for copy in halo:
        copy.wait()
    below[...] = land_below[...]
    above[...] = land_above[...]


def global_max(block, cells, width):
    count_x = lax.axis_size("gx")
    count_y = lax.axis_size("gy")
    vmem = pl.BlockSpec(memory_space=pltpu.VMEM)
    face = cells.shape[:2] + (width,) + cells.shape[3:]
    spreads, below, above = pl.pallas_call(
        lambda *refs: spread_kernel(width, *refs),
        out_shape=(
            jax.ShapeDtypeStruct(block.shape, jnp.float32),
            jax.ShapeDtypeStruct(face, jnp.float32),
            jax.ShapeDtypeStruct(face, jnp.float32),
        ),
        in_specs=[vmem, vmem],
        out_specs=(vmem, vmem, vmem),
        scratch_shapes=[
            pltpu.VMEM((count_x,) + block.shape, jnp.float32),
            pltpu.VMEM((count_y, count_x, 1, block.shape[1]), jnp.float32),
            pltpu.SemaphoreType.DMA((count_x,)),
            pltpu.SemaphoreType.DMA((count_x,)),
            pltpu.SemaphoreType.DMA((count_y,)),
            pltpu.SemaphoreType.DMA((count_y,)),
            pltpu.SemaphoreType.DMA(()),
            pltpu.SemaphoreType.DMA(()),
            pltpu.VMEM(face, jnp.float32),
            pltpu.VMEM(face, jnp.float32),
            pltpu.SemaphoreType.DMA((2,)),
            pltpu.SemaphoreType.DMA((2,)),
        ],
        compiler_params=pltpu.CompilerParams(collective_id=0, has_side_effects=True),
    )(block, cells)
    return spreads, jnp.concatenate([below, cells, above], axis=2)


def restrict(field):
    lead, depth, rows, cols = field.shape
    count = lead * depth * rows
    pick_x = (np.arange(cols)[:, None] // 2 == np.arange(cols // 2)[None, :]).astype(np.float32)
    row = np.arange(count)
    target = ((row // (depth * rows)) * (depth // 2) + (row // rows) % depth // 2) * (rows // 2) + row % rows // 2
    pick_rows = (np.arange(count // 4)[:, None] == target[None, :]).astype(np.float32)
    pairs = jnp.dot(field.reshape(count, cols), pick_x, precision=lax.Precision.HIGHEST)
    blocks = jnp.dot(pick_rows, pairs, precision=lax.Precision.HIGHEST)
    return (blocks * 0.125).reshape(lead, depth // 2, rows // 2, cols // 2)


def prolong(field):
    return jnp.repeat(jnp.repeat(jnp.repeat(field, 2, 1), 2, 2), 2, 3)


def diffusions(level):
    scale = 0.25**level
    return jnp.array(
        [substrate_diffusion * scale, catalyst_diffusion * scale], jnp.float32
    ).reshape(2, 1, 1, 1)


def coefficients(fields, level):
    scale = 0.25**level
    diff_first = substrate_diffusion * scale
    diff_second = catalyst_diffusion * scale
    substrate, catalyst, feed_rate, kill_rate = (fields[0], fields[1], fields[2], fields[3])
    product = substrate * catalyst
    squared = catalyst * catalyst
    self_first = inverse_step + squared + feed_rate + 6.0 * diff_first
    cross_first = 2.0 * product
    cross_second = -squared
    self_second = inverse_step + feed_rate + kill_rate - 2.0 * product + 6.0 * diff_second
    coeff = jnp.stack([self_first, cross_first, cross_second, self_second])
    return coeff, (6.0 * diff_first + cross_first) / self_first, (6.0 * diff_second + squared) / self_second


class Level:
    def __init__(self, coeff, halo, level):
        self.coeff = coeff
        self.halo = halo
        self.level = level

    def at(self, halo):
        return crop(self.coeff, self.halo, halo)

    def operate(self, field, halo):
        coeff = self.at(halo - 1)
        centre = crop(field, halo, halo - 1)
        first = coeff[0] * centre[0] + coeff[1] * centre[1]
        second = coeff[2] * centre[0] + coeff[3] * centre[1]
        return jnp.stack([first, second]) - diffusions(self.level) * shrunk_neighbours(field)

    def diagonal(self, halo):
        coeff = self.at(halo)
        return jnp.stack([coeff[0], coeff[3]])


def chebyshev(ops, source, source_halo, start, start_halo, spread):
    upper = 1.0 + spread
    lower = lower_fraction * upper
    centre = (upper + lower) / 2.0
    half_width = (upper - lower) / 2.0
    ratio = centre / half_width
    damping = 1.0 / ratio
    if start is None:
        halo = source_halo
        resid = source / ops.diagonal(halo)
        update = resid / centre
        iterate = update
    else:
        halo = min(source_halo, start_halo - 1)
        applied = ops.operate(start, start_halo)
        resid = (crop(source, source_halo, halo) - crop(applied, start_halo - 1, halo)) / ops.diagonal(halo)
        update = resid / centre
        iterate = crop(start, start_halo, halo) + update
    for sweep in range(2):
        applied = ops.operate(iterate, halo)
        halo = halo - 1
        resid = (crop(source, source_halo, halo) - applied) / ops.diagonal(halo)
        damping_next = 1.0 / (2.0 * ratio - damping)
        update = damping_next * damping * crop(update, halo + 1, halo) + 2.0 * damping_next / half_width * resid
        iterate = crop(iterate, halo + 1, halo) + update
        damping = damping_next
    return iterate, halo


def body(state, previous, feed, kill):
    deep = 3
    fields = jnp.concatenate([state, feed[None], kill[None]], 0)
    fields_1 = restrict(fields)
    fields_2 = restrict(fields_1)
    lane = lax.broadcasted_iota(jnp.int32, (8, 128), 1)
    local = jnp.zeros((8, 128), jnp.float32)
    for level, level_fields in enumerate((fields, fields_1, fields_2)):
        _, first, second = coefficients(level_fields, level)
        local = jnp.where(lane == level, jnp.maximum(jnp.max(first), jnp.max(second)), local)
    spread_block, wide_y = global_max(local, jnp.concatenate([fields, previous], 0), 6)
    spreads = spread_block[0]
    wide = padded_along(wide_y, 6, "gx", 3)

    ops_0 = Level(coefficients(crop(wide[:4], 6, 5), 0)[0], 5, 0)
    state_w = wide[:2]
    substrate, catalyst = crop(state_w[0], 6, 5), crop(state_w[1], 6, 5)
    centre = crop(state_w, 6, 5)
    reaction = substrate * catalyst * catalyst
    laplace = shrunk_neighbours(state_w) - 6.0 * centre
    feed_w = crop(wide[2], 6, 5)
    kill_w = crop(wide[3], 6, 5)
    previous_w = crop(wide[4:6], 6, 5)
    local_terms = jnp.stack(
        [reaction - feed_w * (1.0 - substrate), -reaction + (feed_w + kill_w) * catalyst]
    )
    nonlinear = inverse_step * (centre - previous_w) - diffusions(0) * laplace + local_terms
    source_0 = -nonlinear
    pre_0, pre_0_halo = chebyshev(ops_0, source_0, 5, None, None, spreads[0])
    resid_0 = crop(source_0, 5, 0) - ops_0.operate(crop(pre_0, pre_0_halo, 1), 1)

    wide_1 = padded(jnp.concatenate([restrict(resid_0), fields_1], 0), 7)
    ops_1 = Level(coefficients(wide_1[2:], 1)[0], 7, 1)
    source_1 = wide_1[:2]
    pre_1, pre_1_halo = chebyshev(ops_1, source_1, 7, None, None, spreads[1])
    resid_1 = crop(source_1, 7, 0) - ops_1.operate(crop(pre_1, pre_1_halo, 1), 1)

    wide_2 = padded(jnp.concatenate([restrict(resid_1), fields_2], 0), 8)
    ops_2 = Level(coefficients(wide_2[2:], 2)[0], 8, 2)
    source_2 = wide_2[:2]
    first_2, first_2_halo = chebyshev(ops_2, source_2, 8, None, None, spreads[2])
    coarse_2, coarse_2_halo = chebyshev(ops_2, source_2, 8, first_2, first_2_halo, spreads[2])

    start_1 = crop(pre_1, pre_1_halo, 5) + crop(prolong(coarse_2), 2 * coarse_2_halo, 5)
    post_1, post_1_halo = chebyshev(ops_1, source_1, 7, start_1, 5, spreads[1])

    start_0 = crop(pre_0, pre_0_halo, 3) + crop(prolong(post_1), 2 * post_1_halo, 3)
    post_0, post_0_halo = chebyshev(ops_0, source_0, 5, start_0, 3, spreads[0])
    return crop(post_0, post_0_halo, 0)


def solution(mesh):
    placed = (
        P(None, None, "gy", "gx"),
        P(None, None, "gy", "gx"),
        P(None, "gy", "gx"),
        P(None, "gy", "gx"),
    )
    return jax.shard_map(
        body, mesh=mesh, in_specs=placed, out_specs=P(None, None, "gy", "gx"), check_vma=False
    )
```

```python
import numpy as np
import jax
import jax.numpy as jnp
from jax import lax
from jax.sharding import PartitionSpec as P
from jax.experimental import pallas as pl
from jax.experimental.pallas import tpu as pltpu

substrate_diffusion = 40.0
catalyst_diffusion = 20.0
inverse_step = 2.0
lower_fraction = 0.25
coarsenings = 2


def padded_along(cells, width, axis, dim):
    count = lax.axis_size(axis)
    size = cells.shape[dim]
    below, above = [], []
    remaining, distance = width, 1
    while remaining > 0:
        take = min(remaining, size)
        tail = lax.slice_in_dim(cells, size - take, size, axis=dim)
        head = lax.slice_in_dim(cells, 0, take, axis=dim)
        below.insert(0, lax.ppermute(tail, axis, [(i, (i + distance) % count) for i in range(count)]))
        above.append(lax.ppermute(head, axis, [((i + distance) % count, i) for i in range(count)]))
        remaining -= take
        distance += 1
    return jnp.concatenate(below + [cells] + above, axis=dim)


def padded(cells, width):
    return padded_along(padded_along(cells, width, "gx", 3), width, "gy", 2)


def crop(cells, have, want):
    cut = have - want
    assert cut >= 0
    if cut == 0:
        return cells
    return cells[..., cut:cells.shape[-2] - cut, cut:cells.shape[-1] - cut]


def shrunk_neighbours(cells):
    centre = cells[:, :, 1:-1, 1:-1]
    along_x = cells[:, :, 1:-1, :-2] + cells[:, :, 1:-1, 2:]
    along_y = cells[:, :, :-2, 1:-1] + cells[:, :, 2:, 1:-1]
    along_z = jnp.roll(centre, 1, 1) + jnp.roll(centre, -1, 1)
    return along_x + along_y + along_z


def spread_kernel(value, out, land_x, land_y, send_x, recv_x, send_y, recv_y, own_x, own_y):
    count_x = lax.axis_size("gx")
    count_y = lax.axis_size("gy")
    at_x = lax.axis_index("gx")
    at_y = lax.axis_index("gy")
    mesh_ids = pl.DeviceIdType.MESH
    barrier = pltpu.get_barrier_semaphore()
    for step in range(1, count_x):
        pl.semaphore_signal(barrier, 1, device_id=(lax.rem(at_x + step, count_x), at_y),
                            device_id_type=mesh_ids)
    for step in range(1, count_y):
        pl.semaphore_signal(barrier, 1, device_id=(at_x, lax.rem(at_y + step, count_y)),
                            device_id_type=mesh_ids)
    pl.semaphore_wait(barrier, count_x + count_y - 2)

    copies = []
    for step in range(1, count_x):
        copy = pltpu.make_async_remote_copy(
            src_ref=value,
            dst_ref=land_x.at[at_x],
            send_sem=send_x.at[step],
            recv_sem=recv_x.at[at_x],
            device_id=(lax.rem(at_x + step, count_x), at_y),
            device_id_type=mesh_ids,
        )
        copy.start()
        copies.append(copy)
    own = pltpu.make_async_copy(value, land_x.at[at_x], own_x)
    own.start()
    for step in range(1, count_x):
        copies[step - 1].wait_send()
        source = lax.rem(at_x + count_x - step, count_x)
        pltpu.make_async_remote_copy(
            src_ref=value,
            dst_ref=land_x.at[source],
            send_sem=send_x.at[step],
            recv_sem=recv_x.at[source],
            device_id=(source, at_y),
            device_id_type=mesh_ids,
        ).wait_recv()
    own.wait()

    rows = land_x.at[:, pl.ds(0, 1), :]
    copies = []
    for step in range(1, count_y):
        copy = pltpu.make_async_remote_copy(
            src_ref=rows,
            dst_ref=land_y.at[at_y],
            send_sem=send_y.at[step],
            recv_sem=recv_y.at[at_y],
            device_id=(at_x, lax.rem(at_y + step, count_y)),
            device_id_type=mesh_ids,
        )
        copy.start()
        copies.append(copy)
    own = pltpu.make_async_copy(rows, land_y.at[at_y], own_y)
    own.start()
    for step in range(1, count_y):
        copies[step - 1].wait_send()
        source = lax.rem(at_y + count_y - step, count_y)
        pltpu.make_async_remote_copy(
            src_ref=rows,
            dst_ref=land_y.at[source],
            send_sem=send_y.at[step],
            recv_sem=recv_y.at[source],
            device_id=(at_x, source),
            device_id_type=mesh_ids,
        ).wait_recv()
    own.wait()
    best = jnp.max(land_y[...], axis=(0, 1))
    out[...] = jnp.broadcast_to(best, out.shape)


def global_max(block):
    count_x = lax.axis_size("gx")
    count_y = lax.axis_size("gy")
    vmem = pl.BlockSpec(memory_space=pltpu.VMEM)
    return pl.pallas_call(
        spread_kernel,
        out_shape=jax.ShapeDtypeStruct(block.shape, jnp.float32),
        in_specs=[vmem],
        out_specs=vmem,
        scratch_shapes=[
            pltpu.VMEM((count_x,) + block.shape, jnp.float32),
            pltpu.VMEM((count_y, count_x, 1, block.shape[1]), jnp.float32),
            pltpu.SemaphoreType.DMA((count_x,)),
            pltpu.SemaphoreType.DMA((count_x,)),
            pltpu.SemaphoreType.DMA((count_y,)),
            pltpu.SemaphoreType.DMA((count_y,)),
            pltpu.SemaphoreType.DMA(()),
            pltpu.SemaphoreType.DMA(()),
        ],
        compiler_params=pltpu.CompilerParams(collective_id=0, has_side_effects=True),
    )(block)


def restrict(field):
    lead, depth, rows, cols = field.shape
    count = lead * depth * rows
    pick_x = (np.arange(cols)[:, None] // 2 == np.arange(cols // 2)[None, :]).astype(np.float32)
    row = np.arange(count)
    target = ((row // (depth * rows)) * (depth // 2) + (row // rows) % depth // 2) * (rows // 2) + row % rows // 2
    pick_rows = (np.arange(count // 4)[:, None] == target[None, :]).astype(np.float32)
    pairs = jnp.dot(field.reshape(count, cols), pick_x, precision=lax.Precision.HIGHEST)
    blocks = jnp.dot(pick_rows, pairs, precision=lax.Precision.HIGHEST)
    return (blocks * 0.125).reshape(lead, depth // 2, rows // 2, cols // 2)


def prolong(field):
    return jnp.repeat(jnp.repeat(jnp.repeat(field, 2, 1), 2, 2), 2, 3)


def diffusions(level):
    scale = 0.25**level
    return jnp.array(
        [substrate_diffusion * scale, catalyst_diffusion * scale], jnp.float32
    ).reshape(2, 1, 1, 1)


def coefficients(fields, level):
    scale = 0.25**level
    diff_first = substrate_diffusion * scale
    diff_second = catalyst_diffusion * scale
    substrate, catalyst, feed_rate, kill_rate = (fields[0], fields[1], fields[2], fields[3])
    product = substrate * catalyst
    squared = catalyst * catalyst
    self_first = inverse_step + squared + feed_rate + 6.0 * diff_first
    cross_first = 2.0 * product
    cross_second = -squared
    self_second = inverse_step + feed_rate + kill_rate - 2.0 * product + 6.0 * diff_second
    coeff = jnp.stack([self_first, cross_first, cross_second, self_second])
    return coeff, (6.0 * diff_first + cross_first) / self_first, (6.0 * diff_second + squared) / self_second


class Level:
    def __init__(self, coeff, halo, level):
        self.coeff = coeff
        self.halo = halo
        self.level = level

    def at(self, halo):
        return crop(self.coeff, self.halo, halo)

    def operate(self, field, halo):
        coeff = self.at(halo - 1)
        centre = crop(field, halo, halo - 1)
        first = coeff[0] * centre[0] + coeff[1] * centre[1]
        second = coeff[2] * centre[0] + coeff[3] * centre[1]
        return jnp.stack([first, second]) - diffusions(self.level) * shrunk_neighbours(field)

    def diagonal(self, halo):
        coeff = self.at(halo)
        return jnp.stack([coeff[0], coeff[3]])


def chebyshev(ops, source, source_halo, start, start_halo, spread):
    upper = 1.0 + spread
    lower = lower_fraction * upper
    centre = (upper + lower) / 2.0
    half_width = (upper - lower) / 2.0
    ratio = centre / half_width
    damping = 1.0 / ratio
    if start is None:
        halo = source_halo
        resid = source / ops.diagonal(halo)
        update = resid / centre
        iterate = update
    else:
        halo = min(source_halo, start_halo - 1)
        applied = ops.operate(start, start_halo)
        resid = (crop(source, source_halo, halo) - crop(applied, start_halo - 1, halo)) / ops.diagonal(halo)
        update = resid / centre
        iterate = crop(start, start_halo, halo) + update
    for sweep in range(2):
        applied = ops.operate(iterate, halo)
        halo = halo - 1
        resid = (crop(source, source_halo, halo) - applied) / ops.diagonal(halo)
        damping_next = 1.0 / (2.0 * ratio - damping)
        update = damping_next * damping * crop(update, halo + 1, halo) + 2.0 * damping_next / half_width * resid
        iterate = crop(iterate, halo + 1, halo) + update
        damping = damping_next
    return iterate, halo


def body(state, previous, feed, kill):
    deep = 3
    fields = jnp.concatenate([state, feed[None], kill[None]], 0)
    fields_1 = restrict(fields)
    fields_2 = restrict(fields_1)
    lane = lax.broadcasted_iota(jnp.int32, (8, 128), 1)
    local = jnp.zeros((8, 128), jnp.float32)
    for level, level_fields in enumerate((fields, fields_1, fields_2)):
        _, first, second = coefficients(level_fields, level)
        local = jnp.where(lane == level, jnp.maximum(jnp.max(first), jnp.max(second)), local)
    wide_x = padded_along(jnp.concatenate([fields, previous], 0), 6, "gy", 2)
    local, wide_x = lax.optimization_barrier((local, wide_x))
    spreads = global_max(local)[0]

    wide = padded_along(wide_x, 6, "gx", 3)
    ops_0 = Level(coefficients(crop(wide[:4], 6, 5), 0)[0], 5, 0)
    state_w = wide[:2]
    substrate, catalyst = crop(state_w[0], 6, 5), crop(state_w[1], 6, 5)
    centre = crop(state_w, 6, 5)
    reaction = substrate * catalyst * catalyst
    laplace = shrunk_neighbours(state_w) - 6.0 * centre
    feed_w = crop(wide[2], 6, 5)
    kill_w = crop(wide[3], 6, 5)
    previous_w = crop(wide[4:6], 6, 5)
    local_terms = jnp.stack(
        [reaction - feed_w * (1.0 - substrate), -reaction + (feed_w + kill_w) * catalyst]
    )
    nonlinear = inverse_step * (centre - previous_w) - diffusions(0) * laplace + local_terms
    source_0 = -nonlinear
    pre_0, pre_0_halo = chebyshev(ops_0, source_0, 5, None, None, spreads[0])
    resid_0 = crop(source_0, 5, 0) - ops_0.operate(crop(pre_0, pre_0_halo, 1), 1)

    wide_1 = padded(jnp.concatenate([restrict(resid_0), fields_1], 0), 7)
    ops_1 = Level(coefficients(wide_1[2:], 1)[0], 7, 1)
    source_1 = wide_1[:2]
    pre_1, pre_1_halo = chebyshev(ops_1, source_1, 7, None, None, spreads[1])
    resid_1 = crop(source_1, 7, 0) - ops_1.operate(crop(pre_1, pre_1_halo, 1), 1)

    wide_2 = padded(jnp.concatenate([restrict(resid_1), fields_2], 0), 8)
    ops_2 = Level(coefficients(wide_2[2:], 2)[0], 8, 2)
    source_2 = wide_2[:2]
    first_2, first_2_halo = chebyshev(ops_2, source_2, 8, None, None, spreads[2])
    coarse_2, coarse_2_halo = chebyshev(ops_2, source_2, 8, first_2, first_2_halo, spreads[2])

    start_1 = crop(pre_1, pre_1_halo, 5) + crop(prolong(coarse_2), 2 * coarse_2_halo, 5)
    post_1, post_1_halo = chebyshev(ops_1, source_1, 7, start_1, 5, spreads[1])

    start_0 = crop(pre_0, pre_0_halo, 3) + crop(prolong(post_1), 2 * post_1_halo, 3)
    post_0, post_0_halo = chebyshev(ops_0, source_0, 5, start_0, 3, spreads[0])
    return crop(post_0, post_0_halo, 0)


def solution(mesh):
    placed = (
        P(None, None, "gy", "gx"),
        P(None, None, "gy", "gx"),
        P(None, "gy", "gx"),
        P(None, "gy", "gx"),
    )
    return jax.shard_map(
        body, mesh=mesh, in_specs=placed, out_specs=P(None, None, "gy", "gx"), check_vma=False
    )
```

```python
import numpy as np
import jax
import jax.numpy as jnp
from jax import lax
from jax.sharding import PartitionSpec as P
from jax.experimental import pallas as pl
from jax.experimental.pallas import tpu as pltpu

substrate_diffusion = 40.0
catalyst_diffusion = 20.0
inverse_step = 2.0
lower_fraction = 0.25
coarsenings = 2


def padded_along(cells, width, axis, dim):
    count = lax.axis_size(axis)
    size = cells.shape[dim]
    below, above = [], []
    remaining, distance = width, 1
    while remaining > 0:
        take = min(remaining, size)
        tail = lax.slice_in_dim(cells, size - take, size, axis=dim)
        head = lax.slice_in_dim(cells, 0, take, axis=dim)
        below.insert(0, lax.ppermute(tail, axis, [(i, (i + distance) % count) for i in range(count)]))
        above.append(lax.ppermute(head, axis, [((i + distance) % count, i) for i in range(count)]))
        remaining -= take
        distance += 1
    return jnp.concatenate(below + [cells] + above, axis=dim)


def padded(cells, width):
    return padded_along(padded_along(cells, width, "gx", 3), width, "gy", 2)


def crop(cells, have, want):
    cut = have - want
    assert cut >= 0
    if cut == 0:
        return cells
    return cells[..., cut:cells.shape[-2] - cut, cut:cells.shape[-1] - cut]


def shrunk_neighbours(cells):
    centre = cells[:, :, 1:-1, 1:-1]
    along_x = cells[:, :, 1:-1, :-2] + cells[:, :, 1:-1, 2:]
    along_y = cells[:, :, :-2, 1:-1] + cells[:, :, 2:, 1:-1]
    along_z = jnp.roll(centre, 1, 1) + jnp.roll(centre, -1, 1)
    return along_x + along_y + along_z


def gather_rows(source, land, send_sem, recv_sem, own_sem, device, count, me):
    mesh_ids = pl.DeviceIdType.MESH
    copies = []
    for step in range(1, count):
        copy = pltpu.make_async_remote_copy(
            src_ref=source,
            dst_ref=land.at[me],
            send_sem=send_sem.at[step],
            recv_sem=recv_sem.at[me],
            device_id=device(lax.rem(me + step, count)),
            device_id_type=mesh_ids,
        )
        copy.start()
        copies.append(copy)
    own = pltpu.make_async_copy(source, land.at[me], own_sem)
    own.start()
    for step in range(1, count):
        copies[step - 1].wait_send()
        sender = lax.rem(me + count - step, count)
        pltpu.make_async_remote_copy(
            src_ref=source,
            dst_ref=land.at[sender],
            send_sem=send_sem.at[step],
            recv_sem=recv_sem.at[sender],
            device_id=device(sender),
            device_id_type=mesh_ids,
        ).wait_recv()
    own.wait()


def spread_kernel(inner, value, out, land_x, land_z, land_y, send_x, recv_x, send_z, recv_z,
                  send_y, recv_y, own_x, own_z, own_y):
    count_x = lax.axis_size("gx")
    count_y = lax.axis_size("gy")
    outer = count_y // inner
    at_x = lax.axis_index("gx")
    at_y = lax.axis_index("gy")
    group, place = at_y // inner, lax.rem(at_y, inner)
    mesh_ids = pl.DeviceIdType.MESH
    along_x = lambda index: (index, at_y)
    along_z = lambda index: (at_x, group * inner + index)
    along_y = lambda index: (at_x, index * inner + place)
    barrier = pltpu.get_barrier_semaphore()
    for count, me, device in ((count_x, at_x, along_x), (inner, place, along_z), (outer, group, along_y)):
        for step in range(1, count):
            pl.semaphore_signal(barrier, 1, device_id=device(lax.rem(me + step, count)),
                                device_id_type=mesh_ids)
    pl.semaphore_wait(barrier, count_x + inner + outer - 3)
    gather_rows(value, land_x, send_x, recv_x, own_x, along_x, count_x, at_x)
    gather_rows(land_x.at[:, pl.ds(0, 1), :], land_z, send_z, recv_z, own_z, along_z, inner, place)
    gather_rows(land_z, land_y, send_y, recv_y, own_y, along_y, outer, group)
    best = jnp.max(land_y[...], axis=(0, 1, 2))
    out[...] = jnp.broadcast_to(best, out.shape)


def global_max(block):
    count_x = lax.axis_size("gx")
    count_y = lax.axis_size("gy")
    inner = 8 if count_y % 8 == 0 else count_y
    outer = count_y // inner
    vmem = pl.BlockSpec(memory_space=pltpu.VMEM)
    lanes = block.shape[1]
    return pl.pallas_call(
        lambda *refs: spread_kernel(inner, *refs),
        out_shape=jax.ShapeDtypeStruct(block.shape, jnp.float32),
        in_specs=[vmem],
        out_specs=vmem,
        scratch_shapes=[
            pltpu.VMEM((count_x,) + block.shape, jnp.float32),
            pltpu.VMEM((inner, count_x, 1, lanes), jnp.float32),
            pltpu.VMEM((outer, inner, count_x, 1, lanes), jnp.float32),
            pltpu.SemaphoreType.DMA((count_x,)),
            pltpu.SemaphoreType.DMA((count_x,)),
            pltpu.SemaphoreType.DMA((inner,)),
            pltpu.SemaphoreType.DMA((inner,)),
            pltpu.SemaphoreType.DMA((outer,)),
            pltpu.SemaphoreType.DMA((outer,)),
            pltpu.SemaphoreType.DMA(()),
            pltpu.SemaphoreType.DMA(()),
            pltpu.SemaphoreType.DMA(()),
        ],
        compiler_params=pltpu.CompilerParams(collective_id=0, has_side_effects=True),
    )(block)


def restrict(field):
    lead, depth, rows, cols = field.shape
    count = lead * depth * rows
    pick_x = (np.arange(cols)[:, None] // 2 == np.arange(cols // 2)[None, :]).astype(np.float32)
    row = np.arange(count)
    target = ((row // (depth * rows)) * (depth // 2) + (row // rows) % depth // 2) * (rows // 2) + row % rows // 2
    pick_rows = (np.arange(count // 4)[:, None] == target[None, :]).astype(np.float32)
    pairs = jnp.dot(field.reshape(count, cols), pick_x, precision=lax.Precision.HIGHEST)
    blocks = jnp.dot(pick_rows, pairs, precision=lax.Precision.HIGHEST)
    return (blocks * 0.125).reshape(lead, depth // 2, rows // 2, cols // 2)


def prolong(field):
    return jnp.repeat(jnp.repeat(jnp.repeat(field, 2, 1), 2, 2), 2, 3)


def diffusions(level):
    scale = 0.25**level
    return jnp.array(
        [substrate_diffusion * scale, catalyst_diffusion * scale], jnp.float32
    ).reshape(2, 1, 1, 1)


def coefficients(fields, level):
    scale = 0.25**level
    diff_first = substrate_diffusion * scale
    diff_second = catalyst_diffusion * scale
    substrate, catalyst, feed_rate, kill_rate = (fields[0], fields[1], fields[2], fields[3])
    product = substrate * catalyst
    squared = catalyst * catalyst
    self_first = inverse_step + squared + feed_rate + 6.0 * diff_first
    cross_first = 2.0 * product
    cross_second = -squared
    self_second = inverse_step + feed_rate + kill_rate - 2.0 * product + 6.0 * diff_second
    coeff = jnp.stack([self_first, cross_first, cross_second, self_second])
    return coeff, (6.0 * diff_first + cross_first) / self_first, (6.0 * diff_second + squared) / self_second


class Level:
    def __init__(self, coeff, halo, level):
        self.coeff = coeff
        self.halo = halo
        self.level = level

    def at(self, halo):
        return crop(self.coeff, self.halo, halo)

    def operate(self, field, halo):
        coeff = self.at(halo - 1)
        centre = crop(field, halo, halo - 1)
        first = coeff[0] * centre[0] + coeff[1] * centre[1]
        second = coeff[2] * centre[0] + coeff[3] * centre[1]
        return jnp.stack([first, second]) - diffusions(self.level) * shrunk_neighbours(field)

    def diagonal(self, halo):
        coeff = self.at(halo)
        return jnp.stack([coeff[0], coeff[3]])


def chebyshev(ops, source, source_halo, start, start_halo, spread):
    upper = 1.0 + spread
    lower = lower_fraction * upper
    centre = (upper + lower) / 2.0
    half_width = (upper - lower) / 2.0
    ratio = centre / half_width
    damping = 1.0 / ratio
    if start is None:
        halo = source_halo
        resid = source / ops.diagonal(halo)
        update = resid / centre
        iterate = update
    else:
        halo = min(source_halo, start_halo - 1)
        applied = ops.operate(start, start_halo)
        resid = (crop(source, source_halo, halo) - crop(applied, start_halo - 1, halo)) / ops.diagonal(halo)
        update = resid / centre
        iterate = crop(start, start_halo, halo) + update
    for sweep in range(2):
        applied = ops.operate(iterate, halo)
        halo = halo - 1
        resid = (crop(source, source_halo, halo) - applied) / ops.diagonal(halo)
        damping_next = 1.0 / (2.0 * ratio - damping)
        update = damping_next * damping * crop(update, halo + 1, halo) + 2.0 * damping_next / half_width * resid
        iterate = crop(iterate, halo + 1, halo) + update
        damping = damping_next
    return iterate, halo


def body(state, previous, feed, kill):
    deep = 3
    fields = jnp.concatenate([state, feed[None], kill[None]], 0)
    fields_1 = restrict(fields)
    fields_2 = restrict(fields_1)
    lane = lax.broadcasted_iota(jnp.int32, (8, 128), 1)
    local = jnp.zeros((8, 128), jnp.float32)
    for level, level_fields in enumerate((fields, fields_1, fields_2)):
        _, first, second = coefficients(level_fields, level)
        local = jnp.where(lane == level, jnp.maximum(jnp.max(first), jnp.max(second)), local)
    wide_x = padded_along(jnp.concatenate([fields, previous], 0), 6, "gx", 3)
    local, wide_x = lax.optimization_barrier((local, wide_x))
    spreads = global_max(local)[0]

    wide = padded_along(wide_x, 6, "gy", 2)
    ops_0 = Level(coefficients(crop(wide[:4], 6, 5), 0)[0], 5, 0)
    state_w = wide[:2]
    substrate, catalyst = crop(state_w[0], 6, 5), crop(state_w[1], 6, 5)
    centre = crop(state_w, 6, 5)
    reaction = substrate * catalyst * catalyst
    laplace = shrunk_neighbours(state_w) - 6.0 * centre
    feed_w = crop(wide[2], 6, 5)
    kill_w = crop(wide[3], 6, 5)
    previous_w = crop(wide[4:6], 6, 5)
    local_terms = jnp.stack(
        [reaction - feed_w * (1.0 - substrate), -reaction + (feed_w + kill_w) * catalyst]
    )
    nonlinear = inverse_step * (centre - previous_w) - diffusions(0) * laplace + local_terms
    source_0 = -nonlinear
    pre_0, pre_0_halo = chebyshev(ops_0, source_0, 5, None, None, spreads[0])
    resid_0 = crop(source_0, 5, 0) - ops_0.operate(crop(pre_0, pre_0_halo, 1), 1)

    wide_1 = padded(jnp.concatenate([restrict(resid_0), fields_1], 0), 7)
    ops_1 = Level(coefficients(wide_1[2:], 1)[0], 7, 1)
    source_1 = wide_1[:2]
    pre_1, pre_1_halo = chebyshev(ops_1, source_1, 7, None, None, spreads[1])
    resid_1 = crop(source_1, 7, 0) - ops_1.operate(crop(pre_1, pre_1_halo, 1), 1)

    wide_2 = padded(jnp.concatenate([restrict(resid_1), fields_2], 0), 8)
    ops_2 = Level(coefficients(wide_2[2:], 2)[0], 8, 2)
    source_2 = wide_2[:2]
    first_2, first_2_halo = chebyshev(ops_2, source_2, 8, None, None, spreads[2])
    coarse_2, coarse_2_halo = chebyshev(ops_2, source_2, 8, first_2, first_2_halo, spreads[2])

    start_1 = crop(pre_1, pre_1_halo, 5) + crop(prolong(coarse_2), 2 * coarse_2_halo, 5)
    post_1, post_1_halo = chebyshev(ops_1, source_1, 7, start_1, 5, spreads[1])

    start_0 = crop(pre_0, pre_0_halo, 3) + crop(prolong(post_1), 2 * post_1_halo, 3)
    post_0, post_0_halo = chebyshev(ops_0, source_0, 5, start_0, 3, spreads[0])
    return crop(post_0, post_0_halo, 0)


def solution(mesh):
    placed = (
        P(None, None, "gy", "gx"),
        P(None, None, "gy", "gx"),
        P(None, "gy", "gx"),
        P(None, "gy", "gx"),
    )
    return jax.shard_map(
        body, mesh=mesh, in_specs=placed, out_specs=P(None, None, "gy", "gx"), check_vma=False
    )
```

```python
import numpy as np
import jax
import jax.numpy as jnp
from jax import lax
from jax.sharding import PartitionSpec as P
from jax.experimental import pallas as pl
from jax.experimental.pallas import tpu as pltpu

substrate_diffusion = 40.0
catalyst_diffusion = 20.0
inverse_step = 2.0
lower_fraction = 0.25
coarsenings = 2


def padded_along(cells, width, axis, dim):
    count = lax.axis_size(axis)
    size = cells.shape[dim]
    below, above = [], []
    remaining, distance = width, 1
    while remaining > 0:
        take = min(remaining, size)
        tail = lax.slice_in_dim(cells, size - take, size, axis=dim)
        head = lax.slice_in_dim(cells, 0, take, axis=dim)
        below.insert(0, lax.ppermute(tail, axis, [(i, (i + distance) % count) for i in range(count)]))
        above.append(lax.ppermute(head, axis, [((i + distance) % count, i) for i in range(count)]))
        remaining -= take
        distance += 1
    return jnp.concatenate(below + [cells] + above, axis=dim)


def padded(cells, width):
    return padded_along(padded_along(cells, width, "gx", 3), width, "gy", 2)


def crop(cells, have, want):
    cut = have - want
    assert cut >= 0
    if cut == 0:
        return cells
    return cells[..., cut:cells.shape[-2] - cut, cut:cells.shape[-1] - cut]


def shrunk_neighbours(cells):
    centre = cells[:, :, 1:-1, 1:-1]
    along_x = cells[:, :, 1:-1, :-2] + cells[:, :, 1:-1, 2:]
    along_y = cells[:, :, :-2, 1:-1] + cells[:, :, 2:, 1:-1]
    along_z = jnp.roll(centre, 1, 1) + jnp.roll(centre, -1, 1)
    return along_x + along_y + along_z


def gather_rows(source, land, send_sem, recv_sem, own_sem, device, count, me):
    mesh_ids = pl.DeviceIdType.MESH
    copies = []
    for step in range(1, count):
        copy = pltpu.make_async_remote_copy(
            src_ref=source,
            dst_ref=land.at[me],
            send_sem=send_sem.at[step],
            recv_sem=recv_sem.at[me],
            device_id=device(lax.rem(me + step, count)),
            device_id_type=mesh_ids,
        )
        copy.start()
        copies.append(copy)
    own = pltpu.make_async_copy(source, land.at[me], own_sem)
    own.start()
    for step in range(1, count):
        copies[step - 1].wait_send()
        sender = lax.rem(me + count - step, count)
        pltpu.make_async_remote_copy(
            src_ref=source,
            dst_ref=land.at[sender],
            send_sem=send_sem.at[step],
            recv_sem=recv_sem.at[sender],
            device_id=device(sender),
            device_id_type=mesh_ids,
        ).wait_recv()
    own.wait()


def spread_kernel(pair, inner, value, out, land_c, land_x, land_z, land_y, send_c, recv_c,
                  send_x, recv_x, send_z, recv_z, send_y, recv_y, own_c, own_x, own_z, own_y):
    count_x = lax.axis_size("gx")
    count_y = lax.axis_size("gy")
    chips, outer = count_x // pair, count_y // inner
    at_x = lax.axis_index("gx")
    at_y = lax.axis_index("gy")
    chip, core = at_x // pair, lax.rem(at_x, pair)
    group, place = at_y // inner, lax.rem(at_y, inner)
    mesh_ids = pl.DeviceIdType.MESH
    along_c = lambda index: (chip * pair + index, at_y)
    along_x = lambda index: (index * pair + core, at_y)
    along_z = lambda index: (at_x, group * inner + index)
    along_y = lambda index: (at_x, index * inner + place)
    stages = ((pair, core, along_c), (chips, chip, along_x), (inner, place, along_z), (outer, group, along_y))
    barrier = pltpu.get_barrier_semaphore()
    for count, me, device in stages:
        for step in range(1, count):
            pl.semaphore_signal(barrier, 1, device_id=device(lax.rem(me + step, count)),
                                device_id_type=mesh_ids)
    pl.semaphore_wait(barrier, pair + chips + inner + outer - 4)
    gather_rows(value, land_c, send_c, recv_c, own_c, along_c, pair, core)
    gather_rows(land_c.at[:, pl.ds(0, 1), :], land_x, send_x, recv_x, own_x, along_x, chips, chip)
    gather_rows(land_x, land_z, send_z, recv_z, own_z, along_z, inner, place)
    gather_rows(land_z, land_y, send_y, recv_y, own_y, along_y, outer, group)
    best = jnp.max(land_y[...], axis=(0, 1, 2, 3))
    out[...] = jnp.broadcast_to(best, out.shape)


def global_max(block):
    count_x = lax.axis_size("gx")
    count_y = lax.axis_size("gy")
    pair = 2 if count_x % 2 == 0 else 1
    inner = 8 if count_y % 8 == 0 else count_y
    chips, outer = count_x // pair, count_y // inner
    vmem = pl.BlockSpec(memory_space=pltpu.VMEM)
    lanes = block.shape[1]
    semaphores = []
    for count in (pair, chips, inner, outer):
        semaphores += [pltpu.SemaphoreType.DMA((count,)), pltpu.SemaphoreType.DMA((count,))]
    return pl.pallas_call(
        lambda *refs: spread_kernel(pair, inner, *refs),
        out_shape=jax.ShapeDtypeStruct(block.shape, jnp.float32),
        in_specs=[vmem],
        out_specs=vmem,
        scratch_shapes=[
            pltpu.VMEM((pair,) + block.shape, jnp.float32),
            pltpu.VMEM((chips, pair, 1, lanes), jnp.float32),
            pltpu.VMEM((inner, chips, pair, 1, lanes), jnp.float32),
            pltpu.VMEM((outer, inner, chips, pair, 1, lanes), jnp.float32),
        ] + semaphores + [pltpu.SemaphoreType.DMA(())] * 4,
        compiler_params=pltpu.CompilerParams(collective_id=0, has_side_effects=True),
    )(block)


def restrict(field):
    lead, depth, rows, cols = field.shape
    count = lead * depth * rows
    pick_x = (np.arange(cols)[:, None] // 2 == np.arange(cols // 2)[None, :]).astype(np.float32)
    row = np.arange(count)
    target = ((row // (depth * rows)) * (depth // 2) + (row // rows) % depth // 2) * (rows // 2) + row % rows // 2
    pick_rows = (np.arange(count // 4)[:, None] == target[None, :]).astype(np.float32)
    pairs = jnp.dot(field.reshape(count, cols), pick_x, precision=lax.Precision.HIGHEST)
    blocks = jnp.dot(pick_rows, pairs, precision=lax.Precision.HIGHEST)
    return (blocks * 0.125).reshape(lead, depth // 2, rows // 2, cols // 2)


def prolong(field):
    return jnp.repeat(jnp.repeat(jnp.repeat(field, 2, 1), 2, 2), 2, 3)


def diffusions(level):
    scale = 0.25**level
    return jnp.array(
        [substrate_diffusion * scale, catalyst_diffusion * scale], jnp.float32
    ).reshape(2, 1, 1, 1)


def coefficients(fields, level):
    scale = 0.25**level
    diff_first = substrate_diffusion * scale
    diff_second = catalyst_diffusion * scale
    substrate, catalyst, feed_rate, kill_rate = (fields[0], fields[1], fields[2], fields[3])
    product = substrate * catalyst
    squared = catalyst * catalyst
    self_first = inverse_step + squared + feed_rate + 6.0 * diff_first
    cross_first = 2.0 * product
    cross_second = -squared
    self_second = inverse_step + feed_rate + kill_rate - 2.0 * product + 6.0 * diff_second
    coeff = jnp.stack([self_first, cross_first, cross_second, self_second])
    return coeff, (6.0 * diff_first + cross_first) / self_first, (6.0 * diff_second + squared) / self_second


class Level:
    def __init__(self, coeff, halo, level):
        self.coeff = coeff
        self.halo = halo
        self.level = level

    def at(self, halo):
        return crop(self.coeff, self.halo, halo)

    def operate(self, field, halo):
        coeff = self.at(halo - 1)
        centre = crop(field, halo, halo - 1)
        first = coeff[0] * centre[0] + coeff[1] * centre[1]
        second = coeff[2] * centre[0] + coeff[3] * centre[1]
        return jnp.stack([first, second]) - diffusions(self.level) * shrunk_neighbours(field)

    def diagonal(self, halo):
        coeff = self.at(halo)
        return jnp.stack([coeff[0], coeff[3]])


def chebyshev(ops, source, source_halo, start, start_halo, spread):
    upper = 1.0 + spread
    lower = lower_fraction * upper
    centre = (upper + lower) / 2.0
    half_width = (upper - lower) / 2.0
    ratio = centre / half_width
    damping = 1.0 / ratio
    if start is None:
        halo = source_halo
        resid = source / ops.diagonal(halo)
        update = resid / centre
        iterate = update
    else:
        halo = min(source_halo, start_halo - 1)
        applied = ops.operate(start, start_halo)
        resid = (crop(source, source_halo, halo) - crop(applied, start_halo - 1, halo)) / ops.diagonal(halo)
        update = resid / centre
        iterate = crop(start, start_halo, halo) + update
    for sweep in range(2):
        applied = ops.operate(iterate, halo)
        halo = halo - 1
        resid = (crop(source, source_halo, halo) - applied) / ops.diagonal(halo)
        damping_next = 1.0 / (2.0 * ratio - damping)
        update = damping_next * damping * crop(update, halo + 1, halo) + 2.0 * damping_next / half_width * resid
        iterate = crop(iterate, halo + 1, halo) + update
        damping = damping_next
    return iterate, halo


def body(state, previous, feed, kill):
    deep = 3
    fields = jnp.concatenate([state, feed[None], kill[None]], 0)
    fields_1 = restrict(fields)
    fields_2 = restrict(fields_1)
    lane = lax.broadcasted_iota(jnp.int32, (8, 128), 1)
    local = jnp.zeros((8, 128), jnp.float32)
    for level, level_fields in enumerate((fields, fields_1, fields_2)):
        _, first, second = coefficients(level_fields, level)
        local = jnp.where(lane == level, jnp.maximum(jnp.max(first), jnp.max(second)), local)
    wide_x = padded_along(jnp.concatenate([fields, previous], 0), 6, "gx", 3)
    local, wide_x = lax.optimization_barrier((local, wide_x))
    spreads = global_max(local)[0]

    wide = padded_along(wide_x, 6, "gy", 2)
    ops_0 = Level(coefficients(crop(wide[:4], 6, 5), 0)[0], 5, 0)
    state_w = wide[:2]
    substrate, catalyst = crop(state_w[0], 6, 5), crop(state_w[1], 6, 5)
    centre = crop(state_w, 6, 5)
    reaction = substrate * catalyst * catalyst
    laplace = shrunk_neighbours(state_w) - 6.0 * centre
    feed_w = crop(wide[2], 6, 5)
    kill_w = crop(wide[3], 6, 5)
    previous_w = crop(wide[4:6], 6, 5)
    local_terms = jnp.stack(
        [reaction - feed_w * (1.0 - substrate), -reaction + (feed_w + kill_w) * catalyst]
    )
    nonlinear = inverse_step * (centre - previous_w) - diffusions(0) * laplace + local_terms
    source_0 = -nonlinear
    pre_0, pre_0_halo = chebyshev(ops_0, source_0, 5, None, None, spreads[0])
    resid_0 = crop(source_0, 5, 0) - ops_0.operate(crop(pre_0, pre_0_halo, 1), 1)

    wide_1 = padded(jnp.concatenate([restrict(resid_0), fields_1], 0), 7)
    ops_1 = Level(coefficients(wide_1[2:], 1)[0], 7, 1)
    source_1 = wide_1[:2]
    pre_1, pre_1_halo = chebyshev(ops_1, source_1, 7, None, None, spreads[1])
    resid_1 = crop(source_1, 7, 0) - ops_1.operate(crop(pre_1, pre_1_halo, 1), 1)

    wide_2 = padded(jnp.concatenate([restrict(resid_1), fields_2], 0), 8)
    ops_2 = Level(coefficients(wide_2[2:], 2)[0], 8, 2)
    source_2 = wide_2[:2]
    first_2, first_2_halo = chebyshev(ops_2, source_2, 8, None, None, spreads[2])
    coarse_2, coarse_2_halo = chebyshev(ops_2, source_2, 8, first_2, first_2_halo, spreads[2])

    start_1 = crop(pre_1, pre_1_halo, 5) + crop(prolong(coarse_2), 2 * coarse_2_halo, 5)
    post_1, post_1_halo = chebyshev(ops_1, source_1, 7, start_1, 5, spreads[1])

    start_0 = crop(pre_0, pre_0_halo, 3) + crop(prolong(post_1), 2 * post_1_halo, 3)
    post_0, post_0_halo = chebyshev(ops_0, source_0, 5, start_0, 3, spreads[0])
    return crop(post_0, post_0_halo, 0)


def solution(mesh):
    placed = (
        P(None, None, "gy", "gx"),
        P(None, None, "gy", "gx"),
        P(None, "gy", "gx"),
        P(None, "gy", "gx"),
    )
    return jax.shard_map(
        body, mesh=mesh, in_specs=placed, out_specs=P(None, None, "gy", "gx"), check_vma=False
    )
```

```python
import numpy as np
import jax
import jax.numpy as jnp
from jax import lax
from jax.sharding import PartitionSpec as P
from jax.experimental import pallas as pl
from jax.experimental.pallas import tpu as pltpu

substrate_diffusion = 40.0
catalyst_diffusion = 20.0
inverse_step = 2.0
lower_fraction = 0.25
coarsenings = 2


def padded_along(cells, width, axis, dim):
    count = lax.axis_size(axis)
    size = cells.shape[dim]
    below, above = [], []
    remaining, distance = width, 1
    while remaining > 0:
        take = min(remaining, size)
        tail = lax.slice_in_dim(cells, size - take, size, axis=dim)
        head = lax.slice_in_dim(cells, 0, take, axis=dim)
        below.insert(0, lax.ppermute(tail, axis, [(i, (i + distance) % count) for i in range(count)]))
        above.append(lax.ppermute(head, axis, [((i + distance) % count, i) for i in range(count)]))
        remaining -= take
        distance += 1
    return jnp.concatenate(below + [cells] + above, axis=dim)


def padded(cells, width):
    return padded_along(padded_along(cells, width, "gx", 3), width, "gy", 2)


def crop(cells, have, want):
    cut = have - want
    assert cut >= 0
    if cut == 0:
        return cells
    return cells[..., cut:cells.shape[-2] - cut, cut:cells.shape[-1] - cut]


def shrunk_neighbours(cells):
    centre = cells[:, :, 1:-1, 1:-1]
    along_x = cells[:, :, 1:-1, :-2] + cells[:, :, 1:-1, 2:]
    along_y = cells[:, :, :-2, 1:-1] + cells[:, :, 2:, 1:-1]
    along_z = jnp.roll(centre, 1, 1) + jnp.roll(centre, -1, 1)
    return along_x + along_y + along_z


def gather_rows(source, land, send_sem, recv_sem, own_sem, device, count, me):
    mesh_ids = pl.DeviceIdType.MESH
    copies = []
    for step in range(1, count):
        copy = pltpu.make_async_remote_copy(
            src_ref=source,
            dst_ref=land.at[me],
            send_sem=send_sem.at[step],
            recv_sem=recv_sem.at[me],
            device_id=device(lax.rem(me + step, count)),
            device_id_type=mesh_ids,
        )
        copy.start()
        copies.append(copy)
    own = pltpu.make_async_copy(source, land.at[me], own_sem)
    own.start()
    for step in range(1, count):
        copies[step - 1].wait_send()
        sender = lax.rem(me + count - step, count)
        pltpu.make_async_remote_copy(
            src_ref=source,
            dst_ref=land.at[sender],
            send_sem=send_sem.at[step],
            recv_sem=recv_sem.at[sender],
            device_id=device(sender),
            device_id_type=mesh_ids,
        ).wait_recv()
    own.wait()


def spread_kernel(inner, value, out, land_x, land_z, land_y, send_x, recv_x, send_z, recv_z,
                  send_y, recv_y, own_x, own_z, own_y):
    count_x = lax.axis_size("gx")
    count_y = lax.axis_size("gy")
    outer = count_y // inner
    at_x = lax.axis_index("gx")
    at_y = lax.axis_index("gy")
    group, place = at_y // inner, lax.rem(at_y, inner)
    mesh_ids = pl.DeviceIdType.MESH
    along_x = lambda index: (index, at_y)
    along_z = lambda index: (at_x, group * inner + index)
    along_y = lambda index: (at_x, index * inner + place)
    barrier = pltpu.get_barrier_semaphore()
    for count, me, device in ((count_x, at_x, along_x), (inner, place, along_z), (outer, group, along_y)):
        for step in range(1, count):
            pl.semaphore_signal(barrier, 1, device_id=device(lax.rem(me + step, count)),
                                device_id_type=mesh_ids)
    pl.semaphore_wait(barrier, count_x + inner + outer - 3)
    gather_rows(value.at[pl.ds(0, 1), :], land_x, send_x, recv_x, own_x, along_x, count_x, at_x)
    gather_rows(land_x, land_z, send_z, recv_z, own_z, along_z, inner, place)
    gather_rows(land_z, land_y, send_y, recv_y, own_y, along_y, outer, group)
    best = jnp.max(land_y[...], axis=(0, 1, 2))
    out[...] = jnp.broadcast_to(best, out.shape)


def global_max(block):
    count_x = lax.axis_size("gx")
    count_y = lax.axis_size("gy")
    inner = 8 if count_y % 8 == 0 else count_y
    outer = count_y // inner
    vmem = pl.BlockSpec(memory_space=pltpu.VMEM)
    lanes = block.shape[1]
    return pl.pallas_call(
        lambda *refs: spread_kernel(inner, *refs),
        out_shape=jax.ShapeDtypeStruct(block.shape, jnp.float32),
        in_specs=[vmem],
        out_specs=vmem,
        scratch_shapes=[
            pltpu.VMEM((count_x, 1, lanes), jnp.float32),
            pltpu.VMEM((inner, count_x, 1, lanes), jnp.float32),
            pltpu.VMEM((outer, inner, count_x, 1, lanes), jnp.float32),
            pltpu.SemaphoreType.DMA((count_x,)),
            pltpu.SemaphoreType.DMA((count_x,)),
            pltpu.SemaphoreType.DMA((inner,)),
            pltpu.SemaphoreType.DMA((inner,)),
            pltpu.SemaphoreType.DMA((outer,)),
            pltpu.SemaphoreType.DMA((outer,)),
            pltpu.SemaphoreType.DMA(()),
            pltpu.SemaphoreType.DMA(()),
            pltpu.SemaphoreType.DMA(()),
        ],
        compiler_params=pltpu.CompilerParams(collective_id=0, has_side_effects=True),
    )(block)


def restrict(field):
    lead, depth, rows, cols = field.shape
    count = lead * depth * rows
    pick_x = (np.arange(cols)[:, None] // 2 == np.arange(cols // 2)[None, :]).astype(np.float32)
    row = np.arange(count)
    target = ((row // (depth * rows)) * (depth // 2) + (row // rows) % depth // 2) * (rows // 2) + row % rows // 2
    pick_rows = (np.arange(count // 4)[:, None] == target[None, :]).astype(np.float32)
    pairs = jnp.dot(field.reshape(count, cols), pick_x, precision=lax.Precision.HIGHEST)
    blocks = jnp.dot(pick_rows, pairs, precision=lax.Precision.HIGHEST)
    return (blocks * 0.125).reshape(lead, depth // 2, rows // 2, cols // 2)


def prolong(field):
    return jnp.repeat(jnp.repeat(jnp.repeat(field, 2, 1), 2, 2), 2, 3)


def diffusions(level):
    scale = 0.25**level
    return jnp.array(
        [substrate_diffusion * scale, catalyst_diffusion * scale], jnp.float32
    ).reshape(2, 1, 1, 1)


def coefficients(fields, level):
    scale = 0.25**level
    diff_first = substrate_diffusion * scale
    diff_second = catalyst_diffusion * scale
    substrate, catalyst, feed_rate, kill_rate = (fields[0], fields[1], fields[2], fields[3])
    product = substrate * catalyst
    squared = catalyst * catalyst
    self_first = inverse_step + squared + feed_rate + 6.0 * diff_first
    cross_first = 2.0 * product
    cross_second = -squared
    self_second = inverse_step + feed_rate + kill_rate - 2.0 * product + 6.0 * diff_second
    coeff = jnp.stack([self_first, cross_first, cross_second, self_second])
    return coeff, (6.0 * diff_first + cross_first) / self_first, (6.0 * diff_second + squared) / self_second


class Level:
    def __init__(self, coeff, halo, level):
        self.coeff = coeff
        self.halo = halo
        self.level = level

    def at(self, halo):
        return crop(self.coeff, self.halo, halo)

    def operate(self, field, halo):
        coeff = self.at(halo - 1)
        centre = crop(field, halo, halo - 1)
        first = coeff[0] * centre[0] + coeff[1] * centre[1]
        second = coeff[2] * centre[0] + coeff[3] * centre[1]
        return jnp.stack([first, second]) - diffusions(self.level) * shrunk_neighbours(field)

    def diagonal(self, halo):
        coeff = self.at(halo)
        return jnp.stack([coeff[0], coeff[3]])


def chebyshev(ops, source, source_halo, start, start_halo, spread):
    upper = 1.0 + spread
    lower = lower_fraction * upper
    centre = (upper + lower) / 2.0
    half_width = (upper - lower) / 2.0
    ratio = centre / half_width
    damping = 1.0 / ratio
    if start is None:
        halo = source_halo
        resid = source / ops.diagonal(halo)
        update = resid / centre
        iterate = update
    else:
        halo = min(source_halo, start_halo - 1)
        applied = ops.operate(start, start_halo)
        resid = (crop(source, source_halo, halo) - crop(applied, start_halo - 1, halo)) / ops.diagonal(halo)
        update = resid / centre
        iterate = crop(start, start_halo, halo) + update
    for sweep in range(2):
        applied = ops.operate(iterate, halo)
        halo = halo - 1
        resid = (crop(source, source_halo, halo) - applied) / ops.diagonal(halo)
        damping_next = 1.0 / (2.0 * ratio - damping)
        update = damping_next * damping * crop(update, halo + 1, halo) + 2.0 * damping_next / half_width * resid
        iterate = crop(iterate, halo + 1, halo) + update
        damping = damping_next
    return iterate, halo


def body(state, previous, feed, kill):
    deep = 3
    fields = jnp.concatenate([state, feed[None], kill[None]], 0)
    fields_1 = restrict(fields)
    fields_2 = restrict(fields_1)
    lane = lax.broadcasted_iota(jnp.int32, (8, 128), 1)
    local = jnp.zeros((8, 128), jnp.float32)
    for level, level_fields in enumerate((fields, fields_1, fields_2)):
        _, first, second = coefficients(level_fields, level)
        local = jnp.where(lane == level, jnp.maximum(jnp.max(first), jnp.max(second)), local)
    wide_x = padded_along(jnp.concatenate([fields, previous], 0), 6, "gx", 3)
    local, wide_x = lax.optimization_barrier((local, wide_x))
    spreads = global_max(local)[0]

    wide = padded_along(wide_x, 6, "gy", 2)
    ops_0 = Level(coefficients(crop(wide[:4], 6, 5), 0)[0], 5, 0)
    state_w = wide[:2]
    substrate, catalyst = crop(state_w[0], 6, 5), crop(state_w[1], 6, 5)
    centre = crop(state_w, 6, 5)
    reaction = substrate * catalyst * catalyst
    laplace = shrunk_neighbours(state_w) - 6.0 * centre
    feed_w = crop(wide[2], 6, 5)
    kill_w = crop(wide[3], 6, 5)
    previous_w = crop(wide[4:6], 6, 5)
    local_terms = jnp.stack(
        [reaction - feed_w * (1.0 - substrate), -reaction + (feed_w + kill_w) * catalyst]
    )
    nonlinear = inverse_step * (centre - previous_w) - diffusions(0) * laplace + local_terms
    source_0 = -nonlinear
    pre_0, pre_0_halo = chebyshev(ops_0, source_0, 5, None, None, spreads[0])
    resid_0 = crop(source_0, 5, 0) - ops_0.operate(crop(pre_0, pre_0_halo, 1), 1)

    wide_1 = padded(jnp.concatenate([restrict(resid_0), fields_1], 0), 7)
    ops_1 = Level(coefficients(wide_1[2:], 1)[0], 7, 1)
    source_1 = wide_1[:2]
    pre_1, pre_1_halo = chebyshev(ops_1, source_1, 7, None, None, spreads[1])
    resid_1 = crop(source_1, 7, 0) - ops_1.operate(crop(pre_1, pre_1_halo, 1), 1)

    wide_2 = padded(jnp.concatenate([restrict(resid_1), fields_2], 0), 8)
    ops_2 = Level(coefficients(wide_2[2:], 2)[0], 8, 2)
    source_2 = wide_2[:2]
    first_2, first_2_halo = chebyshev(ops_2, source_2, 8, None, None, spreads[2])
    coarse_2, coarse_2_halo = chebyshev(ops_2, source_2, 8, first_2, first_2_halo, spreads[2])

    start_1 = crop(pre_1, pre_1_halo, 5) + crop(prolong(coarse_2), 2 * coarse_2_halo, 5)
    post_1, post_1_halo = chebyshev(ops_1, source_1, 7, start_1, 5, spreads[1])

    start_0 = crop(pre_0, pre_0_halo, 3) + crop(prolong(post_1), 2 * post_1_halo, 3)
    post_0, post_0_halo = chebyshev(ops_0, source_0, 5, start_0, 3, spreads[0])
    return crop(post_0, post_0_halo, 0)


def solution(mesh):
    placed = (
        P(None, None, "gy", "gx"),
        P(None, None, "gy", "gx"),
        P(None, "gy", "gx"),
        P(None, "gy", "gx"),
    )
    return jax.shard_map(
        body, mesh=mesh, in_specs=placed, out_specs=P(None, None, "gy", "gx"), check_vma=False
    )
```

```python
import numpy as np
import jax
import jax.numpy as jnp
from jax import lax
from jax.sharding import PartitionSpec as P
from jax.experimental import pallas as pl
from jax.experimental.pallas import tpu as pltpu

substrate_diffusion = 40.0
catalyst_diffusion = 20.0
inverse_step = 2.0
lower_fraction = 0.25
coarsenings = 2


def padded_along(cells, width, axis, dim):
    count = lax.axis_size(axis)
    size = cells.shape[dim]
    below, above = [], []
    remaining, distance = width, 1
    while remaining > 0:
        take = min(remaining, size)
        tail = lax.slice_in_dim(cells, size - take, size, axis=dim)
        head = lax.slice_in_dim(cells, 0, take, axis=dim)
        below.insert(0, lax.ppermute(tail, axis, [(i, (i + distance) % count) for i in range(count)]))
        above.append(lax.ppermute(head, axis, [((i + distance) % count, i) for i in range(count)]))
        remaining -= take
        distance += 1
    return jnp.concatenate(below + [cells] + above, axis=dim)


def padded(cells, width):
    return padded_along(padded_along(cells, width, "gx", 3), width, "gy", 2)


def crop(cells, have, want):
    cut = have - want
    assert cut >= 0
    if cut == 0:
        return cells
    return cells[..., cut:cells.shape[-2] - cut, cut:cells.shape[-1] - cut]


def shrunk_neighbours(cells):
    centre = cells[:, :, 1:-1, 1:-1]
    along_x = cells[:, :, 1:-1, :-2] + cells[:, :, 1:-1, 2:]
    along_y = cells[:, :, :-2, 1:-1] + cells[:, :, 2:, 1:-1]
    along_z = jnp.roll(centre, 1, 1) + jnp.roll(centre, -1, 1)
    return along_x + along_y + along_z


def gather_rows(source, land, send_sem, recv_sem, own_sem, device, count, me):
    mesh_ids = pl.DeviceIdType.MESH
    copies = []
    for step in range(1, count):
        copy = pltpu.make_async_remote_copy(
            src_ref=source,
            dst_ref=land.at[me],
            send_sem=send_sem.at[step],
            recv_sem=recv_sem.at[me],
            device_id=device(lax.rem(me + step, count)),
            device_id_type=mesh_ids,
        )
        copy.start()
        copies.append(copy)
    own = pltpu.make_async_copy(source, land.at[me], own_sem)
    own.start()
    for step in range(1, count):
        copies[step - 1].wait_send()
        sender = lax.rem(me + count - step, count)
        pltpu.make_async_remote_copy(
            src_ref=source,
            dst_ref=land.at[sender],
            send_sem=send_sem.at[step],
            recv_sem=recv_sem.at[sender],
            device_id=device(sender),
            device_id_type=mesh_ids,
        ).wait_recv()
    own.wait()


def spread_kernel(inner, value, out, land_x, land_z, land_y, send_x, recv_x, send_z, recv_z,
                  send_y, recv_y, own_x, own_z, own_y):
    count_x = lax.axis_size("gx")
    count_y = lax.axis_size("gy")
    outer = count_y // inner
    at_x = lax.axis_index("gx")
    at_y = lax.axis_index("gy")
    group, place = at_y // inner, lax.rem(at_y, inner)
    mesh_ids = pl.DeviceIdType.MESH
    along_x = lambda index: (index, at_y)
    along_z = lambda index: (at_x, group * inner + index)
    along_y = lambda index: (at_x, index * inner + place)
    barrier = pltpu.get_barrier_semaphore()
    for count, me, device in ((count_x, at_x, along_x), (inner, place, along_z), (outer, group, along_y)):
        for step in range(1, count):
            pl.semaphore_signal(barrier, 1, device_id=device(lax.rem(me + step, count)),
                                device_id_type=mesh_ids)
    pl.semaphore_wait(barrier, count_x + inner + outer - 3)
    gather_rows(value.at[pl.ds(0, 1), :], land_x, send_x, recv_x, own_x, along_x, count_x, at_x)
    gather_rows(land_x, land_z, send_z, recv_z, own_z, along_z, inner, place)
    gather_rows(land_z, land_y, send_y, recv_y, own_y, along_y, outer, group)
    best = jnp.max(land_y[...], axis=(0, 1, 2))
    out[...] = jnp.broadcast_to(best, out.shape)


def global_max(block):
    count_x = lax.axis_size("gx")
    count_y = lax.axis_size("gy")
    inner = 8 if count_y % 8 == 0 else count_y
    outer = count_y // inner
    vmem = pl.BlockSpec(memory_space=pltpu.VMEM)
    lanes = block.shape[1]
    return pl.pallas_call(
        lambda *refs: spread_kernel(inner, *refs),
        out_shape=jax.ShapeDtypeStruct(block.shape, jnp.float32),
        in_specs=[vmem],
        out_specs=vmem,
        scratch_shapes=[
            pltpu.VMEM((count_x, 1, lanes), jnp.float32),
            pltpu.VMEM((inner, count_x, 1, lanes), jnp.float32),
            pltpu.VMEM((outer, inner, count_x, 1, lanes), jnp.float32),
            pltpu.SemaphoreType.DMA((count_x,)),
            pltpu.SemaphoreType.DMA((count_x,)),
            pltpu.SemaphoreType.DMA((inner,)),
            pltpu.SemaphoreType.DMA((inner,)),
            pltpu.SemaphoreType.DMA((outer,)),
            pltpu.SemaphoreType.DMA((outer,)),
            pltpu.SemaphoreType.DMA(()),
            pltpu.SemaphoreType.DMA(()),
            pltpu.SemaphoreType.DMA(()),
        ],
        compiler_params=pltpu.CompilerParams(collective_id=0, has_side_effects=True),
    )(block)


def restrict(field):
    lead, depth, rows, cols = field.shape
    count = lead * depth * rows
    pick_x = (np.arange(cols)[:, None] // 2 == np.arange(cols // 2)[None, :]).astype(np.float32)
    row = np.arange(count)
    target = ((row // (depth * rows)) * (depth // 2) + (row // rows) % depth // 2) * (rows // 2) + row % rows // 2
    pick_rows = (np.arange(count // 4)[:, None] == target[None, :]).astype(np.float32)
    pairs = jnp.dot(field.reshape(count, cols), pick_x, precision=lax.Precision.HIGHEST)
    blocks = jnp.dot(pick_rows, pairs, precision=lax.Precision.HIGHEST)
    return (blocks * 0.125).reshape(lead, depth // 2, rows // 2, cols // 2)


def prolong(field):
    return jnp.repeat(jnp.repeat(jnp.repeat(field, 2, 1), 2, 2), 2, 3)


def diffusions(level):
    scale = 0.25**level
    return jnp.array(
        [substrate_diffusion * scale, catalyst_diffusion * scale], jnp.float32
    ).reshape(2, 1, 1, 1)


def coefficients(fields, level):
    scale = 0.25**level
    diff_first = substrate_diffusion * scale
    diff_second = catalyst_diffusion * scale
    substrate, catalyst, feed_rate, kill_rate = (fields[0], fields[1], fields[2], fields[3])
    product = substrate * catalyst
    squared = catalyst * catalyst
    self_first = inverse_step + squared + feed_rate + 6.0 * diff_first
    cross_first = 2.0 * product
    cross_second = -squared
    self_second = inverse_step + feed_rate + kill_rate - 2.0 * product + 6.0 * diff_second
    coeff = jnp.stack([self_first, cross_first, cross_second, self_second])
    return coeff, (6.0 * diff_first + cross_first) / self_first, (6.0 * diff_second + squared) / self_second


class Level:
    def __init__(self, coeff, halo, level):
        self.coeff = coeff
        self.halo = halo
        self.level = level

    def at(self, halo):
        return crop(self.coeff, self.halo, halo)

    def operate(self, field, halo):
        coeff = self.at(halo - 1)
        centre = crop(field, halo, halo - 1)
        first = coeff[0] * centre[0] + coeff[1] * centre[1]
        second = coeff[2] * centre[0] + coeff[3] * centre[1]
        return jnp.stack([first, second]) - diffusions(self.level) * shrunk_neighbours(field)

    def diagonal(self, halo):
        coeff = self.at(halo)
        return jnp.stack([coeff[0], coeff[3]])


def chebyshev(ops, source, source_halo, start, start_halo, spread):
    upper = 1.0 + spread
    lower = lower_fraction * upper
    centre = (upper + lower) / 2.0
    half_width = (upper - lower) / 2.0
    ratio = centre / half_width
    damping = 1.0 / ratio
    if start is None:
        halo = source_halo
        resid = source / ops.diagonal(halo)
        update = resid / centre
        iterate = update
    else:
        halo = min(source_halo, start_halo - 1)
        applied = ops.operate(start, start_halo)
        resid = (crop(source, source_halo, halo) - crop(applied, start_halo - 1, halo)) / ops.diagonal(halo)
        update = resid / centre
        iterate = crop(start, start_halo, halo) + update
    for sweep in range(2):
        applied = ops.operate(iterate, halo)
        halo = halo - 1
        resid = (crop(source, source_halo, halo) - applied) / ops.diagonal(halo)
        damping_next = 1.0 / (2.0 * ratio - damping)
        update = damping_next * damping * crop(update, halo + 1, halo) + 2.0 * damping_next / half_width * resid
        iterate = crop(iterate, halo + 1, halo) + update
        damping = damping_next
    return iterate, halo


def body(state, previous, feed, kill):
    deep = 3
    fields = jnp.concatenate([state, feed[None], kill[None]], 0)
    fields_1 = restrict(fields)
    fields_2 = restrict(fields_1)
    lane = lax.broadcasted_iota(jnp.int32, (8, 128), 1)
    local = jnp.zeros((8, 128), jnp.float32)
    for level, level_fields in enumerate((fields, fields_1, fields_2)):
        _, first, second = coefficients(level_fields, level)
        local = jnp.where(lane == level, jnp.maximum(jnp.max(first), jnp.max(second)), local)
    wide_x = padded_along(jnp.concatenate([fields, previous], 0), 6, "gx", 3)
    local, wide_x = lax.optimization_barrier((local, wide_x))
    spreads = global_max(local)[0]
    ops_1 = Level(coefficients(padded(fields_1, 7), 1)[0], 7, 1)
    ops_2 = Level(coefficients(padded(fields_2, 8), 2)[0], 8, 2)

    wide = padded_along(wide_x, 6, "gy", 2)
    ops_0 = Level(coefficients(crop(wide[:4], 6, 5), 0)[0], 5, 0)
    state_w = wide[:2]
    substrate, catalyst = crop(state_w[0], 6, 5), crop(state_w[1], 6, 5)
    centre = crop(state_w, 6, 5)
    reaction = substrate * catalyst * catalyst
    laplace = shrunk_neighbours(state_w) - 6.0 * centre
    feed_w = crop(wide[2], 6, 5)
    kill_w = crop(wide[3], 6, 5)
    previous_w = crop(wide[4:6], 6, 5)
    local_terms = jnp.stack(
        [reaction - feed_w * (1.0 - substrate), -reaction + (feed_w + kill_w) * catalyst]
    )
    nonlinear = inverse_step * (centre - previous_w) - diffusions(0) * laplace + local_terms
    source_0 = -nonlinear
    pre_0, pre_0_halo = chebyshev(ops_0, source_0, 5, None, None, spreads[0])
    resid_0 = crop(source_0, 5, 0) - ops_0.operate(crop(pre_0, pre_0_halo, 1), 1)

    source_1 = padded(restrict(resid_0), 7)
    pre_1, pre_1_halo = chebyshev(ops_1, source_1, 7, None, None, spreads[1])
    resid_1 = crop(source_1, 7, 0) - ops_1.operate(crop(pre_1, pre_1_halo, 1), 1)

    source_2 = padded(restrict(resid_1), 8)
    first_2, first_2_halo = chebyshev(ops_2, source_2, 8, None, None, spreads[2])
    coarse_2, coarse_2_halo = chebyshev(ops_2, source_2, 8, first_2, first_2_halo, spreads[2])

    start_1 = crop(pre_1, pre_1_halo, 5) + crop(prolong(coarse_2), 2 * coarse_2_halo, 5)
    post_1, post_1_halo = chebyshev(ops_1, source_1, 7, start_1, 5, spreads[1])

    start_0 = crop(pre_0, pre_0_halo, 3) + crop(prolong(post_1), 2 * post_1_halo, 3)
    post_0, post_0_halo = chebyshev(ops_0, source_0, 5, start_0, 3, spreads[0])
    return crop(post_0, post_0_halo, 0)


def solution(mesh):
    placed = (
        P(None, None, "gy", "gx"),
        P(None, None, "gy", "gx"),
        P(None, "gy", "gx"),
        P(None, "gy", "gx"),
    )
    return jax.shard_map(
        body, mesh=mesh, in_specs=placed, out_specs=P(None, None, "gy", "gx"), check_vma=False
    )
```
